32 devices in a mesh: dp: 8 (over y, x, core), fsdp: 4 (over z).
Axes of the slice: x: 2, y: 2, z: 4, core: 2. Of those that a mesh axis runs over, the one named last changes fastest.
Arguments:
- tokens: bfloat16 [32768, 768], P(('dp', 'fsdp')), may hold values from -6 to 6
- cotangent: bfloat16 [32768, 768], P(('dp', 'fsdp')), may hold values from -6 to 6
- doc_lengths: int32 [64, 4], P(('dp', 'fsdp')), may hold values from 1 to 288, 512 in all within a row
- query_ids: int32 [256, 1], P(('dp', 'fsdp')), may hold values from 0 to 63
- qkv_weight: bfloat16 [768, 2304], P(('dp', 'fsdp')), may hold values from -0.21875 to 0.21875
- query_bias: bfloat16 [768], P(('dp', 'fsdp')), may hold values from -3 to 3
- value_bias: bfloat16 [768], P(('dp', 'fsdp')), may hold values from -3 to 3
- attn_weight: bfloat16 [768, 768], P(('dp', 'fsdp')), may hold values from -0.875 to 0.875
- attn_bias: bfloat16 [768], P(('dp', 'fsdp')), may hold values from -2 to 2
- first_gain: bfloat16 [768], P(('dp', 'fsdp')), may hold values from 0.5 to 1.5
- first_shift: bfloat16 [768], P(('dp', 'fsdp')), may hold values from -2 to 2
- inner_weight: bfloat16 [768, 3072], P(('dp', 'fsdp')), may hold values from -0.21875 to 0.21875
- inner_bias: bfloat16 [3072], P(('dp', 'fsdp')), may hold values from -3 to 3
- outer_weight: bfloat16 [3072, 768], P(('dp', 'fsdp')), may hold values from -0.21875 to 0.21875
- outer_bias: bfloat16 [768], P(('dp', 'fsdp')), may hold values from -2 to 2
- second_gain: bfloat16 [768], P(('dp', 'fsdp')), may hold values from 0.5 to 1.5
- second_shift: bfloat16 [768], P(('dp', 'fsdp')), may hold values from -2 to 2
- span_weight: bfloat16 [768, 128], P(('dp', 'fsdp')), may hold values from -0.21875 to 0.21875
- answer_vector: bfloat16 [128], P(('dp', 'fsdp')), may hold values from -1 to 1
Outputs:
- log_likelihood: float32 [], replicated
- layer_output: bfloat16 [32768, 768], P(('dp', 'fsdp'))
- input_grad: float32 [32768, 768], P(('dp', 'fsdp'))
- qkv_weight_grad: float32 [768, 2304], P(('dp', 'fsdp'))
- query_bias_grad: float32 [768], P(('dp', 'fsdp'))
- value_bias_grad: float32 [768], P(('dp', 'fsdp'))
- attn_weight_grad: float32 [768, 768], P(('dp', 'fsdp'))
- attn_bias_grad: float32 [768], P(('dp', 'fsdp'))
- first_gain_grad: float32 [768], P(('dp', 'fsdp'))
- first_shift_grad: float32 [768], P(('dp', 'fsdp'))
- inner_weight_grad: float32 [768, 3072], P(('dp', 'fsdp'))
- inner_bias_grad: float32 [3072], P(('dp', 'fsdp'))
- outer_weight_grad: float32 [3072, 768], P(('dp', 'fsdp'))
- outer_bias_grad: float32 [768], P(('dp', 'fsdp'))
- second_gain_grad: float32 [768], P(('dp', 'fsdp'))
- second_shift_grad: float32 [768], P(('dp', 'fsdp'))
- span_weight_grad: float32 [768, 128], P(('dp', 'fsdp'))
- answer_vector_grad: float32 [128], P(('dp', 'fsdp'))
The draws below stay inside these ranges and needn't reach their ends.
Inputs may be any that keep to these rules, and one draw needn't show every extreme that they name: `doc_lengths`: the 4 lengths of a pack sum to 512, and in every pack one of them is 288. `query_ids`: every query has one segment or more.
All inputs are finite; a program needn't handle non-finite values.
Results may differ from the reference program's by a relative error of at most 0.014.
Values may be sent and summed in bfloat16 or wider, within the bound.
No kernel may reach another device: no remote copies, remote signals or barrier semaphores. Data moves between devices by JAX's collectives and lax.ppermute only.
A program may use at most 192 MiB of HBM per device.

```python
import math
import jax
import jax.numpy as jnp
import numpy as np
from jax import lax

D = 768
HEADS = 12
HEAD_DIM = 64
FF = 3072
SPAN = 128
PACK = 512
MOST = 288
SEGS_PACK = 4
PACKS = 64
TOKENS = 32768
SEGS = 256
QUERIES = 64


def steps_of(key, shape, split, low, top_value):
    level = 1.0
    for axis_at, shards_of in split:
        heights = jax.random.uniform(jax.random.fold_in(jax.random.fold_in(key, 6), axis_at), (shards_of,), jnp.float32, low / len(split), top_value / len(split))
        level = level * jnp.repeat(jnp.exp(heights), shape[axis_at] // shards_of).reshape((-1,) + (1,) * (len(shape) - 1 - axis_at))
    return level


def distinct(stream_key, rows, amount, top, lift):
    ranking = jax.random.permutation(jax.random.fold_in(stream_key, 1), amount)
    pull = ranking
    for power in range(3):
        pull = pull * pull // amount
    pull = pull * lift // amount
    tickets = jax.random.randint(jax.random.fold_in(stream_key, 2), (rows, amount), 0, 4096) + pull
    fixed_rows = jax.random.permutation(jax.random.fold_in(stream_key, 3), rows)[jnp.arange(amount) % rows]
    tickets = jnp.where(jnp.arange(rows)[:, None] == fixed_rows[None, :], 1 << 14, tickets)
    priority = tickets * amount + jnp.arange(amount)
    return lax.top_k(priority.astype(jnp.int32), top)[1].astype(jnp.int32)


def split_up(amount, total, bound, slope):
    portions = [(1 << 20) // math.isqrt(grade ** slope) + 1 for grade in range(2, amount + 1)]
    spare, given = total - bound - (amount - 1), [1] * (amount - 1)
    while spare > 0:
        candidates = [i for i in range(amount - 1) if given[i] < bound]
        whole, budget = sum([portions[i] for i in candidates]), spare
        for i in candidates:
            more = min(bound - given[i], max(1, budget * portions[i] // whole), spare)
            given[i] = given[i] + more
            spare = spare - more
    return np.array([bound] + given)


def uneven(own_key, amount, total, most, slope):
    if amount == 2:
        one = jax.random.randint(own_key, (), max(1, total - most), min(most, total - 1) + 1)
        return jnp.stack([one, total - one])
    sizes = jnp.asarray(split_up(amount, total, most, slope), jnp.int32)
    twos = (amount - 1) // 2
    giver, taker = sizes[1:1 + 2 * twos:2], sizes[2:2 + 2 * twos:2]
    margin = jnp.minimum(giver - 1, most - taker)
    shifted = jax.random.randint(jax.random.fold_in(own_key, 1), (twos,), 0, 1 << 20) % (margin + 1)
    sizes = sizes.at[1:1 + 2 * twos:2].set(giver - shifted).at[2:2 + 2 * twos:2].set(taker + shifted)
    return sizes[jax.random.permutation(jax.random.fold_in(own_key, 2), amount)]


def scatter_about(stream_key, shape, spread, limit, shards=(), dtype=jnp.bfloat16):
    loudness = steps_of(stream_key, shape, shards, -0.22, 0.18) if shards else 1.0
    array = jax.random.normal(stream_key, shape, jnp.float32) * spread * loudness
    return jnp.minimum(jnp.maximum(array, -limit), limit).astype(dtype)


def setup_inputs(seed: int = 0) -> dict:
    streams_of = jax.random.split(jax.random.key(seed), 20)
    return {
        "tokens": scatter_about(streams_of[0], (TOKENS, D), 1.0, 6.0, ((0, 32),)),
        "cotangent": scatter_about(streams_of[1], (TOKENS, D), 1.0, 6.0, ((0, 32),)),
        "doc_lengths": jax.vmap(lambda own: uneven(own, SEGS_PACK, PACK, MOST, 1))(jax.random.split(streams_of[2], PACKS)).reshape((PACKS, SEGS_PACK)).astype(jnp.int32),
        "query_ids": distinct(streams_of[3], SEGS, QUERIES, 1, 0),
        "qkv_weight": scatter_about(streams_of[4], (D, 3 * D), D ** -0.5, 0.21875, ((0, 32),)),
        "query_bias": scatter_about(streams_of[5], (D,), 0.5, 3.0, ((0, 32),)),
        "value_bias": scatter_about(streams_of[6], (D,), 0.5, 3.0, ((0, 32),)),
        "attn_weight": scatter_about(streams_of[7], (D, D), (D // 16) ** -0.5, 0.875, ((0, 32),)),
        "attn_bias": scatter_about(streams_of[8], (D,), 0.3, 2.0, ((0, 32),)),
        "first_gain": jnp.clip(1.0 + 0.1 * jax.random.normal(streams_of[9], (D,), jnp.float32), 0.5, 1.5).astype(jnp.bfloat16),
        "first_shift": scatter_about(streams_of[10], (D,), 0.3, 2.0, ((0, 32),)),
        "inner_weight": scatter_about(streams_of[11], (D, FF), D ** -0.5, 0.21875, ((0, 32),)),
        "inner_bias": scatter_about(streams_of[12], (FF,), 0.5, 3.0, ((0, 32),)),
        "outer_weight": scatter_about(streams_of[13], (FF, D), (FF // 4) ** -0.5, 0.21875, ((0, 32),)),
        "outer_bias": scatter_about(streams_of[14], (D,), 0.3, 2.0, ((0, 32),)),
        "second_gain": jnp.clip(1.0 + 0.1 * jax.random.normal(streams_of[15], (D,), jnp.float32), 0.5, 1.5).astype(jnp.bfloat16),
        "second_shift": scatter_about(streams_of[16], (D,), 0.3, 2.0, ((0, 32),)),
        "span_weight": scatter_about(streams_of[17], (D, SPAN), D ** -0.5, 0.21875, ((0, 32),)),
        "answer_vector": scatter_about(streams_of[18], (SPAN,), (SPAN // 4) ** -0.5, 1.0, ((0, 32),)),
    }


@jax.custom_vjp
def low(v):
    return lax.optimization_barrier(v.astype(jnp.bfloat16)).astype(jnp.float32)

@jax.custom_vjp
def low_back(v):
    return v

def low_keep(v):
    return (low(v), None)

def low_pass(kept, grad):
    return (grad,)

def back_keep(v):
    return (v, None)

def back_low(kept, grad):
    return (low(grad),)
low.defvjp(low_keep, low_pass)
low_back.defvjp(back_keep, back_low)
HIGHEST = lax.Precision.HIGHEST
MASKED = -1e+30

def layer_norm(hidden, gain, shift):
    center = hidden - lax.optimization_barrier(jnp.mean(hidden, axis=-1, keepdims=True))
    factor = lax.rsqrt(lax.optimization_barrier(jnp.mean(center * center, axis=-1, keepdims=True)) + 1e-06)
    return center * factor * gain + shift

def project(operand, matrix):
    return jnp.einsum('gpd,de->gpe', operand, matrix, precision=HIGHEST)

def segment_ids(lengths):
    bounds = jnp.cumsum(lengths, axis=1)
    places = lax.broadcasted_iota(jnp.int32, (1, PACK, 1), 1)
    return lax.optimization_barrier(jnp.sum((places >= bounds[:, None, :]).astype(jnp.int32), axis=-1)).astype(jnp.int32)

def group_forward(params, inputs):
    token_rows, segment = inputs
    qkv_weight, query_bias, value_bias, attn_weight, attn_bias, first_gain, first_shift, inner_weight, inner_bias, outer_weight, outer_bias, second_gain, second_shift, span_weight, answer_vector = params
    packs_here = token_rows.shape[0]
    qkv_bias = jnp.concatenate([query_bias, jnp.zeros_like(query_bias), value_bias])
    mixed_rows = low(low_back(project(token_rows, qkv_weight) + qkv_bias))
    head_split = mixed_rows.reshape(packs_here, PACK, 3, HEADS, HEAD_DIM)
    raw_scores = jnp.einsum('gqhd,gkhd->ghqk', head_split[:, :, 0], head_split[:, :, 1], precision=HIGHEST)
    scores = low_back(raw_scores * (1.0 / math.sqrt(HEAD_DIM)))
    same_segment = segment[:, :, None] == segment[:, None, :]
    shares = low(jax.nn.softmax(jnp.where(same_segment[:, None], scores, MASKED), axis=-1))
    context = jnp.einsum('ghqk,gkhd->gqhd', shares, head_split[:, :, 2], precision=HIGHEST)
    context = low(low_back(context.reshape(packs_here, PACK, D)))
    attended = low_back(project(context, attn_weight) + attn_bias)
    first_norm = layer_norm(token_rows + attended, first_gain, first_shift)
    inner_pre = low_back(project(low(first_norm), inner_weight) + inner_bias)
    active = low(jax.nn.gelu(inner_pre, approximate=False))
    outer_out = low_back(project(active, outer_weight) + outer_bias)
    result = low(layer_norm(first_norm + outer_out, second_gain, second_shift))
    span_rows = low_back(project(result, span_weight))
    token_score = jnp.einsum('gpe,e->gp', span_rows, answer_vector, precision=HIGHEST)
    member = segment[:, None, :] == lax.broadcasted_iota(jnp.int32, (1, SEGS_PACK, 1), 1)
    doc_score = jax.nn.logsumexp(jnp.where(member, token_score[:, None, :], MASKED), axis=-1)
    return (result, doc_score)

def forward(token_rows, params, segment, member_query):
    tok_groups = token_rows.reshape(PACKS // 8, 8, PACK, D)
    seg_groups = segment.reshape(PACKS // 8, 8, PACK)
    group_step = jax.checkpoint(group_forward)

    def scan_step(unused, inputs):
        return (unused, group_step(params, inputs))
    unused, (result, doc_score) = lax.scan(scan_step, jnp.zeros((), jnp.float32), (tok_groups, seg_groups))
    marginal = jax.nn.logsumexp(jnp.where(member_query, doc_score.reshape(1, SEGS), MASKED), axis=-1)
    return (result.reshape(TOKENS, D), jnp.sum(marginal))

def reference(tokens, cotangent, doc_lengths, query_ids, qkv_weight, query_bias, value_bias, attn_weight, attn_bias, first_gain, first_shift, inner_weight, inner_bias, outer_weight, outer_bias, second_gain, second_shift, span_weight, answer_vector):
    params = jax.tree.map(lambda weight: weight.astype(jnp.float32), (qkv_weight, query_bias, value_bias, attn_weight, attn_bias, first_gain, first_shift, inner_weight, inner_bias, outer_weight, outer_bias, second_gain, second_shift, span_weight, answer_vector))
    segment = segment_ids(doc_lengths)
    member_query = lax.broadcasted_iota(jnp.int32, (QUERIES, 1), 0) == query_ids.reshape(1, SEGS)
    (result, likelihood), pullback = jax.vjp(lambda token_rows, weight_set: forward(token_rows, weight_set, segment, member_query), tokens.astype(jnp.float32), params)
    input_grad, grads = pullback((cotangent.astype(jnp.float32), jnp.ones((), jnp.float32)))
    return (likelihood, result.astype(jnp.bfloat16), input_grad, grads[0], grads[1], grads[2], grads[3], grads[4], grads[5], grads[6], grads[7], grads[8], grads[9], grads[10], grads[11], grads[12], grads[13], grads[14])
```

```python
import math

import jax
import jax.numpy as jnp
from jax import lax
from jax.sharding import PartitionSpec as P

HEADS = 12
HEAD_DIM = 64
PACK = 512
SEGS_PACK = 4


HIGHEST = lax.Precision.HIGHEST
MASKED = -1e30


AXES = ("dp", "fsdp")
LANES = 128


def pack_small(parts):
    flat = jnp.concatenate(parts, axis=-1)
    wide = -(-flat.shape[-1] // LANES) * LANES
    pad = [(0, 0)] * (flat.ndim - 1) + [(0, wide - flat.shape[-1])]
    return jnp.pad(flat, pad).reshape(flat.shape[:-1] + (wide // LANES, LANES))


def unpack_small(packed, sizes):
    flat = packed.reshape(packed.shape[:-2] + (-1,))
    starts = [sum(sizes[:i]) for i in range(len(sizes))]
    return [flat[..., a : a + n] for a, n in zip(starts, sizes)]


def exchange_small(parts, devices):
    packed = pack_small(parts)
    spread = jnp.broadcast_to(packed[None], (devices,) + packed.shape)
    full = lax.all_to_all(spread, AXES, 0, 0)
    return [v.reshape(-1) for v in unpack_small(full, [p.shape[0] for p in parts])]


def reduce_small(parts, devices):
    packed = pack_small([p.reshape(devices, -1) for p in parts])
    mine = jnp.sum(lax.all_to_all(packed, AXES, 0, 0), axis=0)
    return unpack_small(mine, [p.shape[0] // devices for p in parts])


def split_rows(grad, devices, width):
    low = grad.astype(jnp.bfloat16)
    share = low.shape[0] // devices
    blocks = low.shape[1] // width
    low = low.reshape(devices, share, blocks, width).transpose(0, 2, 1, 3)
    return low.reshape(devices, blocks * share, width)


def join_rows(grad, blocks):
    share = grad.shape[0] // blocks
    return jnp.concatenate([grad[i * share : (i + 1) * share] for i in range(blocks)], axis=1)


def matmul(operand, matrix):
    return jnp.dot(operand, matrix, preferred_element_type=jnp.float32)


def weight_grad(operand, matrix):
    return lax.dot_general(
        operand, matrix, (((0,), (0,)), ((), ())), preferred_element_type=jnp.float32
    )


def back_prod(operand, matrix):
    return lax.dot_general(
        operand, matrix, (((1,), (1,)), ((), ())), preferred_element_type=jnp.float32
    )


def normalize(hidden):
    center = hidden - jnp.mean(hidden, axis=-1, keepdims=True)
    factor = lax.rsqrt(jnp.mean(center * center, axis=-1, keepdims=True) + 1e-06)
    return (center * factor, factor)


def norm_back(gradient, normed, factor):
    return factor * (
        gradient
        - jnp.mean(gradient, axis=-1, keepdims=True)
        - normed * jnp.mean(gradient * normed, axis=-1, keepdims=True)
    )


def segment_ids(lengths):
    bounds = jnp.cumsum(lengths, axis=1)
    places = lax.broadcasted_iota(jnp.int32, (1, PACK, 1), 1)
    return jnp.sum((places >= bounds[:, None, :]).astype(jnp.int32), axis=-1)


def exact_gelu(inner_pre):
    return jax.nn.gelu(inner_pre, approximate=False)


def masked_scores(query_heads, key_heads, segment):
    scaling = 1.0 / math.sqrt(query_heads.shape[-1])
    same_segment = segment[:, None] == segment[None, :]
    raw_scores = (
        jnp.einsum("qhd,khd->hqk", query_heads, key_heads, preferred_element_type=jnp.float32)
        * scaling
    )
    return jnp.where(same_segment[None], raw_scores, MASKED)


def attend(pieces):
    query_heads, key_heads, value_heads, segment = pieces
    scores = masked_scores(query_heads, key_heads, segment)
    highest = jnp.max(scores, axis=-1, keepdims=True)
    weights = jnp.exp(scores - highest)
    totals = jnp.sum(weights, axis=-1, keepdims=True)
    shares = (weights / totals).astype(jnp.bfloat16)
    context = jnp.einsum("hqk,khd->qhd", shares, value_heads, preferred_element_type=jnp.float32)
    return (context.astype(jnp.bfloat16), highest + jnp.log(totals))


def attend_back(pieces):
    query_heads, key_heads, value_heads, segment, logsum, context_grad = pieces
    scaling = 1.0 / math.sqrt(query_heads.shape[-1])
    scores = masked_scores(query_heads, key_heads, segment)
    softmax = jnp.exp(scores - logsum)
    value_grad = jnp.einsum(
        "hqk,qhd->khd",
        softmax.astype(jnp.bfloat16),
        context_grad,
        preferred_element_type=jnp.float32,
    )
    shares_grad = jnp.einsum(
        "qhd,khd->hqk", context_grad, value_heads, preferred_element_type=jnp.float32
    )
    score_grad = softmax * (shares_grad - jnp.sum(softmax * shares_grad, axis=-1, keepdims=True))
    score_low = score_grad.astype(jnp.bfloat16)
    query_grad = (
        jnp.einsum("hqk,khd->qhd", score_low, key_heads, preferred_element_type=jnp.float32)
        * scaling
    )
    key_grad = (
        jnp.einsum("hqk,qhd->khd", score_low, query_heads, preferred_element_type=jnp.float32)
        * scaling
    )
    stacked = jnp.stack([query_grad, key_grad, value_grad], axis=1)
    return stacked.reshape(stacked.shape[0], -1)


def shards(
    tokens,
    cotangent,
    doc_lengths,
    query_ids,
    qkv_weight,
    query_bias,
    value_bias,
    attn_weight,
    attn_bias,
    first_gain,
    first_shift,
    inner_weight,
    inner_bias,
    outer_weight,
    outer_bias,
    second_gain,
    second_shift,
    span_weight,
    answer_vector,
):
    rows_here = tokens.shape[0]
    width = tokens.shape[1]
    packs_here = rows_here // PACK
    devices = lax.axis_size("dp") * lax.axis_size("fsdp")
    share = qkv_weight.shape[0]
    inner_wide = inner_weight.shape[1]
    reps = inner_wide // width
    segs_here = packs_here * SEGS_PACK
    smalls = (
        query_bias,
        value_bias,
        attn_bias,
        first_gain,
        first_shift,
        inner_bias,
        outer_bias,
        second_gain,
        second_shift,
        answer_vector,
    )
    small_all = exchange_small([v.astype(jnp.float32) for v in smalls] + [query_ids[:, 0].astype(jnp.float32)], devices)
    (
        query_add,
        value_add,
        attn_add,
        gain_one,
        shift_one,
        inner_add,
        outer_add,
        gain_two,
        shift_two,
        answer_full,
        ids_all,
    ) = small_all
    mix_full = lax.all_gather(qkv_weight, AXES, axis=0, tiled=True)
    rest = jnp.concatenate(
        [attn_weight, outer_weight]
        + [inner_weight[:, i * width : (i + 1) * width] for i in range(reps)]
        + [span_weight.reshape(-1, width)],
        axis=0,
    )
    rest_all = lax.all_gather(rest, AXES, axis=0)
    attn_full = rest_all[:, :share].reshape(width, width)
    outer_full = rest_all[:, share : share * (1 + reps)].reshape(inner_wide, width)
    inner_full = (
        rest_all[:, share * (1 + reps) : share * (1 + 2 * reps)]
        .reshape(devices, reps, share, width)
        .transpose(0, 2, 1, 3)
        .reshape(width, inner_wide)
    )
    span_full = rest_all[:, share * (1 + 2 * reps) :].reshape(width, -1)
    segment = segment_ids(doc_lengths)
    qkv_add = jnp.concatenate([query_add, jnp.zeros_like(query_add), value_add]).astype(jnp.float32)
    mixed_rows = (matmul(tokens, mix_full) + qkv_add).astype(jnp.bfloat16)
    head_split = mixed_rows.reshape(packs_here, PACK, 3, HEADS, HEAD_DIM)
    query_heads = head_split[:, :, 0]
    key_heads = head_split[:, :, 1]
    value_heads = head_split[:, :, 2]
    context, logsum = lax.map(attend, (query_heads, key_heads, value_heads, segment))
    context = context.reshape(rows_here, width)
    attended = matmul(context, attn_full) + attn_add.astype(jnp.float32)
    normed_one, factor_one = normalize(tokens.astype(jnp.float32) + attended)
    first_norm = normed_one * gain_one.astype(jnp.float32) + shift_one.astype(jnp.float32)
    first_low = first_norm.astype(jnp.bfloat16)
    inner_pre = matmul(first_low, inner_full) + inner_add.astype(jnp.float32)
    active, gelu_back = jax.vjp(exact_gelu, inner_pre)
    active_low = active.astype(jnp.bfloat16)
    outer_out = matmul(active_low, outer_full) + outer_add.astype(jnp.float32)
    normed_two, factor_two = normalize(first_norm + outer_out)
    result = (normed_two * gain_two.astype(jnp.float32) + shift_two.astype(jnp.float32)).astype(
        jnp.bfloat16
    )
    span_rows = matmul(result, span_full)
    answer_wide = answer_full.astype(jnp.float32)
    token_score = jnp.dot(span_rows, answer_wide, precision=HIGHEST).reshape(packs_here, PACK)
    member = segment[:, None, :] == lax.broadcasted_iota(jnp.int32, (1, SEGS_PACK, 1), 1)
    doc_score = jax.nn.logsumexp(jnp.where(member, token_score[:, None, :], MASKED), axis=-1)
    (scores_all,) = exchange_small([doc_score.reshape(-1)], devices)
    member_query = ids_all[None, :] == lax.broadcasted_iota(jnp.float32, (packs_here * devices, 1), 0)
    marginal = jax.nn.logsumexp(jnp.where(member_query, scores_all[None, :], MASKED), axis=1)
    likelihood = jnp.sum(marginal)
    own_query = query_ids.astype(jnp.float32) == ids_all[None, :]
    seg_marginal = jax.nn.logsumexp(
        jnp.where(own_query, scores_all[None, :], MASKED), axis=1
    ).reshape(packs_here, SEGS_PACK)
    doc_weight = jnp.exp(doc_score - seg_marginal)
    token_weight = jnp.sum(
        jnp.where(
            member,
            doc_weight[:, :, None] * jnp.exp(token_score[:, None, :] - doc_score[:, :, None]),
            0.0,
        ),
        axis=1,
    ).reshape(rows_here)
    answer_grad = jnp.dot(token_weight, span_rows, precision=HIGHEST)
    span_grad = (token_weight[:, None] * answer_full.astype(jnp.float32)[None, :]).astype(
        jnp.bfloat16
    )
    span_weight_grad = weight_grad(result, span_grad)
    result_grad = cotangent.astype(jnp.float32) + back_prod(span_grad, span_full)
    second_gain_grad = jnp.sum(result_grad * normed_two, axis=0)
    second_shift_grad = jnp.sum(result_grad, axis=0)
    second_sum_grad = norm_back(result_grad * gain_two.astype(jnp.float32), normed_two, factor_two)
    outer_low = second_sum_grad.astype(jnp.bfloat16)
    outer_weight_grad = weight_grad(active_low, outer_low)
    outer_bias_grad = jnp.sum(outer_low.astype(jnp.float32), axis=0)
    (inner_grad,) = gelu_back(back_prod(outer_low, outer_full))
    inner_low = inner_grad.astype(jnp.bfloat16)
    inner_weight_grad = weight_grad(first_low, inner_low)
    early = jnp.concatenate(
        [
            outer_weight_grad.astype(jnp.bfloat16).reshape(devices, reps * share, width),
            split_rows(inner_weight_grad, devices, width),
            span_weight_grad.astype(jnp.bfloat16).reshape(devices, -1, width),
        ],
        axis=1,
    )
    early_own = lax.psum_scatter(early, AXES, scatter_dimension=0)
    inner_bias_grad = jnp.sum(inner_low.astype(jnp.float32), axis=0)
    first_grad = second_sum_grad + back_prod(inner_low, inner_full)
    first_gain_grad = jnp.sum(first_grad * normed_one, axis=0)
    first_shift_grad = jnp.sum(first_grad, axis=0)
    first_sum_grad = norm_back(first_grad * gain_one.astype(jnp.float32), normed_one, factor_one)
    attended_low = first_sum_grad.astype(jnp.bfloat16)
    attn_weight_grad = weight_grad(context, attended_low)
    attn_bias_grad = jnp.sum(attended_low.astype(jnp.float32), axis=0)
    context_grad = back_prod(attended_low, attn_full).astype(jnp.bfloat16)
    context_grad = context_grad.reshape(packs_here, PACK, HEADS, HEAD_DIM)
    mixed_grad = lax.map(
        attend_back, (query_heads, key_heads, value_heads, segment, logsum, context_grad)
    )
    mixed_low = mixed_grad.reshape(rows_here, 3 * width).astype(jnp.bfloat16)
    qkv_weight_grad = weight_grad(tokens, mixed_low)
    bias_sums = jnp.sum(mixed_low.astype(jnp.float32), axis=0)
    query_bias_grad = bias_sums[:width]
    value_bias_grad = bias_sums[2 * width :]
    input_grad = back_prod(mixed_low, mix_full) + first_sum_grad
    late = jnp.concatenate(
        [
            split_rows(qkv_weight_grad, devices, width),
            split_rows(attn_weight_grad, devices, width),
        ],
        axis=1,
    )
    late_own = lax.psum_scatter(late, AXES, scatter_dimension=0)
    small_grads = (
        query_bias_grad,
        value_bias_grad,
        attn_bias_grad,
        first_gain_grad,
        first_shift_grad,
        inner_bias_grad,
        outer_bias_grad,
        second_gain_grad,
        second_shift_grad,
        answer_grad,
    )
    own_small = reduce_small(small_grads, devices)
    (
        query_bias_own,
        value_bias_own,
        attn_bias_own,
        first_gain_own,
        first_shift_own,
        inner_bias_own,
        outer_bias_own,
        second_gain_own,
        second_shift_own,
        answer_own,
    ) = own_small
    late_own = late_own.astype(jnp.float32)
    early_own = early_own.astype(jnp.float32)
    owned_grads = (
        join_rows(late_own[: 3 * share], 3),
        query_bias_own,
        value_bias_own,
        late_own[3 * share :],
        attn_bias_own,
        first_gain_own,
        first_shift_own,
        join_rows(early_own[reps * share : 2 * reps * share], reps),
        inner_bias_own,
        early_own[: reps * share],
        outer_bias_own,
        second_gain_own,
        second_shift_own,
        early_own[2 * reps * share :].reshape(share, -1),
        answer_own,
    )
    return (likelihood, result, input_grad) + tuple(owned_grads)


def solution(mesh):
    in_specs = (
        P(("dp", "fsdp"), None),
        P(("dp", "fsdp"), None),
        P(("dp", "fsdp"), None),
        P(("dp", "fsdp"), None),
        P(("dp", "fsdp"), None),
        P(("dp", "fsdp")),
        P(("dp", "fsdp")),
        P(("dp", "fsdp"), None),
        P(("dp", "fsdp")),
        P(("dp", "fsdp")),
        P(("dp", "fsdp")),
        P(("dp", "fsdp"), None),
        P(("dp", "fsdp")),
        P(("dp", "fsdp"), None),
        P(("dp", "fsdp")),
        P(("dp", "fsdp")),
        P(("dp", "fsdp")),
        P(("dp", "fsdp"), None),
        P(("dp", "fsdp")),
    )
    out_specs = (
        P(),
        P(("dp", "fsdp"), None),
        P(("dp", "fsdp"), None),
        P(("dp", "fsdp"), None),
        P(("dp", "fsdp")),
        P(("dp", "fsdp")),
        P(("dp", "fsdp"), None),
        P(("dp", "fsdp")),
        P(("dp", "fsdp")),
        P(("dp", "fsdp")),
        P(("dp", "fsdp"), None),
        P(("dp", "fsdp")),
        P(("dp", "fsdp"), None),
        P(("dp", "fsdp")),
        P(("dp", "fsdp")),
        P(("dp", "fsdp")),
        P(("dp", "fsdp"), None),
        P(("dp", "fsdp")),
    )
    return jax.shard_map(shards, mesh=mesh, in_specs=in_specs, out_specs=out_specs, check_vma=False)
```

```python
import functools, math
import jax, jax.numpy as jnp
from jax import lax
from jax.experimental import pallas as pl
from jax.experimental.pallas import tpu as pltpu
from jax.sharding import PartitionSpec as P
PACK=512; SEGS_PACK=4; HEADS=12; HEAD_DIM=64; LANES=128
MASKED=-1e30
VMEM_MOST=60*1024*1024
F32=jnp.float32; BF16=jnp.bfloat16
def dot_nn(a,b): return jnp.dot(a,b,preferred_element_type=F32)
def dot_nt(a,b): return lax.dot_general(a,b,(((1,),(1,)),((),())),preferred_element_type=F32)
def dot_tn(a,b): return lax.dot_general(a,b,(((0,),(0,)),((),())),preferred_element_type=F32)

def segment_tiles(lens_ref, g):
    row=lax.broadcasted_iota(jnp.int32,(PACK,LANES),0)
    lane=lax.broadcasted_iota(jnp.int32,(PACK,LANES),1)
    seg=jnp.zeros((PACK,LANES),jnp.int32); bound=jnp.int32(0)
    for j in range(SEGS_PACK):
        bound=bound+lens_ref[g,j]
        seg=seg+(row>=bound).astype(jnp.int32)
    place=lane-48
    inside=jnp.logical_and(place>=0,place<SEGS_PACK)
    same=place==seg
    apart=jnp.where(jnp.logical_and(inside,jnp.logical_not(same)),MASKED,0.0)
    own=jnp.where(same,1.0,0.0)
    return lane,apart,own

def head_lanes(lane,h):
    return jnp.logical_and(lane<48,lane%16==h)

def attention_kernel(lens_ref,tok_ref,w_ref,b_ref,mix_ref,ctx_ref,lse_ref,acc_ref):
    g=pl.program_id(0)
    wide=w_ref.shape[1]; width=wide//3
    lane,apart,own=segment_tiles(lens_ref,g)
    apart=apart.astype(BF16); own=own.astype(BF16)
    tok=tok_ref[...]
    mix_ref[:,:width]=((dot_nn(tok,w_ref[:,:width])+b_ref[:,:width]).astype(BF16).astype(F32)*(1/math.sqrt(HEAD_DIM))).astype(BF16)
    mix_ref[:,width:2*width]=(dot_nn(tok,w_ref[:,width:2*width])+b_ref[:,width:2*width]).astype(BF16)
    mix_ref[:,2*width:]=(dot_nn(tok,w_ref[:,2*width:])+b_ref[:,2*width:]).astype(BF16)
    acc_ref[...]=jnp.zeros_like(acc_ref)
    ones=jnp.ones((PACK,LANES),BF16)
    def pair(p,carry):
        at=lambda base: pl.ds(pl.multiple_of(base+p*LANES,LANES),LANES)
        q2=mix_ref[:,at(0)]; k2=mix_ref[:,at(width)]; v2=mix_ref[:,at(2*width)]
        kx=jnp.concatenate([k2,own],axis=1)
        vx=jnp.concatenate([v2,ones],axis=1)
        outs=[]
        for half in range(2):
            qm=jnp.where(lane//HEAD_DIM==half,q2,jnp.zeros_like(q2))
            s=dot_nt(jnp.concatenate([qm,apart],axis=1),kx)
            m=jnp.max(s,axis=1,keepdims=True)
            w=jnp.exp(s-m).astype(BF16)
            o=dot_nn(w,vx)
            total=o[:,LANES:]
            outs.append(o[:,:LANES]/total)
            acc_ref[...]=jnp.where(head_lanes(lane,2*p+half),m+jnp.log(total),acc_ref[...])
        ctx_ref[:,at(0)]=jnp.where(lane<HEAD_DIM,outs[0],outs[1]).astype(BF16)
        return carry
    lax.fori_loop(0,HEADS//2,pair,0)
    lse_ref[...]=acc_ref[...]

def attention(lens,tok,w,b):
    rows,width=tok.shape; wide=w.shape[1]
    return pl.pallas_call(attention_kernel,grid=(rows//PACK,),
        in_specs=[pl.BlockSpec(memory_space=pltpu.SMEM),pl.BlockSpec((PACK,width),lambda g:(g,0)),
                  pl.BlockSpec(w.shape,lambda g:(0,0)),pl.BlockSpec((1,wide),lambda g:(0,0))],
        out_specs=[pl.BlockSpec((PACK,wide),lambda g:(g,0)),pl.BlockSpec((PACK,width),lambda g:(g,0)),pl.BlockSpec((PACK,LANES),lambda g:(g,0))],
        out_shape=[jax.ShapeDtypeStruct((rows,wide),BF16),jax.ShapeDtypeStruct((rows,width),BF16),jax.ShapeDtypeStruct((rows,LANES),F32)],
        scratch_shapes=[pltpu.VMEM((PACK,LANES),F32)],
        compiler_params=pltpu.CompilerParams(vmem_limit_bytes=VMEM_MOST),name='attention')(lens,tok,w,b)

def split_three(x,lane):
    hi=x.astype(BF16).astype(F32)
    rest=x-hi
    mid=rest.astype(BF16).astype(F32)
    return jnp.where(lane<16,hi,jnp.where(lane<32,mid,jnp.where(lane<48,rest-mid,0.0)))

def attention_grad_kernel(lens_ref,mix_ref,ctx_ref,dctx_ref,lse_ref,out_ref):
    g=pl.program_id(0)
    width=ctx_ref.shape[1]
    lane,apart,own=segment_tiles(lens_ref,g)
    prod=dctx_ref[...].astype(F32)*ctx_ref[...].astype(F32)
    hi=prod.astype(BF16); lo=(prod-hi.astype(F32)).astype(BF16)
    wr=lax.broadcasted_iota(jnp.int32,(width,LANES),0); wl=lax.broadcasted_iota(jnp.int32,(width,LANES),1)
    pick=jnp.where(jnp.logical_and(wl<48,wl%16==wr//HEAD_DIM),1.0,0.0).astype(BF16)
    dots=dot_nn(hi,pick)+dot_nn(lo,pick)
    qe=(apart-split_three(lse_ref[...],lane)).astype(BF16)
    de=(-split_three(dots,lane)).astype(BF16)
    def pair(p,carry):
        at=lambda base: pl.ds(pl.multiple_of(base+p*LANES,LANES),LANES)
        q2=mix_ref[:,at(0)]; k2=mix_ref[:,at(width)]; v2=mix_ref[:,at(2*width)]; d2=dctx_ref[:,at(0)]
        kt=k2.T
        dk=jnp.zeros((PACK,LANES),F32); dv=jnp.zeros((PACK,LANES),F32); dqs=[]
        for half in range(2):
            here=lane//HEAD_DIM==half
            qm=jnp.where(here,q2,jnp.zeros_like(q2)); dm=jnp.where(here,d2,jnp.zeros_like(d2))
            mark=jnp.where(head_lanes(lane,2*p+half),1.0,0.0)
            kx=jnp.concatenate([k2,(own+mark).astype(BF16)],axis=1)
            vx=jnp.concatenate([v2,mark.astype(BF16)],axis=1)
            st=dot_nt(kx,jnp.concatenate([qm,qe],axis=1))
            pt=jnp.exp(st)
            dpt=dot_nt(vx,jnp.concatenate([dm,de],axis=1))
            ds=(pt*dpt).astype(BF16)
            dv=dv+dot_nn(pt.astype(BF16),dm)
            dk=dk+dot_nn(ds,qm)
            dqs.append(dot_nn(kt[half*HEAD_DIM:(half+1)*HEAD_DIM],ds))
        dq=jnp.concatenate(dqs,axis=0).T*(1/math.sqrt(HEAD_DIM))
        out_ref[:,at(0)]=dq.astype(BF16)
        out_ref[:,at(width)]=dk.astype(BF16)
        out_ref[:,at(2*width)]=dv.astype(BF16)
        return carry
    lax.fori_loop(0,HEADS//2,pair,0)

def attention_grad(lens,mix,ctx,dctx,lse):
    rows,width=ctx.shape; wide=mix.shape[1]
    b=lambda n: pl.BlockSpec((PACK,n),lambda g:(g,0))
    return pl.pallas_call(attention_grad_kernel,grid=(rows//PACK,),
        in_specs=[pl.BlockSpec(memory_space=pltpu.SMEM),b(wide),b(width),b(width),b(LANES)],
        out_specs=b(wide),out_shape=jax.ShapeDtypeStruct((rows,wide),BF16),
        compiler_params=pltpu.CompilerParams(vmem_limit_bytes=VMEM_MOST),name='attention_grad')(lens,mix,ctx,dctx,lse)
EPS=1e-6
TILE=256
def half_tail(a, e):
    t=1.0/(1.0+0.3275911*a)
    p=t*(0.5*0.254829592+t*(0.5*-0.284496736+t*(0.5*1.421413741+t*(0.5*-1.453152027+t*(0.5*1.061405429)))))
    return p*e

def gelu_pair(x):
    z=jnp.abs(x)*(1/math.sqrt(2))
    e=jnp.exp(-z*z)
    h=half_tail(z,e)
    phi=jnp.where(x>0,1.0-h,h)
    return x*phi, phi+x*(e*(1/math.sqrt(2*math.pi)))

def normed(h):
    c=h-jnp.mean(h,axis=1,keepdims=True)
    f=lax.rsqrt(jnp.mean(c*c,axis=1,keepdims=True)+EPS)
    return c*f,f

def norm_back(e,n,f):
    return f*(e-jnp.mean(e,axis=1,keepdims=True)-n*jnp.mean(e*n,axis=1,keepdims=True))

def row_segments(lens_ref,first_row,rows):
    row=first_row+lax.broadcasted_iota(jnp.int32,(rows,LANES),0)
    lane=lax.broadcasted_iota(jnp.int32,(rows,LANES),1)
    packs=lens_ref.shape[0]
    seg=jnp.zeros((rows,LANES),jnp.int32)
    for g in range(packs):
        end=jnp.int32(g*PACK)
        for j in range(SEGS_PACK):
            end=end+lens_ref[g,j]
            seg=seg+(row>=end).astype(jnp.int32)
    return seg==lane

def feed_forward_kernel(lens_ref,ctx_ref,tok_ref,w_ref,vec_ref,n1_ref,r1_ref,low_ref,act_ref,dg_ref,n2_ref,r2_ref,res_ref,span_ref,score_ref,doc_ref,all_ref):
    i=pl.program_id(0)
    width=ctx_ref.shape[1]; rows=ctx_ref.shape[0]; reps=act_ref.shape[1]//width
    vec=lambda k: vec_ref[k:k+1,:]
    base=2*reps*width
    att=dot_nn(ctx_ref[...],w_ref[:,base:base+width])+vec(0)
    n1,f1=normed(tok_ref[...].astype(F32)+att)
    n1_ref[...]=n1; r1_ref[...]=jnp.broadcast_to(f1,(rows,LANES))
    first=n1*vec(1)+vec(2)
    low=first.astype(BF16); low_ref[...]=low
    out=first+vec(3)
    for q in range(reps):
        c=slice(q*width,(q+1)*width)
        x=dot_nn(low,w_ref[:,c])+vec(8+q)
        a,d=gelu_pair(x)
        a=a.astype(BF16)
        act_ref[:,c]=a; dg_ref[:,c]=d.astype(BF16)
        out=out+dot_nn(a,w_ref[:,(reps+q)*width:(reps+q+1)*width])
    n2,f2=normed(out)
    n2_ref[...]=n2; r2_ref[...]=jnp.broadcast_to(f2,(rows,LANES))
    res=(n2*vec(4)+vec(5)).astype(BF16)
    res_ref[...]=res
    span=dot_nn(res,w_ref[:,base+width:base+width+LANES])
    span_ref[...]=span
    score=jnp.broadcast_to(jnp.sum(span*vec_ref[6:7,:LANES],axis=1,keepdims=True),(rows,LANES))
    score_ref[...]=score
    all_ref[pl.ds(pl.multiple_of(i*rows,rows),rows),:]=score
    @pl.when(i==pl.num_programs(0)-1)
    def _():
        member=row_segments(lens_ref,0,all_ref.shape[0])
        s=jnp.where(member,all_ref[...],MASKED)
        top=jnp.max(s,axis=0,keepdims=True)
        total=jnp.sum(jnp.where(member,jnp.exp(s-top),0.0),axis=0,keepdims=True)
        real=lax.broadcasted_iota(jnp.int32,(1,LANES),1)<lens_ref.shape[0]*SEGS_PACK
        doc_ref[...]=jnp.where(real,top+jnp.log(jnp.where(real,total,1.0)),MASKED)

def once(shape):
    return pl.BlockSpec(shape,lambda i:(0,)*len(shape),pipeline_mode=pl.Buffered(1))

def feed_forward(lens,ctx,tok,w,vec,reps):
    rows,width=ctx.shape; ff=reps*width
    b=lambda n: pl.BlockSpec((TILE,n),lambda i:(i,0))
    s=lambda n,t: jax.ShapeDtypeStruct((rows,n),t)
    return pl.pallas_call(feed_forward_kernel,grid=(rows//TILE,),
        in_specs=[pl.BlockSpec(memory_space=pltpu.SMEM),b(width),b(width),once(w.shape),once(vec.shape)],
        out_specs=[b(width),b(LANES),b(width),b(ff),b(ff),b(width),b(LANES),b(width),b(LANES),b(LANES),once((1,LANES))],
        out_shape=[s(width,F32),s(LANES,F32),s(width,BF16),s(ff,BF16),s(ff,BF16),s(width,F32),s(LANES,F32),s(width,BF16),s(LANES,F32),s(LANES,F32),jax.ShapeDtypeStruct((1,LANES),F32)],
        scratch_shapes=[pltpu.VMEM((rows,LANES),F32)],
        compiler_params=pltpu.CompilerParams(vmem_limit_bytes=VMEM_MOST),name='feed_forward')(lens,ctx,tok,w,vec)

def feed_forward_grad_kernel(lens_ref,own_ids_ref,doc_ref,scores_ref,ids_ref,cot_ref,n2_ref,r2_ref,res_ref,span_ref,score_ref,dg_ref,n1_ref,r1_ref,w_ref,vec_ref,
                   olow_ref,ilow_ref,alow_ref,fsum_ref,dctx_ref,small_ref,spanw_ref,weight_ref,acc_ref):
    i=pl.program_id(0); last=pl.num_programs(0)-1
    rows,width=cot_ref.shape; reps=dg_ref.shape[1]//width
    vec=lambda k: vec_ref[k:k+1,:]
    base=2*reps*width
    @pl.when(i==0)
    def _():
        lane=lax.broadcasted_iota(jnp.int32,(1,LANES),1)
        marg=jnp.zeros((1,LANES),F32)
        for s in range(own_ids_ref.shape[0]):
            hit=ids_ref[...]==own_ids_ref[s].astype(F32)
            x=jnp.where(hit,scores_ref[...],MASKED)
            top=jnp.max(jnp.max(x,axis=1,keepdims=True),axis=0,keepdims=True)
            total=jnp.where(hit,jnp.exp(x-top),0.0)
            total=jnp.sum(jnp.sum(total,axis=1,keepdims=True),axis=0,keepdims=True)
            marg=jnp.where(lane==s,top+jnp.log(total),marg)
        weight_ref[...]=jnp.exp(doc_ref[...]-marg)
        small_ref[...]=jnp.zeros_like(small_ref)
        acc_ref[...]=jnp.zeros_like(acc_ref)
    member=row_segments(lens_ref,i*rows,rows)
    part=jnp.where(member,jnp.exp(jnp.where(member,score_ref[...]-doc_ref[...],0.0))*weight_ref[...],0.0)
    tw=jnp.sum(part,axis=1,keepdims=True)
    ans=vec_ref[6:7,:LANES]
    small_ref[6:7,:LANES]+=jnp.sum(tw*span_ref[...],axis=0,keepdims=True)
    sg=(tw*ans).astype(BF16)
    acc_ref[...]+=dot_tn(res_ref[...],sg)
    @pl.when(i==last)
    def _():
        spanw_ref[...]=acc_ref[...].astype(BF16)
    rg=cot_ref[...].astype(F32)+dot_nt(sg,w_ref[:,base+width:base+width+LANES])
    n2=n2_ref[...]
    def colsum(k,v):
        small_ref[k:k+1,:]+=jnp.sum(v,axis=0,keepdims=True)
    colsum(0,rg*n2); colsum(1,rg)
    ssum=norm_back(rg*vec(4),n2,r2_ref[:,:1])
    olow=ssum.astype(BF16); olow_ref[...]=olow
    colsum(2,olow.astype(F32))
    fg=ssum
    for q in range(reps):
        c=slice(q*width,(q+1)*width)
        il=(dot_nt(olow,w_ref[:,(reps+q)*width:(reps+q+1)*width])*dg_ref[:,c].astype(F32)).astype(BF16)
        ilow_ref[:,c]=il
        colsum(8+q,il.astype(F32))
        fg=fg+dot_nt(il,w_ref[:,c])
    n1=n1_ref[...]
    colsum(3,fg*n1); colsum(4,fg)
    fsum=norm_back(fg*vec(1),n1,r1_ref[:,:1])
    fsum_ref[...]=fsum
    alow=fsum.astype(BF16); alow_ref[...]=alow
    colsum(5,alow.astype(F32))
    dctx_ref[...]=dot_nt(alow,w_ref[:,base:base+width]).astype(BF16)

def feed_forward_grad(lens,own_ids,doc,scores,ids,cot,n2,r2,res,span,score,dg,n1,r1,w,vec):
    rows,width=cot.shape; ff=dg.shape[1]
    b=lambda n: pl.BlockSpec((TILE,n),lambda i:(i,0))
    s=lambda n,t: jax.ShapeDtypeStruct((rows,n),t)
    sm=pl.BlockSpec(memory_space=pltpu.SMEM)
    return pl.pallas_call(feed_forward_grad_kernel,grid=(rows//TILE,),
        in_specs=[sm,sm,once(doc.shape),once(scores.shape),once(ids.shape),b(width),b(width),b(LANES),b(width),b(LANES),b(LANES),b(ff),b(width),b(LANES),once(w.shape),once(vec.shape)],
        out_specs=[b(width),b(ff),b(width),b(width),b(width),once(vec.shape),once((width,LANES))],
        out_shape=[s(width,BF16),s(ff,BF16),s(width,BF16),s(width,F32),s(width,BF16),jax.ShapeDtypeStruct(vec.shape,F32),jax.ShapeDtypeStruct((width,LANES),BF16)],
        scratch_shapes=[pltpu.VMEM((1,LANES),F32),pltpu.VMEM((width,LANES),F32)],
        compiler_params=pltpu.CompilerParams(vmem_limit_bytes=VMEM_MOST),name='feed_forward_grad')(lens,own_ids,doc,scores,ids,cot,n2,r2,res,span,score,dg,n1,r1,w,vec)

def early_kernel(reps,low_ref,ilow_ref,act_ref,olow_ref,ctx_ref,alow_ref,out_ref):
    j=pl.program_id(0)
    @pl.when(j<reps)
    def _(): out_ref[...]=dot_tn(low_ref[...],ilow_ref[...]).astype(BF16)
    @pl.when(jnp.logical_and(j>=reps,j<2*reps))
    def _(): out_ref[...]=dot_tn(act_ref[...],olow_ref[...]).astype(BF16)
    @pl.when(j==2*reps)
    def _(): out_ref[...]=dot_tn(ctx_ref[...],alow_ref[...]).astype(BF16)

def early_grads(low,ilow,act,olow,ctx,alow):
    rows,width=low.shape; reps=act.shape[1]//width
    full=once((rows,width))
    return pl.pallas_call(functools.partial(early_kernel,reps),grid=(2*reps+1,),
        in_specs=[full,pl.BlockSpec((rows,width),lambda j:(0,jnp.minimum(j,reps-1))),pl.BlockSpec((rows,width),lambda j:(0,jnp.clip(j-reps,0,reps-1))),full,full,full],
        out_specs=pl.BlockSpec((width,width),lambda j:(0,j)),out_shape=jax.ShapeDtypeStruct((width,(2*reps+1)*width),BF16),
        compiler_params=pltpu.CompilerParams(vmem_limit_bytes=VMEM_MOST),name='early_weight_grads')(low,ilow,act,olow,ctx,alow)

def late_kernel(tok_ref,mg_ref,out_ref,sum_ref):
    mg=mg_ref[...]
    out_ref[...]=dot_tn(tok_ref[...],mg).astype(BF16)
    sum_ref[...]=jnp.broadcast_to(jnp.sum(mg.astype(F32),axis=0,keepdims=True),sum_ref.shape)

def late_grads(tok,mg):
    rows,width=tok.shape; wide=mg.shape[1]
    return pl.pallas_call(late_kernel,grid=(wide//width,),
        in_specs=[once((rows,width)),pl.BlockSpec((rows,width),lambda j:(0,j))],
        out_specs=[pl.BlockSpec((width,width),lambda j:(0,j)),pl.BlockSpec((8,width),lambda j:(0,j))],
        out_shape=[jax.ShapeDtypeStruct((width,wide),BF16),jax.ShapeDtypeStruct((8,wide),F32)],
        compiler_params=pltpu.CompilerParams(vmem_limit_bytes=VMEM_MOST),name='late_weight_grads')(tok,mg)
AXES = ("dp", "fsdp")


def pack_lanes(parts):
    flat = jnp.concatenate(parts, axis=-1)
    wide = -(-flat.shape[-1] // LANES) * LANES
    flat = jnp.pad(flat, [(0, 0)] * (flat.ndim - 1) + [(0, wide - flat.shape[-1])])
    return flat.reshape(flat.shape[:-1] + (wide // LANES, LANES))


def unpack_lanes(packed, sizes):
    flat = packed.reshape(packed.shape[:-2] + (-1,))
    starts = [sum(sizes[:i]) for i in range(len(sizes))]
    return [flat[..., a : a + n] for a, n in zip(starts, sizes)]


def to_all(block, devices):
    return lax.all_to_all(jnp.broadcast_to(block[None], (devices,) + block.shape), AXES, 0, 0)


def shards(
    tokens,
    cotangent,
    doc_lengths,
    query_ids,
    qkv_weight,
    query_bias,
    value_bias,
    attn_weight,
    attn_bias,
    first_gain,
    first_shift,
    inner_weight,
    inner_bias,
    outer_weight,
    outer_bias,
    second_gain,
    second_shift,
    span_weight,
    answer_vector,
):
    rows, width = tokens.shape
    packs_here = rows // PACK
    devices = lax.axis_size("dp") * lax.axis_size("fsdp")
    share = qkv_weight.shape[0]
    ff = inner_weight.shape[1]
    reps = ff // width
    segs_here = packs_here * SEGS_PACK
    span = span_weight.shape[1]

    row_params = (attn_bias, first_gain, first_shift, outer_bias, second_gain, second_shift)
    smalls = row_params + (inner_bias, answer_vector, query_bias, value_bias)
    sizes = [v.shape[0] for v in smalls]
    id_row = jnp.pad(
        query_ids[:, 0].astype(F32)[None], ((0, 0), (0, LANES - segs_here)), constant_values=-1.0
    )
    packed = jnp.concatenate([pack_lanes([v.astype(F32) for v in smalls]), id_row], axis=0)
    small_all = to_all(packed, devices)
    ids_all = small_all[:, -1]
    columns = unpack_lanes(small_all[:, :-1], sizes)
    vectors = jnp.concatenate(
        [c.reshape(1, width) for c in columns[: len(row_params)]]
        + [
            jnp.pad(columns[-3].reshape(1, -1), ((0, 0), (0, width - span))),
            jnp.zeros((1, width), F32),
            columns[-4].reshape(devices, reps, share).transpose(1, 0, 2).reshape(reps, width),
        ],
        axis=0,
    )
    vectors = jnp.pad(vectors, ((0, -vectors.shape[0] % 8), (0, 0)))
    query_row = columns[-2].reshape(1, width)
    value_row = columns[-1].reshape(1, width)
    qkv_row = jnp.concatenate([query_row, jnp.zeros_like(query_row), value_row], axis=1)

    mix_full = lax.all_gather(qkv_weight, AXES, axis=0, tiled=True)
    inner_turned = (
        inner_weight.reshape(share, devices, reps, share).transpose(0, 2, 1, 3).reshape(share, ff)
    )
    outer_blocks = [outer_weight[q * share : (q + 1) * share] for q in range(reps)]
    rest = jnp.concatenate([inner_turned] + outer_blocks + [attn_weight, span_weight], axis=1)
    rest_full = lax.all_gather(rest, AXES, axis=0, tiled=True)

    mixed, context, logsum = attention(doc_lengths, tokens, mix_full, qkv_row)
    (
        normed_one,
        factor_one,
        first_low,
        active,
        gelu_slope,
        normed_two,
        factor_two,
        result,
        span_rows,
        token_score,
        doc_score,
    ) = feed_forward(doc_lengths, context, tokens, rest_full, vectors, reps)
    scores_all = to_all(doc_score, devices)[:, 0]

    outer_low, inner_low, attended_low, first_sum_grad, context_grad, small_sums, span_grad = (
        feed_forward_grad(
            doc_lengths,
            query_ids.reshape(-1),
            doc_score,
            scores_all,
            ids_all,
            cotangent,
            normed_two,
            factor_two,
            result,
            span_rows,
            token_score,
            gelu_slope,
            normed_one,
            factor_one,
            rest_full,
            vectors,
        )
    )
    early = early_grads(first_low, inner_low, active, outer_low, context, attended_low)
    early_own = lax.psum_scatter(early, "dp", scatter_dimension=0, tiled=True)
    early_own = lax.psum_scatter(early_own, "fsdp", scatter_dimension=0, tiled=True).astype(F32)

    mixed_grad = attention_grad(doc_lengths, mixed, context, context_grad, logsum)
    mix_grad, bias_sums = late_grads(tokens, mixed_grad)
    late = jnp.concatenate([mix_grad, span_grad], axis=1)
    late_own = lax.psum_scatter(late, AXES, scatter_dimension=0, tiled=True).astype(F32)
    input_grad = dot_nt(mixed_grad, mix_full) + first_sum_grad

    n_rows = small_sums.shape[0]
    by_owner = small_sums.reshape(n_rows, devices, share).transpose(1, 0, 2)
    biases = bias_sums[0].reshape(3, devices, share).transpose(1, 0, 2)
    small_grads = pack_lanes(
        [
            by_owner.reshape(devices, n_rows * share),
            biases.reshape(devices, 3 * share),
            small_sums[6, :span].reshape(devices, span // devices),
        ]
    )
    mine = jnp.sum(lax.all_to_all(small_grads, AXES, 0, 0), axis=0)
    own_rows, own_biases, answer_own = unpack_lanes(
        mine, [n_rows * share, 3 * share, span // devices]
    )
    row_of = lambda k: own_rows[k * share : (k + 1) * share]

    queries = lax.broadcasted_iota(F32, (packs_here * devices, 1), 0)
    member_query = ids_all[:, :segs_here].reshape(1, -1) == queries
    marginal = jax.nn.logsumexp(
        jnp.where(member_query, scores_all[:, :segs_here].reshape(1, -1), MASKED), axis=1
    )
    inner_own = (
        early_own[:, :ff].reshape(share, reps, devices, share).transpose(0, 2, 1, 3)
    ).reshape(share, ff)
    outer_own = jnp.concatenate(
        [early_own[:, ff + q * width : ff + (q + 1) * width] for q in range(reps)], axis=0
    )
    return (
        jnp.sum(marginal),
        result,
        input_grad,
        late_own[:, : 3 * width],
        own_biases[:share],
        own_biases[2 * share :],
        early_own[:, 2 * ff :],
        row_of(5),
        row_of(3),
        row_of(4),
        inner_own,
        own_rows[8 * share : (8 + reps) * share],
        outer_own,
        row_of(2),
        row_of(0),
        row_of(1),
        late_own[:, 3 * width :],
        answer_own,
    )


def solution(mesh):
    rows = P(AXES, None)
    flat = P(AXES)
    in_specs = (rows,) * 4 + (rows, flat, flat, rows, flat, flat, flat, rows, flat, rows)
    in_specs += (flat, flat, flat, rows, flat)
    out_specs = (P(), rows, rows, rows, flat, flat, rows, flat, flat, flat, rows, flat, rows)
    out_specs += (flat, flat, flat, rows, flat)
    return jax.shard_map(shards, mesh=mesh, in_specs=in_specs, out_specs=out_specs, check_vma=False)
```

```python
import functools, math
import jax, jax.numpy as jnp
from jax import lax
from jax.experimental import pallas as pl
from jax.experimental.pallas import tpu as pltpu
from jax.sharding import PartitionSpec as P
PACK=512; SEGS_PACK=4; HEADS=12; HEAD_DIM=64; LANES=128; SUBLANES=8
MASKED=-1e30
VMEM_MOST=60*1024*1024
F32=jnp.float32; BF16=jnp.bfloat16
def swap(block, axis, mask):
    size = lax.axis_size(axis)
    return lax.ppermute(block, axis, [(i, i ^ mask) for i in range(size)])


def bit_orders(dp):
    bits = [1 << t for t in range(dp.bit_length() - 1)]
    first, others = bits[:1], bits[1:]
    return first + others, first + others[1:] + others[:1]


def offsets(order):
    found = [0]
    for bit in reversed(order):
        found = found + [f | bit for f in found]
    return found


def gather_near(shard):
    if shard.shape[0] % SUBLANES:
        return [lax.all_gather(shard, "fsdp", axis=0, tiled=True)]
    return [shard] + [swap(shard, "fsdp", k) for k in range(1, lax.axis_size("fsdp"))]


class Gathering:
    def __init__(self, pieces, orders, split):
        self.orders = orders
        self.near = len(pieces)
        self.left = len(orders[0]) - 1
        cut = [[p[:, :split] for p in pieces], [p[:, split:] for p in pieces]]
        self.blocks = [jnp.stack(c) for c in cut]
        self.came = None

    def send(self):
        self.came = [swap(b, "dp", o[self.left]) for b, o in zip(self.blocks, self.orders)]

    def join(self):
        self.blocks = [jnp.concatenate([b, c], axis=0) for b, c in zip(self.blocks, self.came)]
        self.left -= 1

    def advance(self, left):
        while self.left > left:
            self.send()
            self.join()

    def parts(self):
        return [self.blocks[0], self.came[0], self.blocks[1], self.came[1]]


def part(block, dim, which):
    return lax.dynamic_index_in_dim(block, which, dim, keepdims=False)


def add_low(a, b):
    return (a.astype(F32) + b.astype(F32)).astype(BF16)


class Reduction:
    def __init__(self, keep, give, order):
        self.order = list(order)
        self.bits = sorted(order, reverse=True)
        self.keep, self.give = keep, give
        self.came = None

    def send(self):
        self.came = swap(self.give, "dp", self.order[0])

    def add(self):
        total = add_low(self.keep, self.came)
        self.bits.remove(self.order.pop(0))
        if not self.order:
            self.keep = total
            return
        total = total.reshape((2,) * len(self.bits) + total.shape[-2:])
        dim = self.bits.index(self.order[0])
        own = (lax.axis_index("dp") // self.order[0]) % 2
        flat = lambda x: x.reshape((-1,) + x.shape[-2:])
        self.keep, self.give = flat(part(total, dim, own)), flat(part(total, dim, 1 - own))

    def advance(self, left):
        while len(self.order) > left:
            self.send()
            self.add()


def start_near(blocks):
    fsdp = lax.axis_size("fsdp")
    split = [b.reshape(fsdp, -1, b.shape[-1]) for b in blocks]
    own = lax.axis_index("fsdp")
    take = lambda k: jnp.concatenate([part(b, 0, own ^ k) for b in split], axis=1)
    return take(0), [swap(take(k), "fsdp", k) for k in range(1, fsdp)]


def add_near(own, came):
    total = own.astype(F32)
    for block in came:
        total = total + block.astype(F32)
    return total


def tie(*groups):
    return lax.optimization_barrier(groups)


def once(shape):
    return pl.BlockSpec(shape,lambda i:(0,)*len(shape),pipeline_mode=pl.Buffered(1))

def dot_nn(a,b): return jnp.dot(a,b,preferred_element_type=F32)
def dot_nt(a,b): return lax.dot_general(a,b,(((1,),(1,)),((),())),preferred_element_type=F32)
def dot_tn(a,b): return lax.dot_general(a,b,(((0,),(0,)),((),())),preferred_element_type=F32)

def segment_tiles(lens_ref, g):
    row=lax.broadcasted_iota(jnp.int32,(PACK,LANES),0)
    lane=lax.broadcasted_iota(jnp.int32,(PACK,LANES),1)
    seg=jnp.zeros((PACK,LANES),jnp.int32); bound=jnp.int32(0)
    for j in range(SEGS_PACK):
        bound=bound+lens_ref[g,j]
        seg=seg+(row>=bound).astype(jnp.int32)
    place=lane-48
    inside=jnp.logical_and(place>=0,place<SEGS_PACK)
    same=place==seg
    apart=jnp.where(jnp.logical_and(inside,jnp.logical_not(same)),MASKED,0.0)
    own=jnp.where(same,1.0,0.0)
    return lane,apart,own

def head_lanes(lane,h):
    return jnp.logical_and(lane<48,lane%16==h)

def assemble(me_ref, orders, fsdp, parts, full_ref, sems):
    copies, start = [], 0
    for color, order in enumerate(orders):
        cols = parts[2 * color].shape[2]
        for half in range(2):
            src = parts[2 * color + half]
            near = offsets(order)[half * src.shape[0] // fsdp :]
            for n in range(src.shape[0]):
                block = (near[n // fsdp] ^ me_ref[0]) * fsdp
                block += (n % fsdp) ^ me_ref[1] if fsdp > 1 else 0
                place = pl.ds(pl.multiple_of(block * src.shape[1], SUBLANES), src.shape[1])
                copies.append(
                    pltpu.make_async_copy(
                        src.at[n], full_ref.at[place, pl.ds(start, cols)], sems.at[len(copies)]
                    )
                )
        start += cols
    for copy in copies:
        copy.start()
    for copy in copies:
        copy.wait()


def whole_div(x, n):
    return jnp.floor((x.astype(F32) + 0.5) * (1.0 / n)).astype(jnp.int32)


def unpack_small(block, share, rows_in, answers):
    width = block.shape[0]
    count = -(-(rows_in * share + answers) // LANES)
    row = lax.broadcasted_iota(jnp.int32, (width, LANES), 0)
    lane = lax.broadcasted_iota(jnp.int32, (width, LANES), 1)
    turned = jnp.concatenate(
        [dot_tn(block, (row == lane * share + k).astype(BF16)) for k in range(count)], axis=0
    ).astype(BF16)
    entry = lax.broadcasted_iota(jnp.int32, (count * LANES, width), 0)
    place = lax.broadcasted_iota(jnp.int32, (count * LANES, width), 1)
    owner = whole_div(lax.broadcasted_iota(jnp.int32, (LANES, width), 1), share)
    owns = (lax.broadcasted_iota(jnp.int32, (LANES, width), 0) == owner).astype(BF16)
    spread = dot_nn(turned, owns)
    fits = entry - whole_div(entry, share) * share == place - whole_div(place, share) * share
    spread = jnp.where(fits, spread, 0.0).astype(BF16)
    vector = lax.broadcasted_iota(jnp.int32, (16, count * LANES), 0)
    source = whole_div(lax.broadcasted_iota(jnp.int32, (16, count * LANES), 1), share)
    vectors = dot_nn((vector == source).astype(BF16), spread)
    line = lax.broadcasted_iota(jnp.int32, (LANES, LANES), 1)
    owns = (lax.broadcasted_iota(jnp.int32, (LANES, LANES), 0) == whole_div(line, answers)).astype(BF16)
    spread = dot_nn(turned, owns)
    entry = lax.broadcasted_iota(jnp.int32, spread.shape, 0) - rows_in * share
    place = lax.broadcasted_iota(jnp.int32, spread.shape, 1)
    fits = entry == place - whole_div(place, answers) * answers
    return vectors, jnp.sum(jnp.where(fits, spread, 0.0), axis=0, keepdims=True)


def attention_kernel(orders,fsdp,small,lens_ref,me_ref,tok_ref,p0,p1,p2,p3,w_ref,vec_ref,mix_ref,ctx_ref,lse_ref,acc_ref,sems):
    pack=pl.program_id(0)
    width=tok_ref.shape[1]; wide=3*width
    @pl.when(pack==0)
    def _():
        assemble(me_ref,orders,fsdp,(p0,p1,p2,p3),w_ref,sems)
        vectors,answer=unpack_small(w_ref[:,wide:],*small)
        vec_ref[...]=vectors
        vec_ref[15:16,:LANES]=answer
    query_row=vec_ref[6:7,:]; value_row=vec_ref[7:8,:]
    lane,apart,own=segment_tiles(lens_ref,pack)
    apart=apart.astype(BF16); own=own.astype(BF16)
    tok=tok_ref[...]
    mix_ref[:,:width]=((dot_nn(tok,w_ref[:,:width])+query_row).astype(BF16).astype(F32)*(1/math.sqrt(HEAD_DIM))).astype(BF16)
    mix_ref[:,width:2*width]=dot_nn(tok,w_ref[:,width:2*width]).astype(BF16)
    mix_ref[:,2*width:]=(dot_nn(tok,w_ref[:,2*width:wide])+value_row).astype(BF16)
    acc_ref[...]=jnp.zeros_like(acc_ref)
    ones=jnp.ones((PACK,LANES),BF16)
    def pair(p,carry):
        at=lambda base: pl.ds(pl.multiple_of(base+p*LANES,LANES),LANES)
        q2=mix_ref[:,at(0)]; k2=mix_ref[:,at(width)]; v2=mix_ref[:,at(2*width)]
        kx=jnp.concatenate([k2,own],axis=1)
        vx=jnp.concatenate([v2,ones],axis=1)
        outs=[]
        for half in range(2):
            qm=jnp.where(lane//HEAD_DIM==half,q2,jnp.zeros_like(q2))
            s=dot_nt(jnp.concatenate([qm,apart],axis=1),kx)
            m=jnp.max(s,axis=1,keepdims=True)
            w=jnp.exp(s-m).astype(BF16)
            o=dot_nn(w,vx)
            total=o[:,LANES:]
            outs.append(o[:,:LANES]/total)
            acc_ref[...]=jnp.where(head_lanes(lane,2*p+half),m+jnp.log(total),acc_ref[...])
        ctx_ref[:,at(0)]=jnp.where(lane<HEAD_DIM,outs[0],outs[1]).astype(BF16)
        return carry
    lax.fori_loop(0,HEADS//2,pair,0)
    lse_ref[...]=acc_ref[...]

def attention(lens,me,tok,parts,orders,fsdp,small):
    rows,width=tok.shape; share=parts[0].shape[1]; full=parts[0].shape[2]+parts[2].shape[2]
    hbm=pl.BlockSpec(memory_space=pl.ANY)
    sm=pl.BlockSpec(memory_space=pltpu.SMEM)
    wide=3*width
    sizes=((wide,BF16),(width,BF16),(LANES,F32))
    outs=[jax.ShapeDtypeStruct((rows,n),t) for n,t in sizes]
    heads=[jax.ShapeDtypeStruct((width,full),BF16),jax.ShapeDtypeStruct((16,width),F32)]
    fixed=[once((width,full)),once((16,width))]
    cost=pl.CostEstimate(flops=2*rows*width*wide+8*rows*PACK*width,bytes_accessed=rows*wide*4,transcendentals=HEADS*PACK*rows)
    spec=lambda n: pl.BlockSpec((PACK,n),lambda g:(g,0))
    return pl.pallas_call(functools.partial(attention_kernel,orders,fsdp,small),grid=(rows//PACK,),
        in_specs=[sm,sm,spec(width)]+[hbm]*4,out_specs=fixed+[spec(n) for n,_ in sizes],out_shape=heads+outs,
        scratch_shapes=[pltpu.VMEM((PACK,LANES),F32),pltpu.SemaphoreType.DMA((4*parts[0].shape[0],))],
        compiler_params=pltpu.CompilerParams(vmem_limit_bytes=VMEM_MOST),name='attention',cost_estimate=cost)(lens,me,tok,*parts)

def split_three(x,lane):
    hi=x.astype(BF16).astype(F32)
    rest=x-hi
    mid=rest.astype(BF16).astype(F32)
    return jnp.where(lane<16,hi,jnp.where(lane<32,mid,jnp.where(lane<48,rest-mid,0.0)))

def attention_grad_kernel(pairs,lens_ref,mix_ref,ctx_ref,dctx_ref,lse_ref,out_ref):
    g=pl.program_id(0)
    width=ctx_ref.shape[1]
    part=(pairs[1]-pairs[0])*LANES
    lane,apart,own=segment_tiles(lens_ref,g)
    prod=dctx_ref[...].astype(F32)*ctx_ref[...].astype(F32)
    hi=prod.astype(BF16); lo=(prod-hi.astype(F32)).astype(BF16)
    wr=lax.broadcasted_iota(jnp.int32,(width,LANES),0); wl=lax.broadcasted_iota(jnp.int32,(width,LANES),1)
    pick=jnp.where(jnp.logical_and(wl<48,wl%16==wr//HEAD_DIM),1.0,0.0).astype(BF16)
    dots=dot_nn(hi,pick)+dot_nn(lo,pick)
    qe=(apart-split_three(lse_ref[...],lane)).astype(BF16)
    de=(-split_three(dots,lane)).astype(BF16)
    def pair(p,carry):
        at=lambda base: pl.ds(pl.multiple_of(base+p*LANES,LANES),LANES)
        q2=mix_ref[:,at(0)]; k2=mix_ref[:,at(width)]; v2=mix_ref[:,at(2*width)]; d2=dctx_ref[:,at(0)]
        kt=k2.T
        dk=jnp.zeros((PACK,LANES),F32); dv=jnp.zeros((PACK,LANES),F32); dqs=[]
        for half in range(2):
            here=lane//HEAD_DIM==half
            qm=jnp.where(here,q2,jnp.zeros_like(q2)); dm=jnp.where(here,d2,jnp.zeros_like(d2))
            mark=jnp.where(head_lanes(lane,2*p+half),1.0,0.0)
            kx=jnp.concatenate([k2,(own+mark).astype(BF16)],axis=1)
            vx=jnp.concatenate([v2,mark.astype(BF16)],axis=1)
            st=dot_nt(kx,jnp.concatenate([qm,qe],axis=1))
            pt=jnp.exp(st)
            dpt=dot_nt(vx,jnp.concatenate([dm,de],axis=1))
            ds=(pt*dpt).astype(BF16)
            dv=dv+dot_nn(pt.astype(BF16),dm)
            dk=dk+dot_nn(ds,qm)
            dqs.append(dot_nn(kt[half*HEAD_DIM:(half+1)*HEAD_DIM],ds))
        dq=jnp.concatenate(dqs,axis=0).T*(1/math.sqrt(HEAD_DIM))
        to=lambda base: pl.ds(pl.multiple_of(base+(p-pairs[0])*LANES,LANES),LANES)
        out_ref[:,to(0)]=dq.astype(BF16)
        out_ref[:,to(part)]=dk.astype(BF16)
        out_ref[:,to(2*part)]=dv.astype(BF16)
        return carry
    lax.fori_loop(pairs[0],pairs[1],pair,0)

def attention_grad(pairs,lens,mix,ctx,dctx,lse):
    rows,width=ctx.shape; wide=mix.shape[1]; part=3*(pairs[1]-pairs[0])*LANES
    b=lambda n: pl.BlockSpec((PACK,n),lambda g:(g,0))
    share=(pairs[1]-pairs[0])/(HEADS//2)
    return pl.pallas_call(functools.partial(attention_grad_kernel,pairs),grid=(rows//PACK,),
        in_specs=[pl.BlockSpec(memory_space=pltpu.SMEM),b(wide),b(width),b(width),b(LANES)],
        out_specs=b(part),out_shape=jax.ShapeDtypeStruct((rows,part),BF16),
        compiler_params=pltpu.CompilerParams(vmem_limit_bytes=VMEM_MOST),name='attention_grad',
        cost_estimate=pl.CostEstimate(flops=int(share*20*rows*PACK*width),bytes_accessed=rows*wide*4,transcendentals=int(share*HEADS*rows*PACK)))(lens,mix,ctx,dctx,lse)
EPS=1e-6
TILE=256
def half_tail(a, e):
    t=1.0/(1.0+0.3275911*a)
    p=t*(0.5*0.254829592+t*(0.5*-0.284496736+t*(0.5*1.421413741+t*(0.5*-1.453152027+t*(0.5*1.061405429)))))
    return p*e

def gelu_pair(x):
    z=jnp.abs(x)*(1/math.sqrt(2))
    e=jnp.exp(-z*z)
    h=half_tail(z,e)
    phi=jnp.where(x>0,1.0-h,h)
    return x*phi, phi+x*(e*(1/math.sqrt(2*math.pi)))

def normed(h):
    c=h-jnp.mean(h,axis=1,keepdims=True)
    f=lax.rsqrt(jnp.mean(c*c,axis=1,keepdims=True)+EPS)
    return c*f,f

def norm_back(e,n,f):
    return f*(e-jnp.mean(e,axis=1,keepdims=True)-n*jnp.mean(e*n,axis=1,keepdims=True))

def row_segments(lens_ref,first_row,rows):
    row=first_row+lax.broadcasted_iota(jnp.int32,(rows,LANES),0)
    lane=lax.broadcasted_iota(jnp.int32,(rows,LANES),1)
    packs=lens_ref.shape[0]
    seg=jnp.zeros((rows,LANES),jnp.int32)
    for g in range(packs):
        end=jnp.int32(g*PACK)
        for j in range(SEGS_PACK):
            end=end+lens_ref[g,j]
            seg=seg+(row>=end).astype(jnp.int32)
    return seg==lane

def feed_forward_kernel(lens_ref,ctx_ref,tok_ref,w_ref,vec_ref,n1_ref,r1_ref,low_ref,act_ref,dg_ref,n2_ref,r2_ref,res_ref,span_ref,score_ref,doc_ref,all_ref):
    i=pl.program_id(0)
    width=ctx_ref.shape[1]; rows=ctx_ref.shape[0]; reps=act_ref.shape[1]//width
    vec=lambda k: vec_ref[k:k+1,:]
    base=2*reps*width
    att=dot_nn(ctx_ref[...],w_ref[:,base:base+width])+vec(0)
    n1,f1=normed(tok_ref[...].astype(F32)+att)
    n1_ref[...]=n1; r1_ref[...]=jnp.broadcast_to(f1,(rows,LANES))
    first=n1*vec(1)+vec(2)
    low=first.astype(BF16); low_ref[...]=low
    out=first+vec(3)
    for q in range(reps):
        c=slice(q*width,(q+1)*width)
        x=dot_nn(low,w_ref[:,c])+vec(8+q)
        a,d=gelu_pair(x)
        a=a.astype(BF16)
        act_ref[:,c]=a; dg_ref[:,c]=d.astype(BF16)
        out=out+dot_nn(a,w_ref[:,(reps+q)*width:(reps+q+1)*width])
    n2,f2=normed(out)
    n2_ref[...]=n2; r2_ref[...]=jnp.broadcast_to(f2,(rows,LANES))
    res=(n2*vec(4)+vec(5)).astype(BF16)
    res_ref[...]=res
    span=dot_nn(res,w_ref[:,base+width:base+width+LANES])
    span_ref[...]=span
    score=jnp.broadcast_to(jnp.sum(span*vec_ref[15:16,:LANES],axis=1,keepdims=True),(rows,LANES))
    score_ref[...]=score
    all_ref[pl.ds(pl.multiple_of(i*rows,rows),rows),:]=score
    @pl.when(i==pl.num_programs(0)-1)
    def _():
        member=row_segments(lens_ref,0,all_ref.shape[0])
        s=jnp.where(member,all_ref[...],MASKED)
        top=jnp.max(s,axis=0,keepdims=True)
        total=jnp.sum(jnp.where(member,jnp.exp(s-top),0.0),axis=0,keepdims=True)
        real=lax.broadcasted_iota(jnp.int32,(1,LANES),1)<lens_ref.shape[0]*SEGS_PACK
        doc_ref[...]=jnp.where(real,top+jnp.log(jnp.where(real,total,1.0)),MASKED)

def feed_forward(lens,ctx,tok,w,vec,reps):
    rows,width=ctx.shape; ff=reps*width
    b=lambda n: pl.BlockSpec((TILE,n),lambda i:(i,0))
    s=lambda n,t: jax.ShapeDtypeStruct((rows,n),t)
    return pl.pallas_call(feed_forward_kernel,grid=(rows//TILE,),
        in_specs=[pl.BlockSpec(memory_space=pltpu.SMEM),b(width),b(width),once(w.shape),once(vec.shape)],
        out_specs=[b(width),b(LANES),b(width),b(ff),b(ff),b(width),b(LANES),b(width),b(LANES),b(LANES),once((1,LANES))],
        out_shape=[s(width,F32),s(LANES,F32),s(width,BF16),s(ff,BF16),s(ff,BF16),s(width,F32),s(LANES,F32),s(width,BF16),s(LANES,F32),s(LANES,F32),jax.ShapeDtypeStruct((1,LANES),F32)],
        scratch_shapes=[pltpu.VMEM((rows,LANES),F32)],
        compiler_params=pltpu.CompilerParams(vmem_limit_bytes=VMEM_MOST),name='feed_forward')(lens,ctx,tok,w,vec)

def feed_forward_grad_kernel(lens_ref,own_ids_ref,doc_ref,scores_ref,ids_ref,cot_ref,n2_ref,r2_ref,res_ref,span_ref,score_ref,dg_ref,n1_ref,r1_ref,w_ref,vec_ref,
                   olow_ref,ilow_ref,alow_ref,fsum_ref,dctx_ref,small_ref,spanw_ref,weight_ref,acc_ref):
    i=pl.program_id(0); last=pl.num_programs(0)-1
    rows,width=cot_ref.shape; reps=dg_ref.shape[1]//width
    vec=lambda k: vec_ref[k:k+1,:]
    base=2*reps*width
    @pl.when(i==0)
    def _():
        lane=lax.broadcasted_iota(jnp.int32,(1,LANES),1)
        marg=jnp.zeros((1,LANES),F32)
        for s in range(own_ids_ref.shape[0]):
            hit=ids_ref[...]==own_ids_ref[s].astype(F32)
            x=jnp.where(hit,scores_ref[...],MASKED)
            top=jnp.max(jnp.max(x,axis=1,keepdims=True),axis=0,keepdims=True)
            total=jnp.where(hit,jnp.exp(x-top),0.0)
            total=jnp.sum(jnp.sum(total,axis=1,keepdims=True),axis=0,keepdims=True)
            marg=jnp.where(lane==s,top+jnp.log(total),marg)
        weight_ref[...]=jnp.exp(doc_ref[...]-marg)
        small_ref[...]=jnp.zeros_like(small_ref)
        acc_ref[...]=jnp.zeros_like(acc_ref)
    member=row_segments(lens_ref,i*rows,rows)
    part=jnp.where(member,jnp.exp(jnp.where(member,score_ref[...]-doc_ref[...],0.0))*weight_ref[...],0.0)
    tw=jnp.sum(part,axis=1,keepdims=True)
    ans=vec_ref[15:16,:LANES]
    small_ref[15:16,:LANES]+=jnp.sum(tw*span_ref[...],axis=0,keepdims=True)
    sg=(tw*ans).astype(BF16)
    acc_ref[...]+=dot_tn(res_ref[...],sg)
    @pl.when(i==last)
    def _():
        spanw_ref[...]=acc_ref[...].astype(BF16)
    rg=cot_ref[...].astype(F32)+dot_nt(sg,w_ref[:,base+width:base+width+LANES])
    n2=n2_ref[...]
    def colsum(k,v):
        small_ref[k:k+1,:]+=jnp.sum(v,axis=0,keepdims=True)
    colsum(0,rg*n2); colsum(1,rg)
    ssum=norm_back(rg*vec(4),n2,r2_ref[:,:1])
    olow=ssum.astype(BF16); olow_ref[...]=olow
    colsum(2,olow.astype(F32))
    fg=ssum
    for q in range(reps):
        c=slice(q*width,(q+1)*width)
        il=(dot_nt(olow,w_ref[:,(reps+q)*width:(reps+q+1)*width])*dg_ref[:,c].astype(F32)).astype(BF16)
        ilow_ref[:,c]=il
        colsum(8+q,il.astype(F32))
        fg=fg+dot_nt(il,w_ref[:,c])
    n1=n1_ref[...]
    colsum(3,fg*n1); colsum(4,fg)
    fsum=norm_back(fg*vec(1),n1,r1_ref[:,:1])
    fsum_ref[...]=fsum
    alow=fsum.astype(BF16); alow_ref[...]=alow
    colsum(5,alow.astype(F32))
    dctx_ref[...]=dot_nt(alow,w_ref[:,base:base+width]).astype(BF16)

def feed_forward_grad(lens,own_ids,doc,scores,ids,cot,n2,r2,res,span,score,dg,n1,r1,w,vec):
    rows,width=cot.shape; ff=dg.shape[1]
    b=lambda n: pl.BlockSpec((TILE,n),lambda i:(i,0))
    s=lambda n,t: jax.ShapeDtypeStruct((rows,n),t)
    sm=pl.BlockSpec(memory_space=pltpu.SMEM)
    return pl.pallas_call(feed_forward_grad_kernel,grid=(rows//TILE,),
        in_specs=[sm,sm,once(doc.shape),once(scores.shape),once(ids.shape),b(width),b(width),b(LANES),b(width),b(LANES),b(LANES),b(ff),b(width),b(LANES),once(w.shape),once(vec.shape)],
        out_specs=[b(width),b(ff),b(width),b(width),b(width),once(vec.shape),once((width,LANES))],
        out_shape=[s(width,BF16),s(ff,BF16),s(width,BF16),s(width,F32),s(width,BF16),jax.ShapeDtypeStruct(vec.shape,F32),jax.ShapeDtypeStruct((width,LANES),BF16)],
        scratch_shapes=[pltpu.VMEM((1,LANES),F32),pltpu.VMEM((width,LANES),F32)],
        compiler_params=pltpu.CompilerParams(vmem_limit_bytes=VMEM_MOST),name='feed_forward_grad')(lens,own_ids,doc,scores,ids,cot,n2,r2,res,span,score,dg,n1,r1,w,vec)

def put_blocks(me_ref,keep_ref,give_ref,value,at):
    blocks,rows,_=keep_ref.shape
    second=me_ref[0]%2
    for t in range(blocks):
        low=value[2*t*rows:(2*t+1)*rows].astype(BF16)
        high=value[(2*t+1)*rows:(2*t+2)*rows].astype(BF16)
        @pl.when(second==0)
        def _():
            keep_ref[t,:,at]=low; give_ref[t,:,at]=high
        @pl.when(second==1)
        def _():
            keep_ref[t,:,at]=high; give_ref[t,:,at]=low

def early_kernel(reps,me_ref,low_ref,ilow_ref,act_ref,olow_ref,ctx_ref,alow_ref,keep_ref,give_ref):
    j=pl.program_id(0); last=pl.num_programs(0)-1
    put=lambda value: put_blocks(me_ref,keep_ref,give_ref,value,slice(None))
    @pl.when(j<reps)
    def _(): put(dot_tn(low_ref[...],ilow_ref[...]))
    @pl.when(jnp.logical_and(j>=reps,j<last))
    def _(): put(dot_tn(act_ref[...],olow_ref[...]))
    @pl.when(j==last)
    def _(): put(dot_tn(ctx_ref[...],alow_ref[...]))

def split_outs(dp,width,n):
    block=(dp//2,width//dp,width)
    return [pl.BlockSpec(block,lambda j:(0,0,j))]*2,[jax.ShapeDtypeStruct(block[:2]+(n*width,),BF16)]*2

def early_grads(me,low,ilow,act,olow,ctx,alow,outer_blocks,dp):
    rows,width=low.shape; reps=act.shape[1]//width
    full=once((rows,width)); n=reps+outer_blocks+1
    specs,shapes=split_outs(dp,width,n)
    return pl.pallas_call(functools.partial(early_kernel,reps),grid=(n,),
        in_specs=[pl.BlockSpec(memory_space=pltpu.SMEM),full,pl.BlockSpec((rows,width),lambda j:(0,jnp.minimum(j,reps-1))),pl.BlockSpec((rows,width),lambda j:(0,jnp.clip(j-reps,0,outer_blocks-1))),full,full,full],
        out_specs=specs,out_shape=shapes,
        compiler_params=pltpu.CompilerParams(vmem_limit_bytes=VMEM_MOST),name='early_weight_grads',
        cost_estimate=pl.CostEstimate(flops=2*rows*width*width*n,bytes_accessed=rows*width*n*4,transcendentals=0))(me,low,ilow,act,olow,ctx,alow)

def outer_kernel(me_ref,act_ref,olow_ref,keep_ref,give_ref):
    put_blocks(me_ref,keep_ref,give_ref,dot_tn(act_ref[...],olow_ref[...]),slice(None))

def outer_grads(me,act,olow,first,dp):
    rows,width=olow.shape; n=act.shape[1]//width-first
    specs,shapes=split_outs(dp,width,n)
    return pl.pallas_call(outer_kernel,grid=(n,),
        in_specs=[pl.BlockSpec(memory_space=pltpu.SMEM),pl.BlockSpec((rows,width),lambda j:(0,j+first)),once((rows,width))],
        out_specs=specs,out_shape=shapes,
        compiler_params=pltpu.CompilerParams(vmem_limit_bytes=VMEM_MOST),name='outer_weight_grad',
        cost_estimate=pl.CostEstimate(flops=2*rows*width*width*n,bytes_accessed=rows*width*n*4,transcendentals=0))(me,act,olow)

def late_kernel(me_ref,tok_ref,mg_ref,span_ref,keep_ref,give_ref,sum_ref):
    j=pl.program_id(0)
    width=tok_ref.shape[1]
    mg=mg_ref[...]
    sum_ref[...]=jnp.broadcast_to(jnp.sum(mg.astype(F32),axis=0,keepdims=True),sum_ref.shape)
    put_blocks(me_ref,keep_ref,give_ref,dot_tn(tok_ref[...],mg),pl.ds(pl.multiple_of(j*width,LANES),width))
    @pl.when(j==pl.num_programs(0)-1)
    def _():
        full=keep_ref.shape[2]
        put_blocks(me_ref,keep_ref,give_ref,span_ref[...].astype(F32),slice(full-span_ref.shape[1],full))

def late_grads(me,tok,mg,span,dp):
    rows,width=tok.shape; wide=mg.shape[1]
    out=(dp//2,width//dp,wide+span.shape[1])
    return pl.pallas_call(late_kernel,grid=(wide//width,),
        in_specs=[pl.BlockSpec(memory_space=pltpu.SMEM),once((rows,width)),pl.BlockSpec((rows,width),lambda j:(0,j)),once(span.shape)],
        out_specs=[once(out),once(out),pl.BlockSpec((8,width),lambda j:(0,j))],
        out_shape=[jax.ShapeDtypeStruct(out,BF16)]*2+[jax.ShapeDtypeStruct((8,wide),F32)],
        compiler_params=pltpu.CompilerParams(vmem_limit_bytes=VMEM_MOST),name='late_weight_grads',
        cost_estimate=pl.CostEstimate(flops=2*rows*width*wide,bytes_accessed=rows*wide*4,transcendentals=0))(me,tok,mg,span)

def input_kernel(sizes,w_ref,fs_ref,*refs):
    *mgs,out_ref=refs
    width=fs_ref.shape[1]
    total=fs_ref[...]
    start=0
    for mg_ref,n in zip(mgs,sizes):
        for k in range(3):
            total=total+dot_nt(mg_ref[:,k*n:(k+1)*n],w_ref[:,k*width+start:k*width+start+n])
        start+=n
    out_ref[...]=total

def input_grads(w,fs,mgs):
    rows,width=fs.shape
    b=lambda n: pl.BlockSpec((TILE,n),lambda i:(i,0))
    return pl.pallas_call(functools.partial(input_kernel,[m.shape[1]//3 for m in mgs]),grid=(rows//TILE,),
        in_specs=[once(w.shape),b(width)]+[b(m.shape[1]) for m in mgs],out_specs=b(width),out_shape=jax.ShapeDtypeStruct((rows,width),F32),
        compiler_params=pltpu.CompilerParams(vmem_limit_bytes=VMEM_MOST),name='input_grad',
        cost_estimate=pl.CostEstimate(flops=6*rows*width*width,bytes_accessed=rows*width*16,transcendentals=0))(w,fs,*mgs)
AXES = ("dp", "fsdp")
LATE_BLOCKS = 3


def pack_lanes(parts):
    flat = jnp.concatenate(parts, axis=-1)
    wide = -(-flat.shape[-1] // LANES) * LANES
    flat = jnp.pad(flat, [(0, 0)] * (flat.ndim - 1) + [(0, wide - flat.shape[-1])])
    return flat.reshape(flat.shape[:-1] + (wide // LANES, LANES))


def unpack_lanes(packed, sizes):
    flat = packed.reshape(packed.shape[:-2] + (-1,))
    starts = [sum(sizes[:i]) for i in range(len(sizes))]
    return [flat[..., a : a + n] for a, n in zip(starts, sizes)]


def to_all(block, devices):
    return lax.all_to_all(jnp.broadcast_to(block[None], (devices,) + block.shape), AXES, 0, 0)


def shards(
    tokens,
    cotangent,
    doc_lengths,
    query_ids,
    qkv_weight,
    query_bias,
    value_bias,
    attn_weight,
    attn_bias,
    first_gain,
    first_shift,
    inner_weight,
    inner_bias,
    outer_weight,
    outer_bias,
    second_gain,
    second_shift,
    span_weight,
    answer_vector,
):
    rows, width = tokens.shape
    packs_here = rows // PACK
    devices = lax.axis_size("dp") * lax.axis_size("fsdp")
    share = qkv_weight.shape[0]
    ff = inner_weight.shape[1]
    reps = ff // width
    segs_here = packs_here * SEGS_PACK
    span = span_weight.shape[1]

    row_params = (attn_bias, first_gain, first_shift, outer_bias, second_gain, second_shift)
    smalls = row_params + (query_bias, value_bias, inner_bias, answer_vector)
    answers = answer_vector.shape[0]
    rows_in = len(row_params) + 2 + reps
    packed = pack_lanes(smalls)
    packed = jnp.pad(packed, ((0, share - packed.shape[0]), (0, 0)))
    id_row = jnp.pad(
        query_ids[:, 0].astype(F32)[None], ((0, 0), (0, LANES - segs_here)), constant_values=-1.0
    )

    orders = bit_orders(lax.axis_size("dp"))
    fsdp = lax.axis_size("fsdp")
    me = jnp.stack([lax.axis_index("dp"), lax.axis_index("fsdp")]).astype(jnp.int32)
    mix = jnp.concatenate([qkv_weight, packed], axis=1)
    mix_near = gather_near(mix)
    near = len(mix_near)
    mix_walk = Gathering(mix_near, orders, qkv_weight.shape[1] // 2)
    mix_walk.advance(0)
    mix_walk.send()
    mix_parts = mix_walk.parts()
    inner_turned = (
        inner_weight.reshape(share, devices, reps, share).transpose(0, 2, 1, 3).reshape(share, ff)
    )
    outer_blocks = [outer_weight[q * share : (q + 1) * share] for q in range(reps)]
    rest = jnp.concatenate([inner_turned] + outer_blocks + [attn_weight, span_weight], axis=1)
    rest_full = lax.all_gather(rest, AXES, axis=0, tiled=True)

    mix_full, vectors, mixed, context, logsum = attention(
        doc_lengths, me, tokens, mix_parts, orders, near, (share, rows_in, answers)
    )
    (
        normed_one,
        factor_one,
        first_low,
        active,
        gelu_slope,
        normed_two,
        factor_two,
        result,
        span_rows,
        token_score,
        doc_score,
    ) = feed_forward(
        doc_lengths, context, tokens, rest_full, vectors, reps
    )
    exchanged = to_all(jnp.concatenate([doc_score, id_row], axis=0), devices)
    scores_all, ids_all = exchanged[:, 0], exchanged[:, 1]

    outer_low, inner_low, attended_low, first_sum_grad, context_grad, small_sums, span_grad = (
        feed_forward_grad(
            doc_lengths,
            query_ids.reshape(-1),
            doc_score,
            scores_all,
            ids_all,
            cotangent,
            normed_two,
            factor_two,
            result,
            span_rows,
            token_score,
            gelu_slope,
            normed_one,
            factor_one,
            rest_full,
            vectors,
        )
    )
    early_blocks = reps - LATE_BLOCKS
    dp = lax.axis_size("dp")
    keep, give = early_grads(
        me, first_low, inner_low, active, outer_low, context, attended_low, early_blocks, dp
    )
    came = swap(give, "dp", orders[0][0])
    outer_low, keep = tie(outer_low, keep)
    outer_walk = Reduction(*outer_grads(me, active, outer_low, early_blocks, dp), orders[1])
    came, outer_walk.keep = tie(came, outer_walk.keep)
    outer_walk.send()
    early = add_low(keep, came)
    cores = [[d for d in range(dp) if d % 2 == c] for c in range(2)]
    early_dp = lax.psum_scatter(
        early.reshape(-1, early.shape[-1]),
        "dp",
        scatter_dimension=0,
        axis_index_groups=cores,
        tiled=True,
    )
    context_grad, early = tie(context_grad, early)
    mixed_grad = attention_grad((0, HEADS // 2), doc_lengths, mixed, context, context_grad, logsum)
    mixed_grad, outer_walk.came = tie(mixed_grad, outer_walk.came)
    *late, bias_sums = late_grads(me, tokens, mixed_grad, span_grad, dp)
    late, outer_walk.came = tie(late, outer_walk.came)
    late_walk = Reduction(*late, orders[0])
    late_walk.send()
    outer_walk.add()
    outer_walk.advance(2)
    outer_walk.send()
    n_rows = small_sums.shape[0]
    by_owner = small_sums.reshape(n_rows, devices, share).transpose(1, 0, 2)
    biases = bias_sums[0].reshape(3, devices, share).transpose(1, 0, 2)
    small_grads = pack_lanes(
        [
            by_owner.reshape(devices, n_rows * share),
            biases.reshape(devices, 3 * share),
            small_sums[15, :span].reshape(devices, span // devices),
        ]
    )
    small_grads, late_walk.came, outer_walk.give = tie(
        small_grads, late_walk.came, outer_walk.give
    )
    late_walk.add()
    late_walk.advance(2)
    late_walk.send()
    small_grads, early_dp, late_walk.keep, outer_walk.keep = tie(
        small_grads, early_dp, late_walk.keep, outer_walk.keep
    )
    received = lax.all_to_all(small_grads, AXES, 0, 0)
    early_sum, early_takes = start_near([early_dp])
    scores_all, first_sum_grad, early_sum = tie(scores_all, first_sum_grad, early_sum)
    input_grad = input_grads(mix_full, first_sum_grad, [mixed_grad])
    input_grad, early_takes, late_walk.came, outer_walk.came = tie(
        input_grad, early_takes, late_walk.came, outer_walk.came
    )
    outer_walk.add()
    outer_walk.send()
    late_walk.add()
    late_walk.send()
    received, late_walk.came, outer_walk.came = tie(
        received, late_walk.came, outer_walk.came
    )
    outer_walk.add()
    late_walk.add()
    late_sum, takes = start_near([late_walk.keep, outer_walk.keep])
    received, early_takes, late_sum = tie(received, early_takes, late_sum)
    early_sum = add_near(early_sum, early_takes)
    mine = jnp.sum(received, axis=0)
    own_rows, own_biases, answer_own = unpack_lanes(
        mine, [n_rows * share, 3 * share, span // devices]
    )
    row_of = lambda k: own_rows[k * share : (k + 1) * share]
    queries = lax.broadcasted_iota(F32, (packs_here * devices, 1), 0)
    member_query = ids_all[:, :segs_here].reshape(1, -1) == queries
    marginal = jax.nn.logsumexp(
        jnp.where(member_query, scores_all[:, :segs_here].reshape(1, -1), MASKED), axis=1
    )
    inner_own = (
        early_sum[:, :ff].reshape(share, reps, devices, share).transpose(0, 2, 1, 3)
    ).reshape(share, ff)
    inner_own, takes = tie(inner_own, takes)
    late_sum = add_near(late_sum, takes)
    outer_own = jnp.concatenate(
        [early_sum[:, ff + q * width : ff + (q + 1) * width] for q in range(early_blocks)]
        + [late_sum[:, 3 * width + span + q * width :][:, :width] for q in range(LATE_BLOCKS)],
        axis=0,
    )
    return (
        jnp.sum(marginal),
        result,
        input_grad,
        late_sum[:, : 3 * width],
        own_biases[:share],
        own_biases[2 * share :],
        early_sum[:, -width:],
        row_of(5),
        row_of(3),
        row_of(4),
        inner_own,
        own_rows[8 * share : (8 + reps) * share],
        outer_own,
        row_of(2),
        row_of(0),
        row_of(1),
        late_sum[:, 3 * width : 3 * width + span],
        answer_own,
    )


def solution(mesh):
    rows = P(AXES, None)
    flat = P(AXES)
    in_specs = (rows,) * 4 + (rows, flat, flat, rows, flat, flat, flat, rows, flat, rows)
    in_specs += (flat, flat, flat, rows, flat)
    out_specs = (P(), rows, rows, rows, flat, flat, rows, flat, flat, flat, rows, flat, rows)
    out_specs += (flat, flat, flat, rows, flat)
    return jax.shard_map(shards, mesh=mesh, in_specs=in_specs, out_specs=out_specs, check_vma=False)
```

```python
import functools, math
import jax, jax.numpy as jnp
from jax import lax
from jax.experimental import pallas as pl
from jax.experimental.pallas import tpu as pltpu
from jax.sharding import PartitionSpec as P
PACK=512; SEGS_PACK=4; HEADS=12; HEAD_DIM=64; LANES=128; SUBLANES=8
MASKED=-1e30
VMEM_MOST=60*1024*1024
F32=jnp.float32; BF16=jnp.bfloat16
def swap(block, axis, mask):
    size = lax.axis_size(axis)
    return lax.ppermute(block, axis, [(i, i ^ mask) for i in range(size)])


def bit_orders(dp):
    bits = [1 << t for t in range(dp.bit_length() - 1)]
    first, others = bits[:1], bits[1:]
    return first + others, first + others[1:] + others[:1]


def offsets(order):
    found = [0]
    for bit in reversed(order):
        found = found + [f | bit for f in found]
    return found


def gather_near(shard):
    if shard.shape[0] % SUBLANES:
        return [lax.all_gather(shard, "fsdp", axis=0, tiled=True)]
    return [shard] + [swap(shard, "fsdp", k) for k in range(1, lax.axis_size("fsdp"))]


class Gathering:
    def __init__(self, pieces, orders, split):
        self.orders = orders
        self.near = len(pieces)
        self.left = len(orders[0]) - 1
        cut = [[p[:, :split] for p in pieces], [p[:, split:] for p in pieces]]
        self.blocks = [jnp.stack(c) for c in cut]
        self.came = None

    def send(self):
        self.came = [swap(b, "dp", o[self.left]) for b, o in zip(self.blocks, self.orders)]

    def join(self):
        self.blocks = [jnp.concatenate([b, c], axis=0) for b, c in zip(self.blocks, self.came)]
        self.left -= 1

    def advance(self, left):
        while self.left > left:
            self.send()
            self.join()

    def parts(self):
        return [self.blocks[0], self.came[0], self.blocks[1], self.came[1]]


def part(block, dim, which):
    return lax.dynamic_index_in_dim(block, which, dim, keepdims=False)


def add_low(a, b):
    return (a.astype(F32) + b.astype(F32)).astype(BF16)


class Reduction:
    def __init__(self, keep, give, order):
        self.order = list(order)
        self.bits = sorted(order, reverse=True)
        self.keep, self.give = keep, give
        self.came = None

    def send(self):
        self.came = swap(self.give, "dp", self.order[0])

    def add(self):
        total = add_low(self.keep, self.came)
        self.bits.remove(self.order.pop(0))
        if not self.order:
            self.keep = total
            return
        total = total.reshape((2,) * len(self.bits) + total.shape[-2:])
        dim = self.bits.index(self.order[0])
        own = (lax.axis_index("dp") // self.order[0]) % 2
        flat = lambda x: x.reshape((-1,) + x.shape[-2:])
        self.keep, self.give = flat(part(total, dim, own)), flat(part(total, dim, 1 - own))

    def advance(self, left):
        while len(self.order) > left:
            self.send()
            self.add()


def start_near(blocks):
    fsdp = lax.axis_size("fsdp")
    split = [b.reshape(fsdp, -1, b.shape[-1]) for b in blocks]
    own = lax.axis_index("fsdp")
    take = lambda k: jnp.concatenate([part(b, 0, own ^ k) for b in split], axis=1)
    return take(0), [swap(take(k), "fsdp", k) for k in range(1, fsdp)]


def add_near(own, came):
    total = own.astype(F32)
    for block in came:
        total = total + block.astype(F32)
    return total


def tie(*groups):
    return lax.optimization_barrier(groups)


def once(shape):
    return pl.BlockSpec(shape,lambda i:(0,)*len(shape),pipeline_mode=pl.Buffered(1))

def dot_nn(a,b): return jnp.dot(a,b,preferred_element_type=F32)
def dot_nt(a,b): return lax.dot_general(a,b,(((1,),(1,)),((),())),preferred_element_type=F32)
def dot_tn(a,b): return lax.dot_general(a,b,(((0,),(0,)),((),())),preferred_element_type=F32)

def segment_tiles(lens_ref, g):
    row=lax.broadcasted_iota(jnp.int32,(PACK,LANES),0)
    lane=lax.broadcasted_iota(jnp.int32,(PACK,LANES),1)
    seg=jnp.zeros((PACK,LANES),jnp.int32); bound=jnp.int32(0)
    for j in range(SEGS_PACK):
        bound=bound+lens_ref[g,j]
        seg=seg+(row>=bound).astype(jnp.int32)
    place=lane-48
    inside=jnp.logical_and(place>=0,place<SEGS_PACK)
    same=place==seg
    apart=jnp.where(jnp.logical_and(inside,jnp.logical_not(same)),MASKED,0.0)
    own=jnp.where(same,1.0,0.0)
    return lane,apart,own

def head_lanes(lane,h):
    return jnp.logical_and(lane<48,lane%16==h)

def assemble(me_ref, orders, fsdp, parts, full_ref, sems):
    copies, start = [], 0
    for color, order in enumerate(orders):
        cols = parts[2 * color].shape[2]
        for half in range(2):
            src = parts[2 * color + half]
            near = offsets(order)[half * src.shape[0] // fsdp :]
            for n in range(src.shape[0]):
                block = (near[n // fsdp] ^ me_ref[0]) * fsdp
                block += (n % fsdp) ^ me_ref[1] if fsdp > 1 else 0
                place = pl.ds(pl.multiple_of(block * src.shape[1], SUBLANES), src.shape[1])
                copies.append(
                    pltpu.make_async_copy(
                        src.at[n], full_ref.at[place, pl.ds(start, cols)], sems.at[len(copies)]
                    )
                )
        start += cols
    for copy in copies:
        copy.start()
    for copy in copies:
        copy.wait()


def whole_div(x, n):
    return jnp.floor((x.astype(F32) + 0.5) * (1.0 / n)).astype(jnp.int32)


def unpack_small(block, share, rows_in, answers):
    width = block.shape[0]
    count = -(-(rows_in * share + answers) // LANES)
    row = lax.broadcasted_iota(jnp.int32, (width, LANES), 0)
    lane = lax.broadcasted_iota(jnp.int32, (width, LANES), 1)
    turned = jnp.concatenate(
        [dot_tn(block, (row == lane * share + k).astype(BF16)) for k in range(count)], axis=0
    ).astype(BF16)
    entry = lax.broadcasted_iota(jnp.int32, (count * LANES, width), 0)
    place = lax.broadcasted_iota(jnp.int32, (count * LANES, width), 1)
    owner = whole_div(lax.broadcasted_iota(jnp.int32, (LANES, width), 1), share)
    owns = (lax.broadcasted_iota(jnp.int32, (LANES, width), 0) == owner).astype(BF16)
    spread = dot_nn(turned, owns)
    fits = entry - whole_div(entry, share) * share == place - whole_div(place, share) * share
    spread = jnp.where(fits, spread, 0.0).astype(BF16)
    vector = lax.broadcasted_iota(jnp.int32, (16, count * LANES), 0)
    source = whole_div(lax.broadcasted_iota(jnp.int32, (16, count * LANES), 1), share)
    vectors = dot_nn((vector == source).astype(BF16), spread)
    line = lax.broadcasted_iota(jnp.int32, (LANES, LANES), 1)
    owns = (lax.broadcasted_iota(jnp.int32, (LANES, LANES), 0) == whole_div(line, answers)).astype(BF16)
    spread = dot_nn(turned, owns)
    entry = lax.broadcasted_iota(jnp.int32, spread.shape, 0) - rows_in * share
    place = lax.broadcasted_iota(jnp.int32, spread.shape, 1)
    fits = entry == place - whole_div(place, answers) * answers
    return vectors, jnp.sum(jnp.where(fits, spread, 0.0), axis=0, keepdims=True)


EPS=1e-6

def normed(h):
    c=h-jnp.mean(h,axis=1,keepdims=True)
    f=lax.rsqrt(jnp.mean(c*c,axis=1,keepdims=True)+EPS)
    return c*f,f

def attention_kernel(orders,fsdp,small,lens_ref,me_ref,tok_ref,p0,p1,p2,p3,w_ref,vec_ref,mix_ref,ctx_ref,inv_ref,wts_ref,n1_ref,r1_ref,low_ref,acc_ref,sems):
    pack=pl.program_id(0)
    width=tok_ref.shape[1]; wide=3*width
    @pl.when(pack==0)
    def _():
        assemble(me_ref,orders,fsdp,(p0,p1,p2,p3),w_ref,sems)
        vectors,answer=unpack_small(w_ref[:,wide+width:],*small)
        vec_ref[...]=vectors
        vec_ref[15:16,:LANES]=answer
    query_row=vec_ref[6:7,:]; value_row=vec_ref[7:8,:]
    lane,apart,own=segment_tiles(lens_ref,pack)
    apart=apart.astype(BF16); own=own.astype(BF16)
    tok=tok_ref[...]
    mix_ref[:,:width]=((dot_nn(tok,w_ref[:,:width])+query_row).astype(BF16).astype(F32)*(1/math.sqrt(HEAD_DIM))).astype(BF16)
    mix_ref[:,width:2*width]=dot_nn(tok,w_ref[:,width:2*width]).astype(BF16)
    mix_ref[:,2*width:]=(dot_nn(tok,w_ref[:,2*width:wide])+value_row).astype(BF16)
    acc_ref[...]=jnp.zeros_like(acc_ref)
    ones=jnp.ones((PACK,LANES),BF16)
    def pair(p,carry):
        at=lambda base: pl.ds(pl.multiple_of(base+p*LANES,LANES),LANES)
        q2=mix_ref[:,at(0)]; k2=mix_ref[:,at(width)]; v2=mix_ref[:,at(2*width)]
        kx=jnp.concatenate([k2,own],axis=1)
        vx=jnp.concatenate([v2,ones],axis=1)
        outs=[]
        for half in range(2):
            qm=jnp.where(lane//HEAD_DIM==half,q2,jnp.zeros_like(q2))
            s=dot_nt(jnp.concatenate([qm,apart],axis=1),kx)
            m=jnp.max(s,axis=1,keepdims=True)
            w=jnp.exp(s-m).astype(BF16)
            wts_ref[2*p+half]=w
            o=dot_nn(w,vx)
            inv=1.0/o[:,LANES:]
            outs.append(o[:,:LANES]*inv)
            acc_ref[...]=jnp.where(head_lanes(lane,2*p+half),inv,acc_ref[...])
        ctx_ref[:,at(0)]=jnp.where(lane<HEAD_DIM,outs[0],outs[1]).astype(BF16)
        return carry
    lax.fori_loop(0,HEADS//2,pair,0)
    inv_ref[...]=acc_ref[...]
    att=dot_nn(ctx_ref[...],w_ref[:,wide:wide+width])+vec_ref[0:1,:]
    n1,f1=normed(tok.astype(F32)+att)
    n1_ref[...]=n1; r1_ref[...]=jnp.broadcast_to(f1,r1_ref.shape)
    low_ref[...]=(n1*vec_ref[1:2,:]+vec_ref[2:3,:]).astype(BF16)

def attention(lens,me,tok,parts,orders,fsdp,small):
    rows,width=tok.shape; share=parts[0].shape[1]; full=parts[0].shape[2]+parts[2].shape[2]
    hbm=pl.BlockSpec(memory_space=pl.ANY)
    sm=pl.BlockSpec(memory_space=pltpu.SMEM)
    wide=3*width
    sizes=((wide,BF16),(width,BF16),(LANES,F32))
    outs=[jax.ShapeDtypeStruct((rows,n),t) for n,t in sizes]
    heads=[jax.ShapeDtypeStruct((width,full),BF16),jax.ShapeDtypeStruct((16,width),F32)]
    fixed=[once((width,full)),once((16,width))]
    cost=pl.CostEstimate(flops=2*rows*width*wide+8*rows*PACK*width,bytes_accessed=rows*wide*4,transcendentals=HEADS*PACK*rows)
    spec=lambda n: pl.BlockSpec((PACK,n),lambda g:(g,0))
    return pl.pallas_call(functools.partial(attention_kernel,orders,fsdp,small),grid=(rows//PACK,),
        in_specs=[sm,sm,spec(width)]+[hbm]*4,out_specs=fixed+[spec(n) for n,_ in sizes]+[pl.BlockSpec((HEADS,PACK,PACK),lambda g:(g,0,0)),spec(width),spec(LANES),spec(width)],
        out_shape=heads+outs+[jax.ShapeDtypeStruct((rows//PACK*HEADS,PACK,PACK),BF16),jax.ShapeDtypeStruct((rows,width),F32),jax.ShapeDtypeStruct((rows,LANES),F32),jax.ShapeDtypeStruct((rows,width),BF16)],
        scratch_shapes=[pltpu.VMEM((PACK,LANES),F32),pltpu.SemaphoreType.DMA((4*parts[0].shape[0],))],
        compiler_params=pltpu.CompilerParams(vmem_limit_bytes=VMEM_MOST),name='attention',cost_estimate=cost)(lens,me,tok,*parts)

def split_three(x,lane):
    hi=x.astype(BF16).astype(F32)
    rest=x-hi
    mid=rest.astype(BF16).astype(F32)
    return jnp.where(lane<16,hi,jnp.where(lane<32,mid,jnp.where(lane<48,rest-mid,0.0)))

def attention_grad_kernel(mix_ref,ctx_ref,dctx_ref,inv_ref,wts_ref,out_ref,de_ref):
    p=pl.program_id(1)
    width=ctx_ref.shape[1]
    lane=lax.broadcasted_iota(jnp.int32,(PACK,LANES),1)
    @pl.when(p==0)
    def _():
        prod=dctx_ref[...].astype(F32)*ctx_ref[...].astype(F32)
        hi=prod.astype(BF16); lo=(prod-hi.astype(F32)).astype(BF16)
        wr=lax.broadcasted_iota(jnp.int32,(width,LANES),0); wl=lax.broadcasted_iota(jnp.int32,(width,LANES),1)
        pick=jnp.where(jnp.logical_and(wl<48,wl%16==wr//HEAD_DIM),1.0,0.0).astype(BF16)
        dots=(dot_nn(hi,pick)+dot_nn(lo,pick))*inv_ref[...]
        de_ref[...]=(-split_three(dots,lane)).astype(BF16)
    at=lambda base: pl.ds(pl.multiple_of(base+p*LANES,LANES),LANES)
    q2=mix_ref[:,at(0)]; k2=mix_ref[:,at(width)]; v2=mix_ref[:,at(2*width)]; d2=dctx_ref[:,at(0)].astype(F32)
    invs=[jnp.sum(jnp.where(lane==2*p+half,inv_ref[...],0.0),axis=1,keepdims=True) for half in range(2)]
    d2=(d2*jnp.where(lane<HEAD_DIM,invs[0],invs[1])).astype(BF16)
    qt=q2.T; dt=d2.T
    de=de_ref[...]
    dq=[]; dks=[]; dvs=[]
    for half in range(2):
        here=lane//HEAD_DIM==half
        dm=jnp.where(here,d2,jnp.zeros_like(d2))
        mark=jnp.where(head_lanes(lane,2*p+half),1.0,0.0).astype(BF16)
        w=wts_ref[half]
        dp=dot_nt(jnp.concatenate([dm,de],axis=1),jnp.concatenate([v2,mark],axis=1))
        ds=(w.astype(F32)*dp).astype(BF16)
        rows=slice(half*HEAD_DIM,(half+1)*HEAD_DIM)
        dq.append(dot_nn(ds,k2))
        dks.append(dot_nn(qt[rows],ds))
        dvs.append(dot_nn(dt[rows],w))
    out_ref[:,at(0)]=(jnp.where(lane<HEAD_DIM,dq[0],dq[1])*(1/math.sqrt(HEAD_DIM))).astype(BF16)
    out_ref[:,at(width)]=jnp.concatenate(dks,axis=0).T.astype(BF16)
    out_ref[:,at(2*width)]=jnp.concatenate(dvs,axis=0).T.astype(BF16)

def attention_grad(mix,ctx,dctx,inv,wts):
    rows,width=ctx.shape; wide=mix.shape[1]; pairs=HEADS//2
    b=lambda n: pl.BlockSpec((PACK,n),lambda g,p:(g,0))
    return pl.pallas_call(attention_grad_kernel,grid=(rows//PACK,pairs),
        in_specs=[b(wide),b(width),b(width),b(LANES),pl.BlockSpec((2,PACK,PACK),lambda g,p:(g*pairs+p,0,0))],
        out_specs=b(wide),out_shape=jax.ShapeDtypeStruct((rows,wide),BF16),
        scratch_shapes=[pltpu.VMEM((PACK,LANES),BF16)],
        compiler_params=pltpu.CompilerParams(vmem_limit_bytes=VMEM_MOST),name='attention_grad',
        cost_estimate=pl.CostEstimate(flops=16*rows*PACK*width,bytes_accessed=rows*wide*8,transcendentals=0))(mix,ctx,dctx,inv,wts)
TILE=256
def half_tail(a, e):
    t=1.0/(1.0+0.3275911*a)
    p=t*(0.5*0.254829592+t*(0.5*-0.284496736+t*(0.5*1.421413741+t*(0.5*-1.453152027+t*(0.5*1.061405429)))))
    return p*e

def gelu_pair(x):
    z=jnp.abs(x)*(1/math.sqrt(2))
    e=jnp.exp(-z*z)
    h=half_tail(z,e)
    phi=jnp.where(x>0,1.0-h,h)
    return x*phi, phi+x*(e*(1/math.sqrt(2*math.pi)))

def norm_back(e,n,f):
    return f*(e-jnp.mean(e,axis=1,keepdims=True)-n*jnp.mean(e*n,axis=1,keepdims=True))

def row_segments(lens_ref,first_row,rows):
    row=first_row+lax.broadcasted_iota(jnp.int32,(rows,LANES),0)
    lane=lax.broadcasted_iota(jnp.int32,(rows,LANES),1)
    packs=lens_ref.shape[0]
    seg=jnp.zeros((rows,LANES),jnp.int32)
    for g in range(packs):
        end=jnp.int32(g*PACK)
        for j in range(SEGS_PACK):
            end=end+lens_ref[g,j]
            seg=seg+(row>=end).astype(jnp.int32)
    return seg==lane

def feed_forward_kernel(lens_ref,n1_ref,low_ref,w_ref,vec_ref,act_ref,dg_ref,n2_ref,r2_ref,res_ref,span_ref,score_ref,doc_ref,all_ref):
    i=pl.program_id(0)
    rows,width=n1_ref.shape; reps=act_ref.shape[1]//width
    vec=lambda k: vec_ref[k:k+1,:]
    base=2*reps*width
    low=low_ref[...]
    out=n1_ref[...]*vec(1)+vec(2)+vec(3)
    for q in range(reps):
        c=slice(q*width,(q+1)*width)
        x=dot_nn(low,w_ref[:,c])+vec(8+q)
        a,d=gelu_pair(x)
        a=a.astype(BF16)
        act_ref[:,c]=a; dg_ref[:,c]=d.astype(BF16)
        out=out+dot_nn(a,w_ref[:,(reps+q)*width:(reps+q+1)*width])
    n2,f2=normed(out)
    n2_ref[...]=n2; r2_ref[...]=jnp.broadcast_to(f2,(rows,LANES))
    res=(n2*vec(4)+vec(5)).astype(BF16)
    res_ref[...]=res
    span=dot_nn(res,w_ref[:,base:base+LANES])
    span_ref[...]=span
    score=jnp.broadcast_to(jnp.sum(span*vec_ref[15:16,:LANES],axis=1,keepdims=True),(rows,LANES))
    score_ref[...]=score
    all_ref[pl.ds(pl.multiple_of(i*rows,rows),rows),:]=score
    @pl.when(i==pl.num_programs(0)-1)
    def _():
        member=row_segments(lens_ref,0,all_ref.shape[0])
        s=jnp.where(member,all_ref[...],MASKED)
        top=jnp.max(s,axis=0,keepdims=True)
        total=jnp.sum(jnp.where(member,jnp.exp(s-top),0.0),axis=0,keepdims=True)
        real=lax.broadcasted_iota(jnp.int32,(1,LANES),1)<lens_ref.shape[0]*SEGS_PACK
        doc_ref[...]=jnp.where(real,top+jnp.log(jnp.where(real,total,1.0)),MASKED)

def feed_forward(lens,n1,low,w,vec,reps):
    rows,width=n1.shape; ff=reps*width
    b=lambda n: pl.BlockSpec((TILE,n),lambda i:(i,0))
    s=lambda n,t: jax.ShapeDtypeStruct((rows,n),t)
    return pl.pallas_call(feed_forward_kernel,grid=(rows//TILE,),
        in_specs=[pl.BlockSpec(memory_space=pltpu.SMEM),b(width),b(width),once(w.shape),once(vec.shape)],
        out_specs=[b(ff),b(ff),b(width),b(LANES),b(width),b(LANES),b(LANES),once((1,LANES))],
        out_shape=[s(ff,BF16),s(ff,BF16),s(width,F32),s(LANES,F32),s(width,BF16),s(LANES,F32),s(LANES,F32),jax.ShapeDtypeStruct((1,LANES),F32)],
        scratch_shapes=[pltpu.VMEM((rows,LANES),F32)],
        compiler_params=pltpu.CompilerParams(vmem_limit_bytes=VMEM_MOST),name='feed_forward')(lens,n1,low,w,vec)

def feed_forward_grad_kernel(lens_ref,own_ids_ref,doc_ref,scores_ref,ids_ref,cot_ref,n2_ref,r2_ref,res_ref,span_ref,score_ref,dg_ref,n1_ref,r1_ref,w_ref,aw_ref,vec_ref,
                   olow_ref,ilow_ref,alow_ref,fsum_ref,dctx_ref,small_ref,spanw_ref,weight_ref,acc_ref):
    i=pl.program_id(0); last=pl.num_programs(0)-1
    rows,width=cot_ref.shape; reps=dg_ref.shape[1]//width
    vec=lambda k: vec_ref[k:k+1,:]
    base=2*reps*width
    @pl.when(i==0)
    def _():
        lane=lax.broadcasted_iota(jnp.int32,(1,LANES),1)
        marg=jnp.zeros((1,LANES),F32)
        for s in range(own_ids_ref.shape[0]):
            hit=ids_ref[...]==own_ids_ref[s].astype(F32)
            x=jnp.where(hit,scores_ref[...],MASKED)
            top=jnp.max(jnp.max(x,axis=1,keepdims=True),axis=0,keepdims=True)
            total=jnp.where(hit,jnp.exp(x-top),0.0)
            total=jnp.sum(jnp.sum(total,axis=1,keepdims=True),axis=0,keepdims=True)
            marg=jnp.where(lane==s,top+jnp.log(total),marg)
        weight_ref[...]=jnp.exp(doc_ref[...]-marg)
        small_ref[...]=jnp.zeros_like(small_ref)
        acc_ref[...]=jnp.zeros_like(acc_ref)
    member=row_segments(lens_ref,i*rows,rows)
    part=jnp.where(member,jnp.exp(jnp.where(member,score_ref[...]-doc_ref[...],0.0))*weight_ref[...],0.0)
    tw=jnp.sum(part,axis=1,keepdims=True)
    ans=vec_ref[15:16,:LANES]
    small_ref[15:16,:LANES]+=jnp.sum(tw*span_ref[...],axis=0,keepdims=True)
    sg=(tw*ans).astype(BF16)
    acc_ref[...]+=dot_tn(res_ref[...],sg)
    @pl.when(i==last)
    def _():
        spanw_ref[...]=acc_ref[...].astype(BF16)
    rg=cot_ref[...].astype(F32)+dot_nt(sg,w_ref[:,base:base+LANES])
    n2=n2_ref[...]
    def colsum(k,v):
        small_ref[k:k+1,:]+=jnp.sum(v,axis=0,keepdims=True)
    colsum(0,rg*n2); colsum(1,rg)
    ssum=norm_back(rg*vec(4),n2,r2_ref[:,:1])
    olow=ssum.astype(BF16); olow_ref[...]=olow
    colsum(2,olow.astype(F32))
    fg=ssum
    for q in range(reps):
        c=slice(q*width,(q+1)*width)
        il=(dot_nt(olow,w_ref[:,(reps+q)*width:(reps+q+1)*width])*dg_ref[:,c].astype(F32)).astype(BF16)
        ilow_ref[:,c]=il
        colsum(8+q,il.astype(F32))
        fg=fg+dot_nt(il,w_ref[:,c])
    n1=n1_ref[...]
    colsum(3,fg*n1); colsum(4,fg)
    fsum=norm_back(fg*vec(1),n1,r1_ref[:,:1])
    fsum_ref[...]=fsum
    alow=fsum.astype(BF16); alow_ref[...]=alow
    colsum(5,alow.astype(F32))
    dctx_ref[...]=dot_nt(alow,aw_ref[...]).astype(BF16)

def feed_forward_grad(lens,own_ids,doc,scores,ids,cot,n2,r2,res,span,score,dg,n1,r1,w,mix,vec):
    rows,width=cot.shape; ff=dg.shape[1]
    b=lambda n: pl.BlockSpec((TILE,n),lambda i:(i,0))
    s=lambda n,t: jax.ShapeDtypeStruct((rows,n),t)
    sm=pl.BlockSpec(memory_space=pltpu.SMEM)
    return pl.pallas_call(feed_forward_grad_kernel,grid=(rows//TILE,),
        in_specs=[sm,sm,once(doc.shape),once(scores.shape),once(ids.shape),b(width),b(width),b(LANES),b(width),b(LANES),b(LANES),b(ff),b(width),b(LANES),once(w.shape),pl.BlockSpec((width,width),lambda i:(0,3),pipeline_mode=pl.Buffered(1)),once(vec.shape)],
        out_specs=[b(width),b(ff),b(width),b(width),b(width),once(vec.shape),once((width,LANES))],
        out_shape=[s(width,BF16),s(ff,BF16),s(width,BF16),s(width,F32),s(width,BF16),jax.ShapeDtypeStruct(vec.shape,F32),jax.ShapeDtypeStruct((width,LANES),BF16)],
        scratch_shapes=[pltpu.VMEM((1,LANES),F32),pltpu.VMEM((width,LANES),F32)],
        compiler_params=pltpu.CompilerParams(vmem_limit_bytes=VMEM_MOST),name='feed_forward_grad')(lens,own_ids,doc,scores,ids,cot,n2,r2,res,span,score,dg,n1,r1,w,mix,vec)

def put_blocks(me_ref,keep_ref,give_ref,value,at):
    blocks,rows,_=keep_ref.shape
    second=me_ref[0]%2
    for t in range(blocks):
        low=value[2*t*rows:(2*t+1)*rows].astype(BF16)
        high=value[(2*t+1)*rows:(2*t+2)*rows].astype(BF16)
        @pl.when(second==0)
        def _():
            keep_ref[t,:,at]=low; give_ref[t,:,at]=high
        @pl.when(second==1)
        def _():
            keep_ref[t,:,at]=high; give_ref[t,:,at]=low

def early_kernel(reps,me_ref,low_ref,ilow_ref,act_ref,olow_hbm,ctx_hbm,alow_hbm,keep_ref,give_ref,olow_ref,ctx_ref,alow_ref,sems):
    j=pl.program_id(0); last=pl.num_programs(0)-1
    moves=[pltpu.make_async_copy(src,dst,sems.at[k]) for k,(src,dst) in enumerate(((olow_hbm,olow_ref),(ctx_hbm,ctx_ref),(alow_hbm,alow_ref)))]
    put=lambda value: put_blocks(me_ref,keep_ref,give_ref,value,slice(None))
    @pl.when(j==0)
    def _():
        for move in moves: move.start()
    @pl.when(j<reps)
    def _(): put(dot_tn(low_ref[...],ilow_ref[...]))
    @pl.when(j==reps)
    def _():
        for move in moves: move.wait()
    @pl.when(jnp.logical_and(j>=reps,j<last))
    def _(): put(dot_tn(act_ref[...],olow_ref[...]))
    @pl.when(j==last)
    def _(): put(dot_tn(ctx_ref[...],alow_ref[...]))

def split_outs(dp,width,n):
    block=(dp//2,width//dp,width)
    return [pl.BlockSpec(block,lambda j:(0,0,j))]*2,[jax.ShapeDtypeStruct(block[:2]+(n*width,),BF16)]*2

def early_grads(me,low,ilow,act,olow,ctx,alow,outer_blocks,dp):
    rows,width=low.shape; reps=act.shape[1]//width
    full=once((rows,width)); n=reps+outer_blocks+1
    specs,shapes=split_outs(dp,width,n)
    return pl.pallas_call(functools.partial(early_kernel,reps),grid=(n,),
        in_specs=[pl.BlockSpec(memory_space=pltpu.SMEM),full,pl.BlockSpec((rows,width),lambda j:(0,jnp.minimum(j,reps-1))),pl.BlockSpec((rows,width),lambda j:(0,jnp.clip(j-reps,0,outer_blocks-1)))]+[pl.BlockSpec(memory_space=pl.ANY)]*3,
        out_specs=specs,out_shape=shapes,scratch_shapes=[pltpu.VMEM((rows,width),BF16)]*3+[pltpu.SemaphoreType.DMA((3,))],
        compiler_params=pltpu.CompilerParams(vmem_limit_bytes=VMEM_MOST),name='early_weight_grads',
        cost_estimate=pl.CostEstimate(flops=2*rows*width*width*n,bytes_accessed=rows*width*n*4,transcendentals=0))(me,low,ilow,act,olow,ctx,alow)

def outer_kernel(me_ref,act_ref,olow_ref,keep_ref,give_ref):
    put_blocks(me_ref,keep_ref,give_ref,dot_tn(act_ref[...],olow_ref[...]),slice(None))

def outer_grads(me,act,olow,first,dp):
    rows,width=olow.shape; n=act.shape[1]//width-first
    specs,shapes=split_outs(dp,width,n)
    return pl.pallas_call(outer_kernel,grid=(n,),
        in_specs=[pl.BlockSpec(memory_space=pltpu.SMEM),pl.BlockSpec((rows,width),lambda j:(0,j+first)),once((rows,width))],
        out_specs=specs,out_shape=shapes,
        compiler_params=pltpu.CompilerParams(vmem_limit_bytes=VMEM_MOST),name='outer_weight_grad',
        cost_estimate=pl.CostEstimate(flops=2*rows*width*width*n,bytes_accessed=rows*width*n*4,transcendentals=0))(me,act,olow)

def late_kernel(me_ref,tok_ref,mg_ref,span_ref,keep_ref,give_ref,sum_ref):
    j=pl.program_id(0)
    width=tok_ref.shape[1]
    mg=mg_ref[...]
    sum_ref[...]=jnp.broadcast_to(jnp.sum(mg.astype(F32),axis=0,keepdims=True),sum_ref.shape)
    put_blocks(me_ref,keep_ref,give_ref,dot_tn(tok_ref[...],mg),pl.ds(pl.multiple_of(j*width,LANES),width))
    @pl.when(j==pl.num_programs(0)-1)
    def _():
        full=keep_ref.shape[2]
        put_blocks(me_ref,keep_ref,give_ref,span_ref[...].astype(F32),slice(full-span_ref.shape[1],full))

def late_grads(me,tok,mg,span,dp):
    rows,width=tok.shape; wide=mg.shape[1]
    out=(dp//2,width//dp,wide+span.shape[1])
    return pl.pallas_call(late_kernel,grid=(wide//width,),
        in_specs=[pl.BlockSpec(memory_space=pltpu.SMEM),once((rows,width)),pl.BlockSpec((rows,width),lambda j:(0,j)),once(span.shape)],
        out_specs=[once(out),once(out),pl.BlockSpec((8,width),lambda j:(0,j))],
        out_shape=[jax.ShapeDtypeStruct(out,BF16)]*2+[jax.ShapeDtypeStruct((8,wide),F32)],
        compiler_params=pltpu.CompilerParams(vmem_limit_bytes=VMEM_MOST),name='late_weight_grads',
        cost_estimate=pl.CostEstimate(flops=2*rows*width*wide,bytes_accessed=rows*wide*4,transcendentals=0))(me,tok,mg,span)

def input_kernel(sizes,w_ref,fs_ref,*refs):
    *mgs,out_ref=refs
    width=fs_ref.shape[1]
    total=fs_ref[...]
    start=0
    for mg_ref,n in zip(mgs,sizes):
        for k in range(3):
            total=total+dot_nt(mg_ref[:,k*n:(k+1)*n],w_ref[:,k*width+start:k*width+start+n])
        start+=n
    out_ref[...]=total

def input_grads(w,fs,mgs):
    rows,width=fs.shape
    b=lambda n: pl.BlockSpec((TILE,n),lambda i:(i,0))
    return pl.pallas_call(functools.partial(input_kernel,[m.shape[1]//3 for m in mgs]),grid=(rows//TILE,),
        in_specs=[once((width,3*width)),b(width)]+[b(m.shape[1]) for m in mgs],out_specs=b(width),out_shape=jax.ShapeDtypeStruct((rows,width),F32),
        compiler_params=pltpu.CompilerParams(vmem_limit_bytes=VMEM_MOST),name='input_grad',
        cost_estimate=pl.CostEstimate(flops=6*rows*width*width,bytes_accessed=rows*width*16,transcendentals=0))(w,fs,*mgs)
AXES = ("dp", "fsdp")
LATE_BLOCKS = 3


def pack_lanes(parts):
    flat = jnp.concatenate(parts, axis=-1)
    wide = -(-flat.shape[-1] // LANES) * LANES
    flat = jnp.pad(flat, [(0, 0)] * (flat.ndim - 1) + [(0, wide - flat.shape[-1])])
    return flat.reshape(flat.shape[:-1] + (wide // LANES, LANES))


def unpack_lanes(packed, sizes):
    flat = packed.reshape(packed.shape[:-2] + (-1,))
    starts = [sum(sizes[:i]) for i in range(len(sizes))]
    return [flat[..., a : a + n] for a, n in zip(starts, sizes)]


def to_all(block, devices):
    return lax.all_to_all(jnp.broadcast_to(block[None], (devices,) + block.shape), AXES, 0, 0)


def shards(
    tokens,
    cotangent,
    doc_lengths,
    query_ids,
    qkv_weight,
    query_bias,
    value_bias,
    attn_weight,
    attn_bias,
    first_gain,
    first_shift,
    inner_weight,
    inner_bias,
    outer_weight,
    outer_bias,
    second_gain,
    second_shift,
    span_weight,
    answer_vector,
):
    rows, width = tokens.shape
    packs_here = rows // PACK
    devices = lax.axis_size("dp") * lax.axis_size("fsdp")
    share = qkv_weight.shape[0]
    ff = inner_weight.shape[1]
    reps = ff // width
    segs_here = packs_here * SEGS_PACK
    span = span_weight.shape[1]

    row_params = (attn_bias, first_gain, first_shift, outer_bias, second_gain, second_shift)
    smalls = row_params + (query_bias, value_bias, inner_bias, answer_vector)
    answers = answer_vector.shape[0]
    rows_in = len(row_params) + 2 + reps
    packed = pack_lanes(smalls)
    packed = jnp.pad(packed, ((0, share - packed.shape[0]), (0, 0)))
    id_row = jnp.pad(
        query_ids[:, 0].astype(F32)[None], ((0, 0), (0, LANES - segs_here)), constant_values=-1.0
    )

    orders = bit_orders(lax.axis_size("dp"))
    fsdp = lax.axis_size("fsdp")
    me = jnp.stack([lax.axis_index("dp"), lax.axis_index("fsdp")]).astype(jnp.int32)
    mix = jnp.concatenate([qkv_weight, attn_weight, packed], axis=1)
    mix_near = gather_near(mix)
    near = len(mix_near)
    mix_walk = Gathering(mix_near, orders, 2 * width)
    mix_walk.advance(0)
    mix_walk.send()
    mix_parts = mix_walk.parts()
    inner_turned = (
        inner_weight.reshape(share, devices, reps, share).transpose(0, 2, 1, 3).reshape(share, ff)
    )
    outer_blocks = [outer_weight[q * share : (q + 1) * share] for q in range(reps)]
    rest = jnp.concatenate([inner_turned] + outer_blocks + [span_weight], axis=1)
    rest_full = lax.all_gather(rest, AXES, axis=0, tiled=True)

    (
        mix_full,
        vectors,
        mixed,
        context,
        inverse,
        weights,
        normed_one,
        factor_one,
        first_low,
    ) = attention(doc_lengths, me, tokens, mix_parts, orders, near, (share, rows_in, answers))
    active, gelu_slope, normed_two, factor_two, result, span_rows, token_score, doc_score = (
        feed_forward(doc_lengths, normed_one, first_low, rest_full, vectors, reps)
    )
    exchanged = to_all(jnp.concatenate([doc_score, id_row], axis=0), devices)
    scores_all, ids_all = exchanged[:, 0], exchanged[:, 1]

    outer_low, inner_low, attended_low, first_sum_grad, context_grad, small_sums, span_grad = (
        feed_forward_grad(
            doc_lengths,
            query_ids.reshape(-1),
            doc_score,
            scores_all,
            ids_all,
            cotangent,
            normed_two,
            factor_two,
            result,
            span_rows,
            token_score,
            gelu_slope,
            normed_one,
            factor_one,
            rest_full,
            mix_full,
            vectors,
        )
    )
    early_blocks = reps - LATE_BLOCKS
    dp = lax.axis_size("dp")
    keep, give = early_grads(
        me, first_low, inner_low, active, outer_low, context, attended_low, early_blocks, dp
    )
    came = swap(give, "dp", orders[0][0])
    outer_low, keep = tie(outer_low, keep)
    outer_walk = Reduction(*outer_grads(me, active, outer_low, early_blocks, dp), orders[1])
    came, outer_walk.keep = tie(came, outer_walk.keep)
    outer_walk.send()
    early = add_low(keep, came)
    cores = [[d for d in range(dp) if d % 2 == c] for c in range(2)]
    early_dp = lax.psum_scatter(
        early.reshape(-1, early.shape[-1]),
        "dp",
        scatter_dimension=0,
        axis_index_groups=cores,
        tiled=True,
    )
    context_grad, early = tie(context_grad, early)
    mixed_grad = attention_grad(mixed, context, context_grad, inverse, weights)
    mixed_grad, outer_walk.came = tie(mixed_grad, outer_walk.came)
    *late, bias_sums = late_grads(me, tokens, mixed_grad, span_grad, dp)
    late, outer_walk.came = tie(late, outer_walk.came)
    late_walk = Reduction(*late, orders[0])
    late_walk.send()
    outer_walk.add()
    outer_walk.advance(2)
    outer_walk.send()
    n_rows = small_sums.shape[0]
    by_owner = small_sums.reshape(n_rows, devices, share).transpose(1, 0, 2)
    biases = bias_sums[0].reshape(3, devices, share).transpose(1, 0, 2)
    small_grads = pack_lanes(
        [
            by_owner.reshape(devices, n_rows * share),
            biases.reshape(devices, 3 * share),
            small_sums[15, :span].reshape(devices, span // devices),
        ]
    )
    small_grads, late_walk.came, outer_walk.give = tie(
        small_grads, late_walk.came, outer_walk.give
    )
    late_walk.add()
    late_walk.advance(2)
    late_walk.send()
    small_grads, early_dp, late_walk.keep, outer_walk.keep = tie(
        small_grads, early_dp, late_walk.keep, outer_walk.keep
    )
    received = lax.all_to_all(small_grads, AXES, 0, 0)
    early_sum, early_takes = start_near([early_dp])
    scores_all, first_sum_grad, early_sum = tie(scores_all, first_sum_grad, early_sum)
    input_grad = input_grads(mix_full, first_sum_grad, [mixed_grad])
    input_grad, early_takes, late_walk.came, outer_walk.came = tie(
        input_grad, early_takes, late_walk.came, outer_walk.came
    )
    outer_walk.add()
    outer_walk.send()
    late_walk.add()
    late_walk.send()
    received, late_walk.came, outer_walk.came = tie(
        received, late_walk.came, outer_walk.came
    )
    outer_walk.add()
    late_walk.add()
    late_sum, takes = start_near([late_walk.keep, outer_walk.keep])
    received, early_takes, late_sum = tie(received, early_takes, late_sum)
    early_sum = add_near(early_sum, early_takes)
    mine = jnp.sum(received, axis=0)
    own_rows, own_biases, answer_own = unpack_lanes(
        mine, [n_rows * share, 3 * share, span // devices]
    )
    row_of = lambda k: own_rows[k * share : (k + 1) * share]
    queries = lax.broadcasted_iota(F32, (packs_here * devices, 1), 0)
    member_query = ids_all[:, :segs_here].reshape(1, -1) == queries
    marginal = jax.nn.logsumexp(
        jnp.where(member_query, scores_all[:, :segs_here].reshape(1, -1), MASKED), axis=1
    )
    inner_own = (
        early_sum[:, :ff].reshape(share, reps, devices, share).transpose(0, 2, 1, 3)
    ).reshape(share, ff)
    inner_own, takes = tie(inner_own, takes)
    late_sum = add_near(late_sum, takes)
    outer_own = jnp.concatenate(
        [early_sum[:, ff + q * width : ff + (q + 1) * width] for q in range(early_blocks)]
        + [late_sum[:, 3 * width + span + q * width :][:, :width] for q in range(LATE_BLOCKS)],
        axis=0,
    )
    return (
        jnp.sum(marginal),
        result,
        input_grad,
        late_sum[:, : 3 * width],
        own_biases[:share],
        own_biases[2 * share :],
        early_sum[:, -width:],
        row_of(5),
        row_of(3),
        row_of(4),
        inner_own,
        own_rows[8 * share : (8 + reps) * share],
        outer_own,
        row_of(2),
        row_of(0),
        row_of(1),
        late_sum[:, 3 * width : 3 * width + span],
        answer_own,
    )


def solution(mesh):
    rows = P(AXES, None)
    flat = P(AXES)
    in_specs = (rows,) * 4 + (rows, flat, flat, rows, flat, flat, flat, rows, flat, rows)
    in_specs += (flat, flat, flat, rows, flat)
    out_specs = (P(), rows, rows, rows, flat, flat, rows, flat, flat, flat, rows, flat, rows)
    out_specs += (flat, flat, flat, rows, flat)
    return jax.shard_map(shards, mesh=mesh, in_specs=in_specs, out_specs=out_specs, check_vma=False)
```

```python
import functools, math
import jax, jax.numpy as jnp
from jax import lax
from jax.experimental import pallas as pl
from jax.experimental.pallas import tpu as pltpu
from jax.sharding import PartitionSpec as P
PACK=512; SEGS_PACK=4; HEADS=12; HEAD_DIM=64; LANES=128; SUBLANES=8
MASKED=-1e30
VMEM_MOST=60*1024*1024
F32=jnp.float32; BF16=jnp.bfloat16
def swap(block, axis, mask):
    size = lax.axis_size(axis)
    return lax.ppermute(block, axis, [(i, i ^ mask) for i in range(size)])


def bit_orders(dp):
    bits = [1 << t for t in range(dp.bit_length() - 1)]
    first, others = bits[:1], bits[1:]
    return first + others, first + others[1:] + others[:1]


def offsets(order):
    found = [0]
    for bit in reversed(order):
        found = found + [f | bit for f in found]
    return found


def gather_near(shard):
    if shard.shape[0] % SUBLANES:
        return [lax.all_gather(shard, "fsdp", axis=0, tiled=True)]
    return [shard] + [swap(shard, "fsdp", k) for k in range(1, lax.axis_size("fsdp"))]


class Gathering:
    def __init__(self, pieces, orders, split):
        self.orders = orders
        self.near = len(pieces)
        self.left = len(orders[0]) - 1
        cut = [[p[:, :split] for p in pieces], [p[:, split:] for p in pieces]]
        self.blocks = [jnp.stack(c) for c in cut]
        self.came = None

    def send(self):
        self.came = [swap(b, "dp", o[self.left]) for b, o in zip(self.blocks, self.orders)]

    def join(self):
        self.blocks = [jnp.concatenate([b, c], axis=0) for b, c in zip(self.blocks, self.came)]
        self.left -= 1

    def advance(self, left):
        while self.left > left:
            self.send()
            self.join()

    def parts(self):
        return [self.blocks[0], self.came[0], self.blocks[1], self.came[1]]


def part(block, dim, which):
    return lax.dynamic_index_in_dim(block, which, dim, keepdims=False)


def add_low(a, b):
    return (a.astype(F32) + b.astype(F32)).astype(BF16)


class Reduction:
    def __init__(self, keep, give, order):
        self.order = list(order)
        self.bits = sorted(order, reverse=True)
        self.keep, self.give = keep, give
        self.came = None

    def send(self):
        self.came = swap(self.give, "dp", self.order[0])

    def add(self):
        total = add_low(self.keep, self.came)
        self.bits.remove(self.order.pop(0))
        if not self.order:
            self.keep = total
            return
        total = total.reshape((2,) * len(self.bits) + total.shape[-2:])
        dim = self.bits.index(self.order[0])
        own = (lax.axis_index("dp") // self.order[0]) % 2
        flat = lambda x: x.reshape((-1,) + x.shape[-2:])
        self.keep, self.give = flat(part(total, dim, own)), flat(part(total, dim, 1 - own))

    def advance(self, left):
        while len(self.order) > left:
            self.send()
            self.add()


def start_near(blocks):
    fsdp = lax.axis_size("fsdp")
    split = [b.reshape(fsdp, -1, b.shape[-1]) for b in blocks]
    own = lax.axis_index("fsdp")
    take = lambda k: jnp.concatenate([part(b, 0, own ^ k) for b in split], axis=1)
    return take(0), [swap(take(k), "fsdp", k) for k in range(1, fsdp)]


def add_near(own, came):
    total = own.astype(F32)
    for block in came:
        total = total + block.astype(F32)
    return total


def tie(*groups):
    return lax.optimization_barrier(groups)


def once(shape):
    return pl.BlockSpec(shape,lambda i:(0,)*len(shape),pipeline_mode=pl.Buffered(1))

def dot_nn(a,b): return jnp.dot(a,b,preferred_element_type=F32)
def dot_nt(a,b): return lax.dot_general(a,b,(((1,),(1,)),((),())),preferred_element_type=F32)
def dot_tn(a,b): return lax.dot_general(a,b,(((0,),(0,)),((),())),preferred_element_type=F32)

def segment_tiles(lens_ref, g):
    row=lax.broadcasted_iota(jnp.int32,(PACK,LANES),0)
    lane=lax.broadcasted_iota(jnp.int32,(PACK,LANES),1)
    seg=jnp.zeros((PACK,LANES),jnp.int32); bound=jnp.int32(0)
    for j in range(SEGS_PACK):
        bound=bound+lens_ref[g,j]
        seg=seg+(row>=bound).astype(jnp.int32)
    place=lane-48
    inside=jnp.logical_and(place>=0,place<SEGS_PACK)
    same=place==seg
    apart=jnp.where(jnp.logical_and(inside,jnp.logical_not(same)),MASKED,0.0)
    own=jnp.where(same,1.0,0.0)
    return lane,apart,own

def head_lanes(lane,h):
    return jnp.logical_and(lane<48,lane%16==h)

def assemble(me_ref, orders, fsdp, parts, full_ref, sems):
    copies, start = [], 0
    for color, order in enumerate(orders):
        cols = parts[2 * color].shape[2]
        for half in range(2):
            src = parts[2 * color + half]
            near = offsets(order)[half * src.shape[0] // fsdp :]
            for n in range(src.shape[0]):
                block = (near[n // fsdp] ^ me_ref[0]) * fsdp
                block += (n % fsdp) ^ me_ref[1] if fsdp > 1 else 0
                place = pl.ds(pl.multiple_of(block * src.shape[1], SUBLANES), src.shape[1])
                copies.append(
                    pltpu.make_async_copy(
                        src.at[n], full_ref.at[place, pl.ds(start, cols)], sems.at[len(copies)]
                    )
                )
        start += cols
    for copy in copies:
        copy.start()
    for copy in copies:
        copy.wait()


def whole_div(x, n):
    return jnp.floor((x.astype(F32) + 0.5) * (1.0 / n)).astype(jnp.int32)


def unpack_small(block, share, rows_in, answers):
    width = block.shape[0]
    count = -(-(rows_in * share + answers) // LANES)
    row = lax.broadcasted_iota(jnp.int32, (width, LANES), 0)
    lane = lax.broadcasted_iota(jnp.int32, (width, LANES), 1)
    turned = jnp.concatenate(
        [dot_tn(block, (row == lane * share + k).astype(BF16)) for k in range(count)], axis=0
    ).astype(BF16)
    entry = lax.broadcasted_iota(jnp.int32, (count * LANES, width), 0)
    place = lax.broadcasted_iota(jnp.int32, (count * LANES, width), 1)
    owner = whole_div(lax.broadcasted_iota(jnp.int32, (LANES, width), 1), share)
    owns = (lax.broadcasted_iota(jnp.int32, (LANES, width), 0) == owner).astype(BF16)
    spread = dot_nn(turned, owns)
    fits = entry - whole_div(entry, share) * share == place - whole_div(place, share) * share
    spread = jnp.where(fits, spread, 0.0).astype(BF16)
    vector = lax.broadcasted_iota(jnp.int32, (16, count * LANES), 0)
    source = whole_div(lax.broadcasted_iota(jnp.int32, (16, count * LANES), 1), share)
    vectors = dot_nn((vector == source).astype(BF16), spread)
    line = lax.broadcasted_iota(jnp.int32, (LANES, LANES), 1)
    owns = (lax.broadcasted_iota(jnp.int32, (LANES, LANES), 0) == whole_div(line, answers)).astype(BF16)
    spread = dot_nn(turned, owns)
    entry = lax.broadcasted_iota(jnp.int32, spread.shape, 0) - rows_in * share
    place = lax.broadcasted_iota(jnp.int32, spread.shape, 1)
    fits = entry == place - whole_div(place, answers) * answers
    return vectors, jnp.sum(jnp.where(fits, spread, 0.0), axis=0, keepdims=True)


EPS=1e-6

def normed(h):
    c=h-jnp.mean(h,axis=1,keepdims=True)
    f=lax.rsqrt(jnp.mean(c*c,axis=1,keepdims=True)+EPS)
    return c*f,f

def attention_kernel(orders,fsdp,small,lens_ref,me_ref,tok_ref,p0,p1,p2,p3,w_ref,vec_ref,mix_ref,ctx_ref,inv_ref,wts_ref,n1_ref,r1_ref,low_ref,acc_ref,sems):
    pack=pl.program_id(0)
    width=tok_ref.shape[1]; wide=3*width
    @pl.when(pack==0)
    def _():
        assemble(me_ref,orders,fsdp,(p0,p1,p2,p3),w_ref,sems)
        vectors,answer=unpack_small(w_ref[:,wide+width:],*small)
        vec_ref[...]=vectors
        vec_ref[15:16,:LANES]=answer
    query_row=vec_ref[6:7,:]; value_row=vec_ref[7:8,:]
    lane,apart,own=segment_tiles(lens_ref,pack)
    apart=apart.astype(BF16); own=own.astype(BF16)
    tok=tok_ref[...]
    mix_ref[:,:width]=((dot_nn(tok,w_ref[:,:width])+query_row).astype(BF16).astype(F32)*(1/math.sqrt(HEAD_DIM))).astype(BF16)
    mix_ref[:,width:2*width]=dot_nn(tok,w_ref[:,width:2*width]).astype(BF16)
    mix_ref[:,2*width:]=(dot_nn(tok,w_ref[:,2*width:wide])+value_row).astype(BF16)
    acc_ref[...]=jnp.zeros_like(acc_ref)
    ones=jnp.ones((PACK,LANES),BF16)
    def pair(p,carry):
        at=lambda base: pl.ds(pl.multiple_of(base+p*LANES,LANES),LANES)
        q2=mix_ref[:,at(0)]; k2=mix_ref[:,at(width)]; v2=mix_ref[:,at(2*width)]
        kx=jnp.concatenate([k2,own],axis=1)
        vx=jnp.concatenate([v2,ones],axis=1)
        outs=[]
        for half in range(2):
            qm=jnp.where(lane//HEAD_DIM==half,q2,jnp.zeros_like(q2))
            s=dot_nt(jnp.concatenate([qm,apart],axis=1),kx)
            m=jnp.max(s,axis=1,keepdims=True)
            w=jnp.exp(s-m).astype(BF16)
            wts_ref[2*p+half]=w
            o=dot_nn(w,vx)
            inv=1.0/o[:,LANES:]
            outs.append(o[:,:LANES]*inv)
            acc_ref[...]=jnp.where(head_lanes(lane,2*p+half),inv,acc_ref[...])
        ctx_ref[:,at(0)]=jnp.where(lane<HEAD_DIM,outs[0],outs[1]).astype(BF16)
        return carry
    lax.fori_loop(0,HEADS//2,pair,0)
    inv_ref[...]=acc_ref[...]
    att=dot_nn(ctx_ref[...],w_ref[:,wide:wide+width])+vec_ref[0:1,:]
    n1,f1=normed(tok.astype(F32)+att)
    n1_ref[...]=n1; r1_ref[...]=jnp.broadcast_to(f1,r1_ref.shape)
    low_ref[...]=(n1*vec_ref[1:2,:]+vec_ref[2:3,:]).astype(BF16)

def attention(lens,me,tok,parts,orders,fsdp,small):
    rows,width=tok.shape; share=parts[0].shape[1]; full=parts[0].shape[2]+parts[2].shape[2]
    hbm=pl.BlockSpec(memory_space=pl.ANY)
    sm=pl.BlockSpec(memory_space=pltpu.SMEM)
    wide=3*width
    sizes=((wide,BF16),(width,BF16),(LANES,F32))
    outs=[jax.ShapeDtypeStruct((rows,n),t) for n,t in sizes]
    heads=[jax.ShapeDtypeStruct((width,full),BF16),jax.ShapeDtypeStruct((16,width),F32)]
    fixed=[once((width,full)),once((16,width))]
    cost=pl.CostEstimate(flops=2*rows*width*wide+8*rows*PACK*width,bytes_accessed=rows*wide*4,transcendentals=HEADS*PACK*rows)
    spec=lambda n: pl.BlockSpec((PACK,n),lambda g:(g,0))
    return pl.pallas_call(functools.partial(attention_kernel,orders,fsdp,small),grid=(rows//PACK,),
        in_specs=[sm,sm,spec(width)]+[hbm]*4,out_specs=fixed+[spec(n) for n,_ in sizes]+[pl.BlockSpec((HEADS,PACK,PACK),lambda g:(g,0,0)),spec(width),spec(LANES),spec(width)],
        out_shape=heads+outs+[jax.ShapeDtypeStruct((rows//PACK*HEADS,PACK,PACK),BF16),jax.ShapeDtypeStruct((rows,width),F32),jax.ShapeDtypeStruct((rows,LANES),F32),jax.ShapeDtypeStruct((rows,width),BF16)],
        scratch_shapes=[pltpu.VMEM((PACK,LANES),F32),pltpu.SemaphoreType.DMA((4*parts[0].shape[0],))],
        compiler_params=pltpu.CompilerParams(vmem_limit_bytes=VMEM_MOST),name='attention',cost_estimate=cost)(lens,me,tok,*parts)

def split_three(x,lane):
    hi=x.astype(BF16).astype(F32)
    rest=x-hi
    mid=rest.astype(BF16).astype(F32)
    return jnp.where(lane<16,hi,jnp.where(lane<32,mid,jnp.where(lane<48,rest-mid,0.0)))

def attention_grad_kernel(mix_ref,ctx_ref,dctx_ref,inv_ref,wts_ref,out_ref,de_ref):
    p=pl.program_id(1)
    width=ctx_ref.shape[1]
    lane=lax.broadcasted_iota(jnp.int32,(PACK,LANES),1)
    @pl.when(p==0)
    def _():
        prod=dctx_ref[...].astype(F32)*ctx_ref[...].astype(F32)
        hi=prod.astype(BF16); lo=(prod-hi.astype(F32)).astype(BF16)
        wr=lax.broadcasted_iota(jnp.int32,(width,LANES),0); wl=lax.broadcasted_iota(jnp.int32,(width,LANES),1)
        pick=jnp.where(jnp.logical_and(wl<48,wl%16==wr//HEAD_DIM),1.0,0.0).astype(BF16)
        dots=(dot_nn(hi,pick)+dot_nn(lo,pick))*inv_ref[...]
        de_ref[...]=(-split_three(dots,lane)).astype(BF16)
    at=lambda base: pl.ds(pl.multiple_of(base+p*LANES,LANES),LANES)
    q2=mix_ref[:,at(0)]; k2=mix_ref[:,at(width)]; v2=mix_ref[:,at(2*width)]; d2=dctx_ref[:,at(0)].astype(F32)
    invs=[jnp.sum(jnp.where(lane==2*p+half,inv_ref[...],0.0),axis=1,keepdims=True) for half in range(2)]
    d2=(d2*jnp.where(lane<HEAD_DIM,invs[0],invs[1])).astype(BF16)
    qt=q2.T; dt=d2.T
    de=de_ref[...]
    dq=[]; dks=[]; dvs=[]
    for half in range(2):
        here=lane//HEAD_DIM==half
        dm=jnp.where(here,d2,jnp.zeros_like(d2))
        mark=jnp.where(head_lanes(lane,2*p+half),1.0,0.0).astype(BF16)
        w=wts_ref[half]
        dp=dot_nt(jnp.concatenate([dm,de],axis=1),jnp.concatenate([v2,mark],axis=1))
        ds=(w.astype(F32)*dp).astype(BF16)
        rows=slice(half*HEAD_DIM,(half+1)*HEAD_DIM)
        dq.append(dot_nn(ds,k2))
        dks.append(dot_nn(qt[rows],ds))
        dvs.append(dot_nn(dt[rows],w))
    out_ref[:,at(0)]=(jnp.where(lane<HEAD_DIM,dq[0],dq[1])*(1/math.sqrt(HEAD_DIM))).astype(BF16)
    out_ref[:,at(width)]=jnp.concatenate(dks,axis=0).T.astype(BF16)
    out_ref[:,at(2*width)]=jnp.concatenate(dvs,axis=0).T.astype(BF16)

def attention_grad(mix,ctx,dctx,inv,wts):
    rows,width=ctx.shape; wide=mix.shape[1]; pairs=HEADS//2
    b=lambda n: pl.BlockSpec((PACK,n),lambda g,p:(g,0))
    return pl.pallas_call(attention_grad_kernel,grid=(rows//PACK,pairs),
        in_specs=[b(wide),b(width),b(width),b(LANES),pl.BlockSpec((2,PACK,PACK),lambda g,p:(g*pairs+p,0,0))],
        out_specs=b(wide),out_shape=jax.ShapeDtypeStruct((rows,wide),BF16),
        scratch_shapes=[pltpu.VMEM((PACK,LANES),BF16)],
        compiler_params=pltpu.CompilerParams(vmem_limit_bytes=VMEM_MOST),name='attention_grad',
        cost_estimate=pl.CostEstimate(flops=16*rows*PACK*width,bytes_accessed=rows*wide*8,transcendentals=0))(mix,ctx,dctx,inv,wts)
TILE=256
def half_tail(a, e):
    t=1.0/(1.0+0.3275911*a)
    p=t*(0.5*0.254829592+t*(0.5*-0.284496736+t*(0.5*1.421413741+t*(0.5*-1.453152027+t*(0.5*1.061405429)))))
    return p*e

def gelu_pair(x):
    z=jnp.abs(x)*(1/math.sqrt(2))
    e=jnp.exp(-z*z)
    h=half_tail(z,e)
    phi=jnp.where(x>0,1.0-h,h)
    return x*phi, phi+x*(e*(1/math.sqrt(2*math.pi)))

def norm_back(e,n,f):
    return f*(e-jnp.mean(e,axis=1,keepdims=True)-n*jnp.mean(e*n,axis=1,keepdims=True))

def row_segments(lens_ref,first_row,rows):
    row=first_row+lax.broadcasted_iota(jnp.int32,(rows,LANES),0)
    lane=lax.broadcasted_iota(jnp.int32,(rows,LANES),1)
    packs=lens_ref.shape[0]
    seg=jnp.zeros((rows,LANES),jnp.int32)
    for g in range(packs):
        end=jnp.int32(g*PACK)
        for j in range(SEGS_PACK):
            end=end+lens_ref[g,j]
            seg=seg+(row>=end).astype(jnp.int32)
    return seg==lane

def feed_forward_kernel(lens_ref,n1_ref,low_ref,w_ref,vec_ref,act_ref,dg_ref,n2_ref,r2_ref,res_ref,span_ref,score_ref,doc_ref,all_ref):
    i=pl.program_id(0)
    rows,width=n1_ref.shape; reps=act_ref.shape[1]//width
    vec=lambda k: vec_ref[k:k+1,:]
    base=2*reps*width
    low=low_ref[...]
    out=n1_ref[...]*vec(1)+vec(2)+vec(3)
    for q in range(reps):
        c=slice(q*width,(q+1)*width)
        x=dot_nn(low,w_ref[:,c])+vec(8+q)
        a,d=gelu_pair(x)
        a=a.astype(BF16)
        act_ref[:,c]=a; dg_ref[:,c]=d.astype(BF16)
        out=out+dot_nn(a,w_ref[:,(reps+q)*width:(reps+q+1)*width])
    n2,f2=normed(out)
    n2_ref[...]=n2; r2_ref[...]=jnp.broadcast_to(f2,(rows,LANES))
    res=(n2*vec(4)+vec(5)).astype(BF16)
    res_ref[...]=res
    span=dot_nn(res,w_ref[:,base:base+LANES])
    span_ref[...]=span
    score=jnp.broadcast_to(jnp.sum(span*vec_ref[15:16,:LANES],axis=1,keepdims=True),(rows,LANES))
    score_ref[...]=score
    all_ref[pl.ds(pl.multiple_of(i*rows,rows),rows),:]=score
    @pl.when(i==pl.num_programs(0)-1)
    def _():
        member=row_segments(lens_ref,0,all_ref.shape[0])
        s=jnp.where(member,all_ref[...],MASKED)
        top=jnp.max(s,axis=0,keepdims=True)
        total=jnp.sum(jnp.where(member,jnp.exp(s-top),0.0),axis=0,keepdims=True)
        real=lax.broadcasted_iota(jnp.int32,(1,LANES),1)<lens_ref.shape[0]*SEGS_PACK
        doc_ref[...]=jnp.where(real,top+jnp.log(jnp.where(real,total,1.0)),MASKED)

def feed_forward(lens,n1,low,w,vec,reps):
    rows,width=n1.shape; ff=reps*width
    b=lambda n: pl.BlockSpec((TILE,n),lambda i:(i,0))
    s=lambda n,t: jax.ShapeDtypeStruct((rows,n),t)
    return pl.pallas_call(feed_forward_kernel,grid=(rows//TILE,),
        in_specs=[pl.BlockSpec(memory_space=pltpu.SMEM),b(width),b(width),once(w.shape),once(vec.shape)],
        out_specs=[b(ff),b(ff),b(width),b(LANES),b(width),b(LANES),b(LANES),once((1,LANES))],
        out_shape=[s(ff,BF16),s(ff,BF16),s(width,F32),s(LANES,F32),s(width,BF16),s(LANES,F32),s(LANES,F32),jax.ShapeDtypeStruct((1,LANES),F32)],
        scratch_shapes=[pltpu.VMEM((rows,LANES),F32)],
        compiler_params=pltpu.CompilerParams(vmem_limit_bytes=VMEM_MOST),name='feed_forward')(lens,n1,low,w,vec)

def feed_forward_grad_kernel(lens_ref,own_ids_ref,doc_ref,scores_ref,ids_ref,cot_ref,n2_ref,r2_ref,res_ref,span_ref,score_ref,dg_ref,n1_ref,r1_ref,w_ref,aw_ref,vec_ref,
                   low_ref,fsum_ref,dctx_ref,small_ref,spanw_ref,weight_ref,acc_ref):
    i=pl.program_id(0); last=pl.num_programs(0)-1
    rows,width=cot_ref.shape; reps=dg_ref.shape[1]//width
    vec=lambda k: vec_ref[k:k+1,:]
    base=2*reps*width
    @pl.when(i==0)
    def _():
        lane=lax.broadcasted_iota(jnp.int32,(1,LANES),1)
        marg=jnp.zeros((1,LANES),F32)
        for s in range(own_ids_ref.shape[0]):
            hit=ids_ref[...]==own_ids_ref[s].astype(F32)
            x=jnp.where(hit,scores_ref[...],MASKED)
            top=jnp.max(jnp.max(x,axis=1,keepdims=True),axis=0,keepdims=True)
            total=jnp.where(hit,jnp.exp(x-top),0.0)
            total=jnp.sum(jnp.sum(total,axis=1,keepdims=True),axis=0,keepdims=True)
            marg=jnp.where(lane==s,top+jnp.log(total),marg)
        weight_ref[...]=jnp.exp(doc_ref[...]-marg)
        small_ref[...]=jnp.zeros_like(small_ref)
        acc_ref[...]=jnp.zeros_like(acc_ref)
    member=row_segments(lens_ref,i*rows,rows)
    part=jnp.where(member,jnp.exp(jnp.where(member,score_ref[...]-doc_ref[...],0.0))*weight_ref[...],0.0)
    tw=jnp.sum(part,axis=1,keepdims=True)
    ans=vec_ref[15:16,:LANES]
    small_ref[15:16,:LANES]+=jnp.sum(tw*span_ref[...],axis=0,keepdims=True)
    sg=(tw*ans).astype(BF16)
    acc_ref[...]+=dot_tn(res_ref[...],sg)
    @pl.when(i==last)
    def _():
        spanw_ref[...]=acc_ref[...].astype(BF16)
    rg=cot_ref[...].astype(F32)+dot_nt(sg,w_ref[:,base:base+LANES])
    n2=n2_ref[...]
    def colsum(k,v):
        small_ref[k:k+1,:]+=jnp.sum(v,axis=0,keepdims=True)
    colsum(0,rg*n2); colsum(1,rg)
    ssum=norm_back(rg*vec(4),n2,r2_ref[:,:1])
    olow=ssum.astype(BF16); low_ref[:,reps*width:(reps+1)*width]=olow
    colsum(2,olow.astype(F32))
    fg=ssum
    for q in range(reps):
        c=slice(q*width,(q+1)*width)
        il=(dot_nt(olow,w_ref[:,(reps+q)*width:(reps+q+1)*width])*dg_ref[:,c].astype(F32)).astype(BF16)
        low_ref[:,c]=il
        colsum(8+q,il.astype(F32))
        fg=fg+dot_nt(il,w_ref[:,c])
    n1=n1_ref[...]
    colsum(3,fg*n1); colsum(4,fg)
    fsum=norm_back(fg*vec(1),n1,r1_ref[:,:1])
    fsum_ref[...]=fsum
    alow=fsum.astype(BF16); low_ref[:,(reps+1)*width:]=alow
    colsum(5,alow.astype(F32))
    dctx_ref[...]=dot_nt(alow,aw_ref[...]).astype(BF16)

def feed_forward_grad(lens,own_ids,doc,scores,ids,cot,n2,r2,res,span,score,dg,n1,r1,w,mix,vec):
    rows,width=cot.shape; ff=dg.shape[1]
    b=lambda n: pl.BlockSpec((TILE,n),lambda i:(i,0))
    s=lambda n,t: jax.ShapeDtypeStruct((rows,n),t)
    sm=pl.BlockSpec(memory_space=pltpu.SMEM)
    return pl.pallas_call(feed_forward_grad_kernel,grid=(rows//TILE,),
        in_specs=[sm,sm,once(doc.shape),once(scores.shape),once(ids.shape),b(width),b(width),b(LANES),b(width),b(LANES),b(LANES),b(ff),b(width),b(LANES),once(w.shape),pl.BlockSpec((width,width),lambda i:(0,3),pipeline_mode=pl.Buffered(1)),once(vec.shape)],
        out_specs=[b(ff+2*width),b(width),b(width),once(vec.shape),once((width,LANES))],
        out_shape=[s(ff+2*width,BF16),s(width,F32),s(width,BF16),jax.ShapeDtypeStruct(vec.shape,F32),jax.ShapeDtypeStruct((width,LANES),BF16)],
        scratch_shapes=[pltpu.VMEM((1,LANES),F32),pltpu.VMEM((width,LANES),F32)],
        compiler_params=pltpu.CompilerParams(vmem_limit_bytes=VMEM_MOST),name='feed_forward_grad')(lens,own_ids,doc,scores,ids,cot,n2,r2,res,span,score,dg,n1,r1,w,mix,vec)

def put_blocks(me_ref,keep_ref,give_ref,value,at):
    blocks,rows,_=keep_ref.shape
    second=me_ref[0]%2
    for t in range(blocks):
        low=value[2*t*rows:(2*t+1)*rows].astype(BF16)
        high=value[(2*t+1)*rows:(2*t+2)*rows].astype(BF16)
        @pl.when(second==0)
        def _():
            keep_ref[t,:,at]=low; give_ref[t,:,at]=high
        @pl.when(second==1)
        def _():
            keep_ref[t,:,at]=high; give_ref[t,:,at]=low

def early_kernel(reps,me_ref,low_hbm,act_hbm,ctx_hbm,right_ref,keep_ref,give_ref,left_ref,sems):
    j=pl.program_id(0); slots,_,width=left_ref.shape
    sources=[low_hbm]+[act_hbm.at[:,pl.ds(k*width,width)] for k in range(slots-2)]+[ctx_hbm]
    moves=[pltpu.make_async_copy(src,left_ref.at[k],sems.at[k]) for k,src in enumerate(sources)]
    @pl.when(j==0)
    def _():
        for move in moves: move.start()
    for k,move in enumerate(moves):
        @pl.when(j==(0 if k==0 else reps+k-1))
        def _(): move.wait()
    put_blocks(me_ref,keep_ref,give_ref,dot_tn(left_ref[jnp.maximum(j-reps+1,0)],right_ref[...]),slice(None))

def split_outs(dp,width,n):
    block=(dp//2,width//dp,width)
    return [pl.BlockSpec(block,lambda j:(0,0,j))]*2,[jax.ShapeDtypeStruct(block[:2]+(n*width,),BF16)]*2

def early_grads(me,low,act,ctx,right,outer_blocks,dp):
    rows,width=low.shape; reps=act.shape[1]//width
    n=reps+outer_blocks+1
    specs,shapes=split_outs(dp,width,n)
    hbm=pl.BlockSpec(memory_space=pl.ANY)
    column=lambda j: jnp.where(j<reps,j,jnp.where(j<n-1,reps,reps+1))
    return pl.pallas_call(functools.partial(early_kernel,reps),grid=(n,),
        in_specs=[pl.BlockSpec(memory_space=pltpu.SMEM),hbm,hbm,hbm,pl.BlockSpec((rows,width),lambda j:(0,column(j)))],
        out_specs=specs,out_shape=shapes,scratch_shapes=[pltpu.VMEM((outer_blocks+2,rows,width),BF16),pltpu.SemaphoreType.DMA((outer_blocks+2,))],
        compiler_params=pltpu.CompilerParams(vmem_limit_bytes=VMEM_MOST),name='early_weight_grads',
        cost_estimate=pl.CostEstimate(flops=2*rows*width*width*n,bytes_accessed=rows*width*n*4,transcendentals=0))(me,low,act,ctx,right)

def outer_kernel(me_ref,act_ref,olow_ref,keep_ref,give_ref):
    put_blocks(me_ref,keep_ref,give_ref,dot_tn(act_ref[...],olow_ref[...]),slice(None))

def outer_grads(me,act,right,first,dp):
    rows,ff=act.shape; width=right.shape[1]-ff>>1; n=ff//width-first
    specs,shapes=split_outs(dp,width,n)
    return pl.pallas_call(outer_kernel,grid=(n,),
        in_specs=[pl.BlockSpec(memory_space=pltpu.SMEM),pl.BlockSpec((rows,width),lambda j:(0,j+first)),pl.BlockSpec((rows,width),lambda j:(0,ff//width),pipeline_mode=pl.Buffered(1))],
        out_specs=specs,out_shape=shapes,
        compiler_params=pltpu.CompilerParams(vmem_limit_bytes=VMEM_MOST),name='outer_weight_grad',
        cost_estimate=pl.CostEstimate(flops=2*rows*width*width*n,bytes_accessed=rows*width*n*4,transcendentals=0))(me,act,right)

def late_kernel(me_ref,tok_ref,mg_ref,span_ref,keep_ref,give_ref,sum_ref):
    j=pl.program_id(0)
    width=tok_ref.shape[1]
    mg=mg_ref[...]
    sum_ref[...]=jnp.broadcast_to(jnp.sum(mg.astype(F32),axis=0,keepdims=True),sum_ref.shape)
    put_blocks(me_ref,keep_ref,give_ref,dot_tn(tok_ref[...],mg),pl.ds(pl.multiple_of(j*width,LANES),width))
    @pl.when(j==pl.num_programs(0)-1)
    def _():
        full=keep_ref.shape[2]
        put_blocks(me_ref,keep_ref,give_ref,span_ref[...].astype(F32),slice(full-span_ref.shape[1],full))

def late_grads(me,tok,mg,span,dp):
    rows,width=tok.shape; wide=mg.shape[1]
    out=(dp//2,width//dp,wide+span.shape[1])
    return pl.pallas_call(late_kernel,grid=(wide//width,),
        in_specs=[pl.BlockSpec(memory_space=pltpu.SMEM),once((rows,width)),pl.BlockSpec((rows,width),lambda j:(0,j)),once(span.shape)],
        out_specs=[once(out),once(out),pl.BlockSpec((8,width),lambda j:(0,j))],
        out_shape=[jax.ShapeDtypeStruct(out,BF16)]*2+[jax.ShapeDtypeStruct((8,wide),F32)],
        compiler_params=pltpu.CompilerParams(vmem_limit_bytes=VMEM_MOST),name='late_weight_grads',
        cost_estimate=pl.CostEstimate(flops=2*rows*width*wide,bytes_accessed=rows*wide*4,transcendentals=0))(me,tok,mg,span)

def input_kernel(sizes,w_ref,fs_ref,*refs):
    *mgs,out_ref=refs
    width=fs_ref.shape[1]
    total=fs_ref[...]
    start=0
    for mg_ref,n in zip(mgs,sizes):
        for k in range(3):
            total=total+dot_nt(mg_ref[:,k*n:(k+1)*n],w_ref[:,k*width+start:k*width+start+n])
        start+=n
    out_ref[...]=total

def input_grads(w,fs,mgs):
    rows,width=fs.shape
    b=lambda n: pl.BlockSpec((TILE,n),lambda i:(i,0))
    return pl.pallas_call(functools.partial(input_kernel,[m.shape[1]//3 for m in mgs]),grid=(rows//TILE,),
        in_specs=[once((width,3*width)),b(width)]+[b(m.shape[1]) for m in mgs],out_specs=b(width),out_shape=jax.ShapeDtypeStruct((rows,width),F32),
        compiler_params=pltpu.CompilerParams(vmem_limit_bytes=VMEM_MOST),name='input_grad',
        cost_estimate=pl.CostEstimate(flops=6*rows*width*width,bytes_accessed=rows*width*16,transcendentals=0))(w,fs,*mgs)
AXES = ("dp", "fsdp")
LATE_BLOCKS = 3


def pack_lanes(parts):
    flat = jnp.concatenate(parts, axis=-1)
    wide = -(-flat.shape[-1] // LANES) * LANES
    flat = jnp.pad(flat, [(0, 0)] * (flat.ndim - 1) + [(0, wide - flat.shape[-1])])
    return flat.reshape(flat.shape[:-1] + (wide // LANES, LANES))


def unpack_lanes(packed, sizes):
    flat = packed.reshape(packed.shape[:-2] + (-1,))
    starts = [sum(sizes[:i]) for i in range(len(sizes))]
    return [flat[..., a : a + n] for a, n in zip(starts, sizes)]


def to_all(block, devices):
    return lax.all_to_all(jnp.broadcast_to(block[None], (devices,) + block.shape), AXES, 0, 0)


def shards(
    tokens,
    cotangent,
    doc_lengths,
    query_ids,
    qkv_weight,
    query_bias,
    value_bias,
    attn_weight,
    attn_bias,
    first_gain,
    first_shift,
    inner_weight,
    inner_bias,
    outer_weight,
    outer_bias,
    second_gain,
    second_shift,
    span_weight,
    answer_vector,
):
    rows, width = tokens.shape
    packs_here = rows // PACK
    devices = lax.axis_size("dp") * lax.axis_size("fsdp")
    share = qkv_weight.shape[0]
    ff = inner_weight.shape[1]
    reps = ff // width
    segs_here = packs_here * SEGS_PACK
    span = span_weight.shape[1]

    row_params = (attn_bias, first_gain, first_shift, outer_bias, second_gain, second_shift)
    smalls = row_params + (query_bias, value_bias, inner_bias, answer_vector)
    answers = answer_vector.shape[0]
    rows_in = len(row_params) + 2 + reps
    packed = pack_lanes(smalls)
    packed = jnp.pad(packed, ((0, share - packed.shape[0]), (0, 0)))
    id_row = jnp.pad(
        query_ids[:, 0].astype(F32)[None], ((0, 0), (0, LANES - segs_here)), constant_values=-1.0
    )

    orders = bit_orders(lax.axis_size("dp"))
    fsdp = lax.axis_size("fsdp")
    me = jnp.stack([lax.axis_index("dp"), lax.axis_index("fsdp")]).astype(jnp.int32)
    mix = jnp.concatenate([qkv_weight, attn_weight, packed], axis=1)
    mix_near = gather_near(mix)
    near = len(mix_near)
    mix_walk = Gathering(mix_near, orders, 2 * width)
    mix_walk.advance(0)
    mix_walk.send()
    mix_parts = mix_walk.parts()
    inner_turned = (
        inner_weight.reshape(share, devices, reps, share).transpose(0, 2, 1, 3).reshape(share, ff)
    )
    outer_blocks = [outer_weight[q * share : (q + 1) * share] for q in range(reps)]
    rest = jnp.concatenate([inner_turned] + outer_blocks + [span_weight], axis=1)
    rest_full = lax.all_gather(rest, AXES, axis=0, tiled=True)

    (
        mix_full,
        vectors,
        mixed,
        context,
        inverse,
        weights,
        normed_one,
        factor_one,
        first_low,
    ) = attention(doc_lengths, me, tokens, mix_parts, orders, near, (share, rows_in, answers))
    active, gelu_slope, normed_two, factor_two, result, span_rows, token_score, doc_score = (
        feed_forward(doc_lengths, normed_one, first_low, rest_full, vectors, reps)
    )
    exchanged = to_all(jnp.concatenate([doc_score, id_row], axis=0), devices)
    scores_all, ids_all = exchanged[:, 0], exchanged[:, 1]

    lows, first_sum_grad, context_grad, small_sums, span_grad = (
        feed_forward_grad(
            doc_lengths,
            query_ids.reshape(-1),
            doc_score,
            scores_all,
            ids_all,
            cotangent,
            normed_two,
            factor_two,
            result,
            span_rows,
            token_score,
            gelu_slope,
            normed_one,
            factor_one,
            rest_full,
            mix_full,
            vectors,
        )
    )
    early_blocks = reps - LATE_BLOCKS
    dp = lax.axis_size("dp")
    keep, give = early_grads(me, first_low, active, context, lows, early_blocks, dp)
    came = swap(give, "dp", orders[0][0])
    lows, keep = tie(lows, keep)
    outer_walk = Reduction(*outer_grads(me, active, lows, early_blocks, dp), orders[1])
    came, outer_walk.keep = tie(came, outer_walk.keep)
    outer_walk.send()
    early = add_low(keep, came)
    cores = [[d for d in range(dp) if d % 2 == c] for c in range(2)]
    early_dp = lax.psum_scatter(
        early.reshape(-1, early.shape[-1]),
        "dp",
        scatter_dimension=0,
        axis_index_groups=cores,
        tiled=True,
    )
    context_grad, early = tie(context_grad, early)
    mixed_grad = attention_grad(mixed, context, context_grad, inverse, weights)
    mixed_grad, outer_walk.came = tie(mixed_grad, outer_walk.came)
    *late, bias_sums = late_grads(me, tokens, mixed_grad, span_grad, dp)
    late, outer_walk.came = tie(late, outer_walk.came)
    late_walk = Reduction(*late, orders[0])
    late_walk.send()
    outer_walk.add()
    outer_walk.advance(2)
    outer_walk.send()
    n_rows = small_sums.shape[0]
    by_owner = small_sums.reshape(n_rows, devices, share).transpose(1, 0, 2)
    biases = bias_sums[0].reshape(3, devices, share).transpose(1, 0, 2)
    small_grads = pack_lanes(
        [
            by_owner.reshape(devices, n_rows * share),
            biases.reshape(devices, 3 * share),
            small_sums[15, :span].reshape(devices, span // devices),
        ]
    )
    small_grads, late_walk.came, outer_walk.give = tie(
        small_grads, late_walk.came, outer_walk.give
    )
    late_walk.add()
    late_walk.advance(2)
    late_walk.send()
    small_grads, early_dp, late_walk.keep, outer_walk.keep = tie(
        small_grads, early_dp, late_walk.keep, outer_walk.keep
    )
    received = lax.all_to_all(small_grads, AXES, 0, 0)
    early_sum, early_takes = start_near([early_dp])
    scores_all, first_sum_grad, early_sum = tie(scores_all, first_sum_grad, early_sum)
    input_grad = input_grads(mix_full, first_sum_grad, [mixed_grad])
    input_grad, early_takes, late_walk.came, outer_walk.came = tie(
        input_grad, early_takes, late_walk.came, outer_walk.came
    )
    outer_walk.add()
    outer_walk.send()
    late_walk.add()
    late_walk.send()
    received, late_walk.came, outer_walk.came = tie(
        received, late_walk.came, outer_walk.came
    )
    outer_walk.add()
    late_walk.add()
    late_sum, takes = start_near([late_walk.keep, outer_walk.keep])
    received, early_takes, late_sum = tie(received, early_takes, late_sum)
    early_sum = add_near(early_sum, early_takes)
    mine = jnp.sum(received, axis=0)
    own_rows, own_biases, answer_own = unpack_lanes(
        mine, [n_rows * share, 3 * share, span // devices]
    )
    row_of = lambda k: own_rows[k * share : (k + 1) * share]
    queries = lax.broadcasted_iota(F32, (packs_here * devices, 1), 0)
    member_query = ids_all[:, :segs_here].reshape(1, -1) == queries
    marginal = jax.nn.logsumexp(
        jnp.where(member_query, scores_all[:, :segs_here].reshape(1, -1), MASKED), axis=1
    )
    inner_own = (
        early_sum[:, :ff].reshape(share, reps, devices, share).transpose(0, 2, 1, 3)
    ).reshape(share, ff)
    inner_own, takes = tie(inner_own, takes)
    late_sum = add_near(late_sum, takes)
    outer_own = jnp.concatenate(
        [early_sum[:, ff + q * width : ff + (q + 1) * width] for q in range(early_blocks)]
        + [late_sum[:, 3 * width + span + q * width :][:, :width] for q in range(LATE_BLOCKS)],
        axis=0,
    )
    return (
        jnp.sum(marginal),
        result,
        input_grad,
        late_sum[:, : 3 * width],
        own_biases[:share],
        own_biases[2 * share :],
        early_sum[:, -width:],
        row_of(5),
        row_of(3),
        row_of(4),
        inner_own,
        own_rows[8 * share : (8 + reps) * share],
        outer_own,
        row_of(2),
        row_of(0),
        row_of(1),
        late_sum[:, 3 * width : 3 * width + span],
        answer_own,
    )


def solution(mesh):
    rows = P(AXES, None)
    flat = P(AXES)
    in_specs = (rows,) * 4 + (rows, flat, flat, rows, flat, flat, flat, rows, flat, rows)
    in_specs += (flat, flat, flat, rows, flat)
    out_specs = (P(), rows, rows, rows, flat, flat, rows, flat, flat, flat, rows, flat, rows)
    out_specs += (flat, flat, flat, rows, flat)
    return jax.shard_map(shards, mesh=mesh, in_specs=in_specs, out_specs=out_specs, check_vma=False)
```

```python
import functools, math
import jax, jax.numpy as jnp
from jax import lax
from jax.experimental import pallas as pl
from jax.experimental.pallas import tpu as pltpu
from jax.sharding import PartitionSpec as P
PACK=512; SEGS_PACK=4; HEADS=12; HEAD_DIM=64; LANES=128; SUBLANES=8
MASKED=-1e30
VMEM_MOST=60*1024*1024
F32=jnp.float32; BF16=jnp.bfloat16
def swap(block, axis, mask):
    size = lax.axis_size(axis)
    return lax.ppermute(block, axis, [(i, i ^ mask) for i in range(size)])


def bit_orders(dp):
    bits = [1 << t for t in range(dp.bit_length() - 1)]
    first, others = bits[:1], bits[1:]
    return first + others, first + others[1:] + others[:1]


def offsets(order):
    found = [0]
    for bit in reversed(order):
        found = found + [f | bit for f in found]
    return found


def gather_near(shard):
    if shard.shape[0] % SUBLANES:
        return [lax.all_gather(shard, "fsdp", axis=0, tiled=True)]
    return [shard] + [swap(shard, "fsdp", k) for k in range(1, lax.axis_size("fsdp"))]


class Gathering:
    def __init__(self, pieces, orders, split):
        self.orders = orders
        self.near = len(pieces)
        self.left = len(orders[0]) - 1
        cut = [[p[:, :split] for p in pieces], [p[:, split:] for p in pieces]]
        self.blocks = [jnp.stack(c) for c in cut]
        self.came = None

    def send(self):
        self.came = [swap(b, "dp", o[self.left]) for b, o in zip(self.blocks, self.orders)]

    def join(self):
        self.blocks = [jnp.concatenate([b, c], axis=0) for b, c in zip(self.blocks, self.came)]
        self.left -= 1

    def advance(self, left):
        while self.left > left:
            self.send()
            self.join()

    def parts(self):
        return [self.blocks[0], self.came[0], self.blocks[1], self.came[1]]


def part(block, dim, which):
    return lax.dynamic_index_in_dim(block, which, dim, keepdims=False)


def add_low(a, b):
    return (a.astype(F32) + b.astype(F32)).astype(BF16)


class Reduction:
    def __init__(self, keep, give, order):
        self.order = list(order)
        self.bits = sorted(order, reverse=True)
        self.keep, self.give = keep, give
        self.came = None

    def send(self):
        self.came = swap(self.give, "dp", self.order[0])

    def add(self):
        total = add_low(self.keep, self.came)
        self.bits.remove(self.order.pop(0))
        if not self.order:
            self.keep = total
            return
        total = total.reshape((2,) * len(self.bits) + total.shape[-2:])
        dim = self.bits.index(self.order[0])
        own = (lax.axis_index("dp") // self.order[0]) % 2
        flat = lambda x: x.reshape((-1,) + x.shape[-2:])
        self.keep, self.give = flat(part(total, dim, own)), flat(part(total, dim, 1 - own))

    def advance(self, left):
        while len(self.order) > left:
            self.send()
            self.add()


def start_near(blocks):
    fsdp = lax.axis_size("fsdp")
    split = [b.reshape(fsdp, -1, b.shape[-1]) for b in blocks]
    own = lax.axis_index("fsdp")
    take = lambda k: jnp.concatenate([part(b, 0, own ^ k) for b in split], axis=1)
    return take(0), [swap(take(k), "fsdp", k) for k in range(1, fsdp)]


def add_near(own, came):
    total = own.astype(F32)
    for block in came:
        total = total + block.astype(F32)
    return total


def tie(*groups):
    return lax.optimization_barrier(groups)


def once(shape):
    return pl.BlockSpec(shape,lambda i:(0,)*len(shape),pipeline_mode=pl.Buffered(1))

def dot_nn(a,b): return jnp.dot(a,b,preferred_element_type=F32)
def dot_nt(a,b): return lax.dot_general(a,b,(((1,),(1,)),((),())),preferred_element_type=F32)
def dot_tn(a,b): return lax.dot_general(a,b,(((0,),(0,)),((),())),preferred_element_type=F32)

def segment_tiles(lens_ref, g):
    row=lax.broadcasted_iota(jnp.int32,(PACK,LANES),0)
    lane=lax.broadcasted_iota(jnp.int32,(PACK,LANES),1)
    seg=jnp.zeros((PACK,LANES),jnp.int32); bound=jnp.int32(0)
    for j in range(SEGS_PACK):
        bound=bound+lens_ref[g,j]
        seg=seg+(row>=bound).astype(jnp.int32)
    place=lane-48
    inside=jnp.logical_and(place>=0,place<SEGS_PACK)
    same=place==seg
    apart=jnp.where(jnp.logical_and(inside,jnp.logical_not(same)),MASKED,0.0)
    own=jnp.where(same,1.0,0.0)
    return lane,apart,own

def head_lanes(lane,h):
    return jnp.logical_and(lane<48,lane%16==h)

def assemble(me_ref, orders, fsdp, parts, full_ref, sems):
    copies, start = [], 0
    for color, order in enumerate(orders):
        cols = parts[2 * color].shape[2]
        for half in range(2):
            src = parts[2 * color + half]
            near = offsets(order)[half * src.shape[0] // fsdp :]
            for n in range(src.shape[0]):
                block = (near[n // fsdp] ^ me_ref[0]) * fsdp
                block += (n % fsdp) ^ me_ref[1] if fsdp > 1 else 0
                place = pl.ds(pl.multiple_of(block * src.shape[1], SUBLANES), src.shape[1])
                copies.append(
                    pltpu.make_async_copy(
                        src.at[n], full_ref.at[place, pl.ds(start, cols)], sems.at[len(copies)]
                    )
                )
        start += cols
    for copy in copies:
        copy.start()
    for copy in copies:
        copy.wait()


def whole_div(x, n):
    return jnp.floor((x.astype(F32) + 0.5) * (1.0 / n)).astype(jnp.int32)


def unpack_small(block, share, rows_in, answers):
    width = block.shape[0]
    count = -(-(rows_in * share + answers) // LANES)
    row = lax.broadcasted_iota(jnp.int32, (width, LANES), 0)
    lane = lax.broadcasted_iota(jnp.int32, (width, LANES), 1)
    turned = jnp.concatenate(
        [dot_tn(block, (row == lane * share + k).astype(BF16)) for k in range(count)], axis=0
    ).astype(BF16)
    entry = lax.broadcasted_iota(jnp.int32, (count * LANES, width), 0)
    place = lax.broadcasted_iota(jnp.int32, (count * LANES, width), 1)
    owner = whole_div(lax.broadcasted_iota(jnp.int32, (LANES, width), 1), share)
    owns = (lax.broadcasted_iota(jnp.int32, (LANES, width), 0) == owner).astype(BF16)
    spread = dot_nn(turned, owns)
    fits = entry - whole_div(entry, share) * share == place - whole_div(place, share) * share
    spread = jnp.where(fits, spread, 0.0).astype(BF16)
    vector = lax.broadcasted_iota(jnp.int32, (16, count * LANES), 0)
    source = whole_div(lax.broadcasted_iota(jnp.int32, (16, count * LANES), 1), share)
    vectors = dot_nn((vector == source).astype(BF16), spread)
    line = lax.broadcasted_iota(jnp.int32, (LANES, LANES), 1)
    owns = (lax.broadcasted_iota(jnp.int32, (LANES, LANES), 0) == whole_div(line, answers)).astype(BF16)
    spread = dot_nn(turned, owns)
    entry = lax.broadcasted_iota(jnp.int32, spread.shape, 0) - rows_in * share
    place = lax.broadcasted_iota(jnp.int32, spread.shape, 1)
    fits = entry == place - whole_div(place, answers) * answers
    return vectors, jnp.sum(jnp.where(fits, spread, 0.0), axis=0, keepdims=True)


EPS=1e-6

def normed(h):
    c=h-jnp.mean(h,axis=1,keepdims=True)
    f=lax.rsqrt(jnp.mean(c*c,axis=1,keepdims=True)+EPS)
    return c*f,f

def attention_kernel(orders,fsdp,small,lens_ref,me_ref,tok_ref,p0,p1,p2,p3,w_ref,vec_ref,mix_ref,ctx_ref,inv_ref,wts_ref,n1_ref,r1_ref,low_ref,acc_ref,sems):
    pack=pl.program_id(0)
    width=tok_ref.shape[1]; wide=3*width
    @pl.when(pack==0)
    def _():
        assemble(me_ref,orders,fsdp,(p0,p1,p2,p3),w_ref,sems)
        vectors,answer=unpack_small(w_ref[:,wide+width:],*small)
        vec_ref[...]=vectors
        vec_ref[15:16,:LANES]=answer
    query_row=vec_ref[6:7,:]; value_row=vec_ref[7:8,:]
    lane,apart,own=segment_tiles(lens_ref,pack)
    apart=apart.astype(BF16); own=own.astype(BF16)
    tok=tok_ref[...]
    mix_ref[:,:width]=((dot_nn(tok,w_ref[:,:width])+query_row).astype(BF16).astype(F32)*(1/math.sqrt(HEAD_DIM))).astype(BF16)
    mix_ref[:,width:2*width]=dot_nn(tok,w_ref[:,width:2*width]).astype(BF16)
    mix_ref[:,2*width:]=(dot_nn(tok,w_ref[:,2*width:wide])+value_row).astype(BF16)
    acc_ref[...]=jnp.zeros_like(acc_ref)
    ones=jnp.ones((PACK,LANES),BF16)
    def pair(p,carry):
        at=lambda base: pl.ds(pl.multiple_of(base+p*LANES,LANES),LANES)
        q2=mix_ref[:,at(0)]; k2=mix_ref[:,at(width)]; v2=mix_ref[:,at(2*width)]
        kx=jnp.concatenate([k2,own],axis=1)
        vx=jnp.concatenate([v2,ones],axis=1)
        outs=[]
        for half in range(2):
            qm=jnp.where(lane//HEAD_DIM==half,q2,jnp.zeros_like(q2))
            s=dot_nt(jnp.concatenate([qm,apart],axis=1),kx)
            m=jnp.max(s,axis=1,keepdims=True)
            w=jnp.exp(s-m).astype(BF16)
            wts_ref[2*p+half]=w
            o=dot_nn(w,vx)
            inv=1.0/o[:,LANES:]
            outs.append(o[:,:LANES]*inv)
            acc_ref[...]=jnp.where(head_lanes(lane,2*p+half),inv,acc_ref[...])
        ctx_ref[:,at(0)]=jnp.where(lane<HEAD_DIM,outs[0],outs[1]).astype(BF16)
        return carry
    lax.fori_loop(0,HEADS//2,pair,0)
    inv_ref[...]=acc_ref[...]
    att=dot_nn(ctx_ref[...],w_ref[:,wide:wide+width])+vec_ref[0:1,:]
    n1,f1=normed(tok.astype(F32)+att)
    n1_ref[...]=n1; r1_ref[...]=jnp.broadcast_to(f1,r1_ref.shape)
    low_ref[...]=(n1*vec_ref[1:2,:]+vec_ref[2:3,:]).astype(BF16)

def attention(lens,me,tok,parts,orders,fsdp,small):
    rows,width=tok.shape; share=parts[0].shape[1]; full=parts[0].shape[2]+parts[2].shape[2]
    hbm=pl.BlockSpec(memory_space=pl.ANY)
    sm=pl.BlockSpec(memory_space=pltpu.SMEM)
    wide=3*width
    sizes=((wide,BF16),(width,BF16),(LANES,F32))
    outs=[jax.ShapeDtypeStruct((rows,n),t) for n,t in sizes]
    heads=[jax.ShapeDtypeStruct((width,full),BF16),jax.ShapeDtypeStruct((16,width),F32)]
    fixed=[once((width,full)),once((16,width))]
    cost=pl.CostEstimate(flops=2*rows*width*wide+8*rows*PACK*width,bytes_accessed=rows*wide*4,transcendentals=HEADS*PACK*rows)
    spec=lambda n: pl.BlockSpec((PACK,n),lambda g:(g,0))
    return pl.pallas_call(functools.partial(attention_kernel,orders,fsdp,small),grid=(rows//PACK,),
        in_specs=[sm,sm,spec(width)]+[hbm]*4,out_specs=fixed+[spec(n) for n,_ in sizes]+[pl.BlockSpec((HEADS,PACK,PACK),lambda g:(g,0,0)),spec(width),spec(LANES),spec(width)],
        out_shape=heads+outs+[jax.ShapeDtypeStruct((rows//PACK*HEADS,PACK,PACK),BF16),jax.ShapeDtypeStruct((rows,width),F32),jax.ShapeDtypeStruct((rows,LANES),F32),jax.ShapeDtypeStruct((rows,width),BF16)],
        scratch_shapes=[pltpu.VMEM((PACK,LANES),F32),pltpu.SemaphoreType.DMA((4*parts[0].shape[0],))],
        compiler_params=pltpu.CompilerParams(vmem_limit_bytes=VMEM_MOST),name='attention',cost_estimate=cost)(lens,me,tok,*parts)

def split_three(x,lane):
    hi=x.astype(BF16).astype(F32)
    rest=x-hi
    mid=rest.astype(BF16).astype(F32)
    return jnp.where(lane<16,hi,jnp.where(lane<32,mid,jnp.where(lane<48,rest-mid,0.0)))

def attention_grad_kernel(q_ref,k_ref,v_ref,ctx_ref,dctx_ref,inv_ref,wts_ref,out_ref):
    p=pl.program_id(1)
    width=out_ref.shape[1]//3
    lane=lax.broadcasted_iota(jnp.int32,(PACK,LANES),1)
    at=lambda base: pl.ds(pl.multiple_of(base+p*LANES,LANES),LANES)
    q2=q_ref[...]; k2=k_ref[...]; v2=v_ref[...]; d2=dctx_ref[...].astype(F32)
    invs=[jnp.sum(jnp.where(lane==2*p+half,inv_ref[...],0.0),axis=1,keepdims=True) for half in range(2)]
    d2=d2*jnp.where(lane<HEAD_DIM,invs[0],invs[1])
    prod=d2*ctx_ref[...].astype(F32)
    d2=d2.astype(BF16)
    qt=q2.T; dt=d2.T
    mark=head_lanes(lane,0).astype(BF16)
    vx=jnp.concatenate([v2,mark],axis=1)
    dq=[]; dks=[]; dvs=[]
    for half in range(2):
        here=lane//HEAD_DIM==half
        dm=jnp.where(here,d2,jnp.zeros_like(d2))
        dots=jnp.sum(jnp.where(here,prod,0.0),axis=1,keepdims=True)
        de=(-split_three(jnp.broadcast_to(dots,(PACK,LANES)),lane)).astype(BF16)
        w=wts_ref[half]
        dp=dot_nt(jnp.concatenate([dm,de],axis=1),vx)
        ds=(w.astype(F32)*dp).astype(BF16)
        rows=slice(half*HEAD_DIM,(half+1)*HEAD_DIM)
        dq.append(dot_nn(ds,k2))
        dks.append(dot_nn(qt[rows],ds))
        dvs.append(dot_nn(dt[rows],w))
    out_ref[:,at(0)]=(jnp.where(lane<HEAD_DIM,dq[0],dq[1])*(1/math.sqrt(HEAD_DIM))).astype(BF16)
    out_ref[:,at(width)]=jnp.concatenate(dks,axis=0).T.astype(BF16)
    out_ref[:,at(2*width)]=jnp.concatenate(dvs,axis=0).T.astype(BF16)

def attention_grad(mix,ctx,dctx,inv,wts):
    rows,width=ctx.shape; wide=mix.shape[1]; pairs=HEADS//2
    pair=lambda at: pl.BlockSpec((PACK,LANES),lambda g,p:(g,at*pairs+p))
    return pl.pallas_call(attention_grad_kernel,grid=(rows//PACK,pairs),
        in_specs=[pair(0),pair(1),pair(2),pair(0),pair(0),pl.BlockSpec((PACK,LANES),lambda g,p:(g,0)),pl.BlockSpec((2,PACK,PACK),lambda g,p:(g*pairs+p,0,0))],
        out_specs=pl.BlockSpec((PACK,wide),lambda g,p:(g,0)),out_shape=jax.ShapeDtypeStruct((rows,wide),BF16),
        compiler_params=pltpu.CompilerParams(vmem_limit_bytes=VMEM_MOST),name='attention_grad',
        cost_estimate=pl.CostEstimate(flops=16*rows*PACK*width,bytes_accessed=rows*wide*8,transcendentals=0))(mix,mix,mix,ctx,dctx,inv,wts)
TILE=256
def half_tail(a, e):
    t=1.0/(1.0+0.3275911*a)
    p=t*(0.5*0.254829592+t*(0.5*-0.284496736+t*(0.5*1.421413741+t*(0.5*-1.453152027+t*(0.5*1.061405429)))))
    return p*e

def gelu_pair(x):
    z=jnp.abs(x)*(1/math.sqrt(2))
    e=jnp.exp(-z*z)
    h=half_tail(z,e)
    phi=jnp.where(x>0,1.0-h,h)
    return x*phi, phi+x*(e*(1/math.sqrt(2*math.pi)))

def norm_back(e,n,f):
    return f*(e-jnp.mean(e,axis=1,keepdims=True)-n*jnp.mean(e*n,axis=1,keepdims=True))

def row_segments(lens_ref,first_row,rows):
    row=first_row+lax.broadcasted_iota(jnp.int32,(rows,LANES),0)
    lane=lax.broadcasted_iota(jnp.int32,(rows,LANES),1)
    packs=lens_ref.shape[0]
    seg=jnp.zeros((rows,LANES),jnp.int32)
    for g in range(packs):
        end=jnp.int32(g*PACK)
        for j in range(SEGS_PACK):
            end=end+lens_ref[g,j]
            seg=seg+(row>=end).astype(jnp.int32)
    return seg==lane

def feed_forward_kernel(lens_ref,n1_ref,low_ref,w_ref,vec_ref,act_ref,dg_ref,n2_ref,r2_ref,res_ref,span_ref,score_ref,doc_ref,all_ref):
    i=pl.program_id(0)
    rows,width=n1_ref.shape; reps=act_ref.shape[1]//width
    vec=lambda k: vec_ref[k:k+1,:]
    base=2*reps*width
    low=low_ref[...]
    out=n1_ref[...]*vec(1)+vec(2)+vec(3)
    for q in range(reps):
        c=slice(q*width,(q+1)*width)
        x=dot_nn(low,w_ref[:,c])+vec(8+q)
        a,d=gelu_pair(x)
        a=a.astype(BF16)
        act_ref[:,c]=a; dg_ref[:,c]=d.astype(BF16)
        out=out+dot_nn(a,w_ref[:,(reps+q)*width:(reps+q+1)*width])
    n2,f2=normed(out)
    n2_ref[...]=n2; r2_ref[...]=jnp.broadcast_to(f2,(rows,LANES))
    res=(n2*vec(4)+vec(5)).astype(BF16)
    res_ref[...]=res
    span=dot_nn(res,w_ref[:,base:base+LANES])
    span_ref[...]=span
    score=jnp.broadcast_to(jnp.sum(span*vec_ref[15:16,:LANES],axis=1,keepdims=True),(rows,LANES))
    score_ref[...]=score
    all_ref[pl.ds(pl.multiple_of(i*rows,rows),rows),:]=score
    @pl.when(i==pl.num_programs(0)-1)
    def _():
        member=row_segments(lens_ref,0,all_ref.shape[0])
        s=jnp.where(member,all_ref[...],MASKED)
        top=jnp.max(s,axis=0,keepdims=True)
        total=jnp.sum(jnp.where(member,jnp.exp(s-top),0.0),axis=0,keepdims=True)
        real=lax.broadcasted_iota(jnp.int32,(1,LANES),1)<lens_ref.shape[0]*SEGS_PACK
        doc_ref[...]=jnp.where(real,top+jnp.log(jnp.where(real,total,1.0)),MASKED)

def feed_forward(lens,n1,low,w,vec,reps):
    rows,width=n1.shape; ff=reps*width
    b=lambda n: pl.BlockSpec((TILE,n),lambda i:(i,0))
    s=lambda n,t: jax.ShapeDtypeStruct((rows,n),t)
    return pl.pallas_call(feed_forward_kernel,grid=(rows//TILE,),
        in_specs=[pl.BlockSpec(memory_space=pltpu.SMEM),b(width),b(width),once(w.shape),once(vec.shape)],
        out_specs=[b(ff),b(ff),b(width),b(LANES),b(width),b(LANES),b(LANES),once((1,LANES))],
        out_shape=[s(ff,BF16),s(ff,BF16),s(width,F32),s(LANES,F32),s(width,BF16),s(LANES,F32),s(LANES,F32),jax.ShapeDtypeStruct((1,LANES),F32)],
        scratch_shapes=[pltpu.VMEM((rows,LANES),F32)],
        compiler_params=pltpu.CompilerParams(vmem_limit_bytes=VMEM_MOST),name='feed_forward')(lens,n1,low,w,vec)

def feed_forward_grad_kernel(lens_ref,own_ids_ref,doc_ref,scores_ref,ids_ref,cot_ref,n2_ref,r2_ref,res_ref,span_ref,score_ref,dg_ref,n1_ref,r1_ref,w_ref,aw_ref,vec_ref,
                   low_ref,fsum_ref,dctx_ref,small_ref,spanw_ref,weight_ref,acc_ref):
    i=pl.program_id(0); last=pl.num_programs(0)-1
    rows,width=cot_ref.shape; reps=dg_ref.shape[1]//width
    vec=lambda k: vec_ref[k:k+1,:]
    base=2*reps*width
    @pl.when(i==0)
    def _():
        lane=lax.broadcasted_iota(jnp.int32,(1,LANES),1)
        marg=jnp.zeros((1,LANES),F32)
        for s in range(own_ids_ref.shape[0]):
            hit=ids_ref[...]==own_ids_ref[s].astype(F32)
            x=jnp.where(hit,scores_ref[...],MASKED)
            top=jnp.max(jnp.max(x,axis=1,keepdims=True),axis=0,keepdims=True)
            total=jnp.where(hit,jnp.exp(x-top),0.0)
            total=jnp.sum(jnp.sum(total,axis=1,keepdims=True),axis=0,keepdims=True)
            marg=jnp.where(lane==s,top+jnp.log(total),marg)
        weight_ref[...]=jnp.exp(doc_ref[...]-marg)
        small_ref[...]=jnp.zeros_like(small_ref)
        acc_ref[...]=jnp.zeros_like(acc_ref)
    member=row_segments(lens_ref,i*rows,rows)
    part=jnp.where(member,jnp.exp(jnp.where(member,score_ref[...]-doc_ref[...],0.0))*weight_ref[...],0.0)
    tw=jnp.sum(part,axis=1,keepdims=True)
    ans=vec_ref[15:16,:LANES]
    small_ref[15:16,:LANES]+=jnp.sum(tw*span_ref[...],axis=0,keepdims=True)
    sg=(tw*ans).astype(BF16)
    acc_ref[...]+=dot_tn(res_ref[...],sg)
    @pl.when(i==last)
    def _():
        spanw_ref[...]=acc_ref[...].astype(BF16)
    rg=cot_ref[...].astype(F32)+dot_nt(sg,w_ref[:,base:base+LANES])
    n2=n2_ref[...]
    def colsum(k,v):
        small_ref[k:k+1,:]+=jnp.sum(v,axis=0,keepdims=True)
    colsum(0,rg*n2); colsum(1,rg)
    ssum=norm_back(rg*vec(4),n2,r2_ref[:,:1])
    olow=ssum.astype(BF16); low_ref[:,reps*width:(reps+1)*width]=olow
    colsum(2,olow.astype(F32))
    fg=ssum
    for q in range(reps):
        c=slice(q*width,(q+1)*width)
        il=(dot_nt(olow,w_ref[:,(reps+q)*width:(reps+q+1)*width])*dg_ref[:,c].astype(F32)).astype(BF16)
        low_ref[:,c]=il
        colsum(8+q,il.astype(F32))
        fg=fg+dot_nt(il,w_ref[:,c])
    n1=n1_ref[...]
    colsum(3,fg*n1); colsum(4,fg)
    fsum=norm_back(fg*vec(1),n1,r1_ref[:,:1])
    fsum_ref[...]=fsum
    alow=fsum.astype(BF16); low_ref[:,(reps+1)*width:]=alow
    colsum(5,alow.astype(F32))
    dctx_ref[...]=dot_nt(alow,aw_ref[...]).astype(BF16)

def feed_forward_grad(lens,own_ids,doc,scores,ids,cot,n2,r2,res,span,score,dg,n1,r1,w,mix,vec):
    rows,width=cot.shape; ff=dg.shape[1]
    b=lambda n: pl.BlockSpec((TILE,n),lambda i:(i,0))
    s=lambda n,t: jax.ShapeDtypeStruct((rows,n),t)
    sm=pl.BlockSpec(memory_space=pltpu.SMEM)
    return pl.pallas_call(feed_forward_grad_kernel,grid=(rows//TILE,),
        in_specs=[sm,sm,once(doc.shape),once(scores.shape),once(ids.shape),b(width),b(width),b(LANES),b(width),b(LANES),b(LANES),b(ff),b(width),b(LANES),once(w.shape),pl.BlockSpec((width,width),lambda i:(0,3),pipeline_mode=pl.Buffered(1)),once(vec.shape)],
        out_specs=[b(ff+2*width),b(width),b(width),once(vec.shape),once((width,LANES))],
        out_shape=[s(ff+2*width,BF16),s(width,F32),s(width,BF16),jax.ShapeDtypeStruct(vec.shape,F32),jax.ShapeDtypeStruct((width,LANES),BF16)],
        scratch_shapes=[pltpu.VMEM((1,LANES),F32),pltpu.VMEM((width,LANES),F32)],
        compiler_params=pltpu.CompilerParams(vmem_limit_bytes=VMEM_MOST),name='feed_forward_grad')(lens,own_ids,doc,scores,ids,cot,n2,r2,res,span,score,dg,n1,r1,w,mix,vec)

def put_blocks(me_ref,keep_ref,give_ref,value,at):
    blocks,rows,_=keep_ref.shape
    second=me_ref[0]%2
    for t in range(blocks):
        low=value[2*t*rows:(2*t+1)*rows].astype(BF16)
        high=value[(2*t+1)*rows:(2*t+2)*rows].astype(BF16)
        @pl.when(second==0)
        def _():
            keep_ref[t,:,at]=low; give_ref[t,:,at]=high
        @pl.when(second==1)
        def _():
            keep_ref[t,:,at]=high; give_ref[t,:,at]=low

def early_kernel(reps,me_ref,low_hbm,act_hbm,ctx_hbm,right_ref,keep_ref,give_ref,left_ref,sems):
    j=pl.program_id(0); slots,_,width=left_ref.shape
    sources=[low_hbm]+[act_hbm.at[:,pl.ds(k*width,width)] for k in range(slots-2)]+[ctx_hbm]
    moves=[pltpu.make_async_copy(src,left_ref.at[k],sems.at[k]) for k,src in enumerate(sources)]
    @pl.when(j==0)
    def _():
        for move in moves: move.start()
    for k,move in enumerate(moves):
        @pl.when(j==(0 if k==0 else reps+k-1))
        def _(): move.wait()
    put_blocks(me_ref,keep_ref,give_ref,dot_tn(left_ref[jnp.maximum(j-reps+1,0)],right_ref[...]),slice(None))

def split_outs(dp,width,n):
    block=(dp//2,width//dp,width)
    return [pl.BlockSpec(block,lambda j:(0,0,j))]*2,[jax.ShapeDtypeStruct(block[:2]+(n*width,),BF16)]*2

def early_grads(me,low,act,ctx,right,outer_blocks,dp):
    rows,width=low.shape; reps=act.shape[1]//width
    n=reps+outer_blocks+1
    specs,shapes=split_outs(dp,width,n)
    hbm=pl.BlockSpec(memory_space=pl.ANY)
    column=lambda j: jnp.where(j<reps,j,jnp.where(j<n-1,reps,reps+1))
    return pl.pallas_call(functools.partial(early_kernel,reps),grid=(n,),
        in_specs=[pl.BlockSpec(memory_space=pltpu.SMEM),hbm,hbm,hbm,pl.BlockSpec((rows,width),lambda j:(0,column(j)))],
        out_specs=specs,out_shape=shapes,scratch_shapes=[pltpu.VMEM((outer_blocks+2,rows,width),BF16),pltpu.SemaphoreType.DMA((outer_blocks+2,))],
        compiler_params=pltpu.CompilerParams(vmem_limit_bytes=VMEM_MOST),name='early_weight_grads',
        cost_estimate=pl.CostEstimate(flops=2*rows*width*width*n,bytes_accessed=rows*width*n*4,transcendentals=0))(me,low,act,ctx,right)

def outer_kernel(me_ref,act_ref,olow_ref,keep_ref,give_ref):
    put_blocks(me_ref,keep_ref,give_ref,dot_tn(act_ref[...],olow_ref[...]),slice(None))

def outer_grads(me,act,right,first,dp):
    rows,ff=act.shape; width=right.shape[1]-ff>>1; n=ff//width-first
    specs,shapes=split_outs(dp,width,n)
    return pl.pallas_call(outer_kernel,grid=(n,),
        in_specs=[pl.BlockSpec(memory_space=pltpu.SMEM),pl.BlockSpec((rows,width),lambda j:(0,j+first)),pl.BlockSpec((rows,width),lambda j:(0,ff//width),pipeline_mode=pl.Buffered(1))],
        out_specs=specs,out_shape=shapes,
        compiler_params=pltpu.CompilerParams(vmem_limit_bytes=VMEM_MOST),name='outer_weight_grad',
        cost_estimate=pl.CostEstimate(flops=2*rows*width*width*n,bytes_accessed=rows*width*n*4,transcendentals=0))(me,act,right)

def late_kernel(me_ref,tok_ref,mg_ref,span_ref,keep_ref,give_ref,sum_ref):
    j=pl.program_id(0)
    width=tok_ref.shape[1]
    mg=mg_ref[...]
    sum_ref[...]=jnp.broadcast_to(jnp.sum(mg.astype(F32),axis=0,keepdims=True),sum_ref.shape)
    put_blocks(me_ref,keep_ref,give_ref,dot_tn(tok_ref[...],mg),pl.ds(pl.multiple_of(j*width,LANES),width))
    @pl.when(j==pl.num_programs(0)-1)
    def _():
        full=keep_ref.shape[2]
        put_blocks(me_ref,keep_ref,give_ref,span_ref[...].astype(F32),slice(full-span_ref.shape[1],full))

def late_grads(me,tok,mg,span,dp):
    rows,width=tok.shape; wide=mg.shape[1]
    out=(dp//2,width//dp,wide+span.shape[1])
    return pl.pallas_call(late_kernel,grid=(wide//width,),
        in_specs=[pl.BlockSpec(memory_space=pltpu.SMEM),once((rows,width)),pl.BlockSpec((rows,width),lambda j:(0,j)),once(span.shape)],
        out_specs=[once(out),once(out),pl.BlockSpec((8,width),lambda j:(0,j))],
        out_shape=[jax.ShapeDtypeStruct(out,BF16)]*2+[jax.ShapeDtypeStruct((8,wide),F32)],
        compiler_params=pltpu.CompilerParams(vmem_limit_bytes=VMEM_MOST),name='late_weight_grads',
        cost_estimate=pl.CostEstimate(flops=2*rows*width*wide,bytes_accessed=rows*wide*4,transcendentals=0))(me,tok,mg,span)

def input_kernel(sizes,w_ref,fs_ref,*refs):
    *mgs,out_ref=refs
    width=fs_ref.shape[1]
    total=fs_ref[...]
    start=0
    for mg_ref,n in zip(mgs,sizes):
        for k in range(3):
            total=total+dot_nt(mg_ref[:,k*n:(k+1)*n],w_ref[:,k*width+start:k*width+start+n])
        start+=n
    out_ref[...]=total

def input_grads(w,fs,mgs):
    rows,width=fs.shape
    b=lambda n: pl.BlockSpec((TILE,n),lambda i:(i,0))
    return pl.pallas_call(functools.partial(input_kernel,[m.shape[1]//3 for m in mgs]),grid=(rows//TILE,),
        in_specs=[once((width,3*width)),b(width)]+[b(m.shape[1]) for m in mgs],out_specs=b(width),out_shape=jax.ShapeDtypeStruct((rows,width),F32),
        compiler_params=pltpu.CompilerParams(vmem_limit_bytes=VMEM_MOST),name='input_grad',
        cost_estimate=pl.CostEstimate(flops=6*rows*width*width,bytes_accessed=rows*width*16,transcendentals=0))(w,fs,*mgs)
AXES = ("dp", "fsdp")
LATE_BLOCKS = 3


def pack_lanes(parts):
    flat = jnp.concatenate(parts, axis=-1)
    wide = -(-flat.shape[-1] // LANES) * LANES
    flat = jnp.pad(flat, [(0, 0)] * (flat.ndim - 1) + [(0, wide - flat.shape[-1])])
    return flat.reshape(flat.shape[:-1] + (wide // LANES, LANES))


def unpack_lanes(packed, sizes):
    flat = packed.reshape(packed.shape[:-2] + (-1,))
    starts = [sum(sizes[:i]) for i in range(len(sizes))]
    return [flat[..., a : a + n] for a, n in zip(starts, sizes)]


def to_all(block, devices):
    return lax.all_to_all(jnp.broadcast_to(block[None], (devices,) + block.shape), AXES, 0, 0)


def shards(
    tokens,
    cotangent,
    doc_lengths,
    query_ids,
    qkv_weight,
    query_bias,
    value_bias,
    attn_weight,
    attn_bias,
    first_gain,
    first_shift,
    inner_weight,
    inner_bias,
    outer_weight,
    outer_bias,
    second_gain,
    second_shift,
    span_weight,
    answer_vector,
):
    rows, width = tokens.shape
    packs_here = rows // PACK
    devices = lax.axis_size("dp") * lax.axis_size("fsdp")
    share = qkv_weight.shape[0]
    ff = inner_weight.shape[1]
    reps = ff // width
    segs_here = packs_here * SEGS_PACK
    span = span_weight.shape[1]

    row_params = (attn_bias, first_gain, first_shift, outer_bias, second_gain, second_shift)
    smalls = row_params + (query_bias, value_bias, inner_bias, answer_vector)
    answers = answer_vector.shape[0]
    rows_in = len(row_params) + 2 + reps
    packed = pack_lanes(smalls)
    packed = jnp.pad(packed, ((0, share - packed.shape[0]), (0, 0)))
    id_row = jnp.pad(
        query_ids[:, 0].astype(F32)[None], ((0, 0), (0, LANES - segs_here)), constant_values=-1.0
    )

    orders = bit_orders(lax.axis_size("dp"))
    fsdp = lax.axis_size("fsdp")
    me = jnp.stack([lax.axis_index("dp"), lax.axis_index("fsdp")]).astype(jnp.int32)
    mix = jnp.concatenate([qkv_weight, attn_weight, packed], axis=1)
    mix_near = gather_near(mix)
    near = len(mix_near)
    mix_walk = Gathering(mix_near, orders, 2 * width)
    mix_walk.advance(0)
    mix_walk.send()
    mix_parts = mix_walk.parts()
    inner_turned = (
        inner_weight.reshape(share, devices, reps, share).transpose(0, 2, 1, 3).reshape(share, ff)
    )
    outer_blocks = [outer_weight[q * share : (q + 1) * share] for q in range(reps)]
    rest = jnp.concatenate([inner_turned] + outer_blocks + [span_weight], axis=1)
    rest_full = lax.all_gather(rest, AXES, axis=0, tiled=True)

    (
        mix_full,
        vectors,
        mixed,
        context,
        inverse,
        weights,
        normed_one,
        factor_one,
        first_low,
    ) = attention(doc_lengths, me, tokens, mix_parts, orders, near, (share, rows_in, answers))
    active, gelu_slope, normed_two, factor_two, result, span_rows, token_score, doc_score = (
        feed_forward(doc_lengths, normed_one, first_low, rest_full, vectors, reps)
    )
    exchanged = to_all(jnp.concatenate([doc_score, id_row], axis=0), devices)
    scores_all, ids_all = exchanged[:, 0], exchanged[:, 1]

    lows, first_sum_grad, context_grad, small_sums, span_grad = (
        feed_forward_grad(
            doc_lengths,
            query_ids.reshape(-1),
            doc_score,
            scores_all,
            ids_all,
            cotangent,
            normed_two,
            factor_two,
            result,
            span_rows,
            token_score,
            gelu_slope,
            normed_one,
            factor_one,
            rest_full,
            mix_full,
            vectors,
        )
    )
    early_blocks = reps - LATE_BLOCKS
    dp = lax.axis_size("dp")
    keep, give = early_grads(me, first_low, active, context, lows, early_blocks, dp)
    came = swap(give, "dp", orders[0][0])
    lows, keep = tie(lows, keep)
    outer_walk = Reduction(*outer_grads(me, active, lows, early_blocks, dp), orders[1])
    came, outer_walk.keep = tie(came, outer_walk.keep)
    outer_walk.send()
    early = add_low(keep, came)
    cores = [[d for d in range(dp) if d % 2 == c] for c in range(2)]
    early_dp = lax.psum_scatter(
        early.reshape(-1, early.shape[-1]),
        "dp",
        scatter_dimension=0,
        axis_index_groups=cores,
        tiled=True,
    )
    context_grad, early = tie(context_grad, early)
    mixed_grad = attention_grad(mixed, context, context_grad, inverse, weights)
    mixed_grad, outer_walk.came = tie(mixed_grad, outer_walk.came)
    *late, bias_sums = late_grads(me, tokens, mixed_grad, span_grad, dp)
    late, outer_walk.came = tie(late, outer_walk.came)
    late_walk = Reduction(*late, orders[0])
    late_walk.send()
    outer_walk.add()
    outer_walk.advance(2)
    outer_walk.send()
    n_rows = small_sums.shape[0]
    by_owner = small_sums.reshape(n_rows, devices, share).transpose(1, 0, 2)
    biases = bias_sums[0].reshape(3, devices, share).transpose(1, 0, 2)
    small_grads = pack_lanes(
        [
            by_owner.reshape(devices, n_rows * share),
            biases.reshape(devices, 3 * share),
            small_sums[15, :span].reshape(devices, span // devices),
        ]
    )
    small_grads, late_walk.came, outer_walk.give = tie(
        small_grads, late_walk.came, outer_walk.give
    )
    late_walk.add()
    late_walk.advance(2)
    late_walk.send()
    small_grads, early_dp, late_walk.keep, outer_walk.keep = tie(
        small_grads, early_dp, late_walk.keep, outer_walk.keep
    )
    received = lax.all_to_all(small_grads, AXES, 0, 0)
    early_sum, early_takes = start_near([early_dp])
    scores_all, first_sum_grad, early_sum = tie(scores_all, first_sum_grad, early_sum)
    input_grad = input_grads(mix_full, first_sum_grad, [mixed_grad])
    input_grad, early_takes, late_walk.came, outer_walk.came = tie(
        input_grad, early_takes, late_walk.came, outer_walk.came
    )
    outer_walk.add()
    outer_walk.send()
    late_walk.add()
    late_walk.send()
    received, late_walk.came, outer_walk.came = tie(
        received, late_walk.came, outer_walk.came
    )
    outer_walk.add()
    late_walk.add()
    late_sum, takes = start_near([late_walk.keep, outer_walk.keep])
    received, early_takes, late_sum = tie(received, early_takes, late_sum)
    early_sum = add_near(early_sum, early_takes)
    mine = jnp.sum(received, axis=0)
    own_rows, own_biases, answer_own = unpack_lanes(
        mine, [n_rows * share, 3 * share, span // devices]
    )
    row_of = lambda k: own_rows[k * share : (k + 1) * share]
    queries = lax.broadcasted_iota(F32, (packs_here * devices, 1), 0)
    member_query = ids_all[:, :segs_here].reshape(1, -1) == queries
    marginal = jax.nn.logsumexp(
        jnp.where(member_query, scores_all[:, :segs_here].reshape(1, -1), MASKED), axis=1
    )
    inner_own = (
        early_sum[:, :ff].reshape(share, reps, devices, share).transpose(0, 2, 1, 3)
    ).reshape(share, ff)
    inner_own, takes = tie(inner_own, takes)
    late_sum = add_near(late_sum, takes)
    outer_own = jnp.concatenate(
        [early_sum[:, ff + q * width : ff + (q + 1) * width] for q in range(early_blocks)]
        + [late_sum[:, 3 * width + span + q * width :][:, :width] for q in range(LATE_BLOCKS)],
        axis=0,
    )
    return (
        jnp.sum(marginal),
        result,
        input_grad,
        late_sum[:, : 3 * width],
        own_biases[:share],
        own_biases[2 * share :],
        early_sum[:, -width:],
        row_of(5),
        row_of(3),
        row_of(4),
        inner_own,
        own_rows[8 * share : (8 + reps) * share],
        outer_own,
        row_of(2),
        row_of(0),
        row_of(1),
        late_sum[:, 3 * width : 3 * width + span],
        answer_own,
    )


def solution(mesh):
    rows = P(AXES, None)
    flat = P(AXES)
    in_specs = (rows,) * 4 + (rows, flat, flat, rows, flat, flat, flat, rows, flat, rows)
    in_specs += (flat, flat, flat, rows, flat)
    out_specs = (P(), rows, rows, rows, flat, flat, rows, flat, flat, flat, rows, flat, rows)
    out_specs += (flat, flat, flat, rows, flat)
    return jax.shard_map(shards, mesh=mesh, in_specs=in_specs, out_specs=out_specs, check_vma=False)
```

```python
import functools, math
import jax, jax.numpy as jnp
from jax import lax
from jax.experimental import pallas as pl
from jax.experimental.pallas import tpu as pltpu
from jax.sharding import PartitionSpec as P
PACK=512; SEGS_PACK=4; HEADS=12; HEAD_DIM=64; LANES=128; SUBLANES=8
MASKED=-1e30
VMEM_MOST=60*1024*1024
F32=jnp.float32; BF16=jnp.bfloat16
def swap(block, axis, mask):
    size = lax.axis_size(axis)
    return lax.ppermute(block, axis, [(i, i ^ mask) for i in range(size)])


def bit_orders(dp):
    bits = [1 << t for t in range(dp.bit_length() - 1)]
    first, others = bits[:1], bits[1:]
    return first + others, first + others[1:] + others[:1]


def offsets(order):
    found = [0]
    for bit in reversed(order):
        found = found + [f | bit for f in found]
    return found


def gather_near(shard):
    if shard.shape[0] % SUBLANES:
        return [lax.all_gather(shard, "fsdp", axis=0, tiled=True)]
    return [shard] + [swap(shard, "fsdp", k) for k in range(1, lax.axis_size("fsdp"))]


class Gathering:
    def __init__(self, pieces, orders, split):
        self.orders = orders
        self.near = len(pieces)
        self.left = len(orders[0]) - 1
        cut = [[p[:, :split] for p in pieces], [p[:, split:] for p in pieces]]
        self.blocks = [jnp.stack(c) for c in cut]
        self.came = None

    def send(self):
        self.came = [swap(b, "dp", o[self.left]) for b, o in zip(self.blocks, self.orders)]

    def join(self):
        self.blocks = [jnp.concatenate([b, c], axis=0) for b, c in zip(self.blocks, self.came)]
        self.left -= 1

    def advance(self, left):
        while self.left > left:
            self.send()
            self.join()

    def parts(self):
        return [self.blocks[0], self.came[0], self.blocks[1], self.came[1]]


def part(block, dim, which):
    return lax.dynamic_index_in_dim(block, which, dim, keepdims=False)


def add_low(a, b):
    return (a.astype(F32) + b.astype(F32)).astype(BF16)


class Reduction:
    def __init__(self, keep, give, order):
        self.order = list(order)
        self.bits = sorted(order, reverse=True)
        self.keep, self.give = keep, give
        self.came = None

    def send(self):
        self.came = swap(self.give, "dp", self.order[0])

    def add(self):
        total = add_low(self.keep, self.came)
        self.bits.remove(self.order.pop(0))
        if not self.order:
            self.keep = total
            return
        total = total.reshape((2,) * len(self.bits) + total.shape[-2:])
        dim = self.bits.index(self.order[0])
        own = (lax.axis_index("dp") // self.order[0]) % 2
        flat = lambda x: x.reshape((-1,) + x.shape[-2:])
        self.keep, self.give = flat(part(total, dim, own)), flat(part(total, dim, 1 - own))

    def advance(self, left):
        while len(self.order) > left:
            self.send()
            self.add()


def start_near(blocks):
    fsdp = lax.axis_size("fsdp")
    split = [b.reshape(fsdp, -1, b.shape[-1]) for b in blocks]
    own = lax.axis_index("fsdp")
    take = lambda k: jnp.concatenate([part(b, 0, own ^ k) for b in split], axis=1)
    return take(0), [swap(take(k), "fsdp", k) for k in range(1, fsdp)]


def add_near(own, came):
    total = own.astype(F32)
    for block in came:
        total = total + block.astype(F32)
    return total


def tie(*groups):
    return lax.optimization_barrier(groups)


def once(shape):
    return pl.BlockSpec(shape,lambda i:(0,)*len(shape),pipeline_mode=pl.Buffered(1))

def dot_nn(a,b): return jnp.dot(a,b,preferred_element_type=F32)
def dot_nt(a,b): return lax.dot_general(a,b,(((1,),(1,)),((),())),preferred_element_type=F32)
def dot_tn(a,b): return lax.dot_general(a,b,(((0,),(0,)),((),())),preferred_element_type=F32)

def segment_tiles(lens_ref, g):
    row=lax.broadcasted_iota(jnp.int32,(PACK,LANES),0)
    lane=lax.broadcasted_iota(jnp.int32,(PACK,LANES),1)
    seg=jnp.zeros((PACK,LANES),jnp.int32); bound=jnp.int32(0)
    for j in range(SEGS_PACK):
        bound=bound+lens_ref[g,j]
        seg=seg+(row>=bound).astype(jnp.int32)
    place=lane-48
    inside=jnp.logical_and(place>=0,place<SEGS_PACK)
    same=place==seg
    apart=jnp.where(jnp.logical_and(inside,jnp.logical_not(same)),MASKED,0.0)
    own=jnp.where(same,1.0,0.0)
    return lane,apart,own

def head_lanes(lane,h):
    return jnp.logical_and(lane<48,lane%16==h)

def assemble(me_ref, orders, fsdp, parts, full_ref, sems):
    copies, start = [], 0
    for color, order in enumerate(orders):
        cols = parts[2 * color].shape[2]
        for half in range(2):
            src = parts[2 * color + half]
            near = offsets(order)[half * src.shape[0] // fsdp :]
            for n in range(src.shape[0]):
                block = (near[n // fsdp] ^ me_ref[0]) * fsdp
                block += (n % fsdp) ^ me_ref[1] if fsdp > 1 else 0
                place = pl.ds(pl.multiple_of(block * src.shape[1], SUBLANES), src.shape[1])
                copies.append(
                    pltpu.make_async_copy(
                        src.at[n], full_ref.at[place, pl.ds(start, cols)], sems.at[len(copies)]
                    )
                )
        start += cols
    for copy in copies:
        copy.start()
    for copy in copies:
        copy.wait()


def whole_div(x, n):
    return jnp.floor((x.astype(F32) + 0.5) * (1.0 / n)).astype(jnp.int32)


def unpack_small(block, share, rows_in, answers):
    width = block.shape[0]
    count = -(-(rows_in * share + answers) // LANES)
    row = lax.broadcasted_iota(jnp.int32, (width, LANES), 0)
    lane = lax.broadcasted_iota(jnp.int32, (width, LANES), 1)
    turned = jnp.concatenate(
        [dot_tn(block, (row == lane * share + k).astype(BF16)) for k in range(count)], axis=0
    ).astype(BF16)
    entry = lax.broadcasted_iota(jnp.int32, (count * LANES, width), 0)
    place = lax.broadcasted_iota(jnp.int32, (count * LANES, width), 1)
    owner = whole_div(lax.broadcasted_iota(jnp.int32, (LANES, width), 1), share)
    owns = (lax.broadcasted_iota(jnp.int32, (LANES, width), 0) == owner).astype(BF16)
    spread = dot_nn(turned, owns)
    fits = entry - whole_div(entry, share) * share == place - whole_div(place, share) * share
    spread = jnp.where(fits, spread, 0.0).astype(BF16)
    vector = lax.broadcasted_iota(jnp.int32, (16, count * LANES), 0)
    source = whole_div(lax.broadcasted_iota(jnp.int32, (16, count * LANES), 1), share)
    vectors = dot_nn((vector == source).astype(BF16), spread)
    line = lax.broadcasted_iota(jnp.int32, (LANES, LANES), 1)
    owns = (lax.broadcasted_iota(jnp.int32, (LANES, LANES), 0) == whole_div(line, answers)).astype(BF16)
    spread = dot_nn(turned, owns)
    entry = lax.broadcasted_iota(jnp.int32, spread.shape, 0) - rows_in * share
    place = lax.broadcasted_iota(jnp.int32, spread.shape, 1)
    fits = entry == place - whole_div(place, answers) * answers
    return vectors, jnp.sum(jnp.where(fits, spread, 0.0), axis=0, keepdims=True)


EPS=1e-6

def normed(h):
    c=h-jnp.mean(h,axis=1,keepdims=True)
    f=lax.rsqrt(jnp.mean(c*c,axis=1,keepdims=True)+EPS)
    return c*f,f

def attention_kernel(orders,fsdp,small,lens_ref,me_ref,tok_ref,p0,p1,p2,p3,w_ref,vec_ref,mix_ref,ctx_ref,inv_ref,wts_ref,n1_ref,r1_ref,low_ref,acc_ref,sems):
    pack=pl.program_id(0)
    width=tok_ref.shape[1]; wide=3*width
    @pl.when(pack==0)
    def _():
        assemble(me_ref,orders,fsdp,(p0,p1,p2,p3),w_ref,sems)
        vectors,answer=unpack_small(w_ref[:,wide+width:],*small)
        vec_ref[...]=vectors
        vec_ref[15:16,:LANES]=answer
    query_row=vec_ref[6:7,:]; value_row=vec_ref[7:8,:]
    lane,apart,own=segment_tiles(lens_ref,pack)
    apart=apart.astype(BF16); own=own.astype(BF16)
    tok=tok_ref[...]
    mix_ref[:,:width]=((dot_nn(tok,w_ref[:,:width])+query_row).astype(BF16).astype(F32)*(1/math.sqrt(HEAD_DIM))).astype(BF16)
    mix_ref[:,width:2*width]=dot_nn(tok,w_ref[:,width:2*width]).astype(BF16)
    mix_ref[:,2*width:]=(dot_nn(tok,w_ref[:,2*width:wide])+value_row).astype(BF16)
    acc_ref[...]=jnp.zeros_like(acc_ref)
    ones=jnp.ones((PACK,LANES),BF16)
    def pair(p,carry):
        at=lambda base: pl.ds(pl.multiple_of(base+p*LANES,LANES),LANES)
        q2=mix_ref[:,at(0)]; k2=mix_ref[:,at(width)]; v2=mix_ref[:,at(2*width)]
        kx=jnp.concatenate([k2,own],axis=1)
        vx=jnp.concatenate([v2,ones],axis=1)
        outs=[]
        for half in range(2):
            qm=jnp.where(lane//HEAD_DIM==half,q2,jnp.zeros_like(q2))
            s=dot_nt(jnp.concatenate([qm,apart],axis=1),kx)
            m=jnp.max(s,axis=1,keepdims=True)
            w=jnp.exp(s-m).astype(BF16)
            wts_ref[2*p+half]=w
            o=dot_nn(w,vx)
            inv=1.0/o[:,LANES:]
            outs.append(o[:,:LANES]*inv)
            acc_ref[...]=jnp.where(head_lanes(lane,2*p+half),inv,acc_ref[...])
        ctx_ref[:,at(0)]=jnp.where(lane<HEAD_DIM,outs[0],outs[1]).astype(BF16)
        return carry
    lax.fori_loop(0,HEADS//2,pair,0)
    inv_ref[...]=acc_ref[...]
    att=dot_nn(ctx_ref[...],w_ref[:,wide:wide+width])+vec_ref[0:1,:]
    n1,f1=normed(tok.astype(F32)+att)
    n1_ref[...]=n1; r1_ref[...]=jnp.broadcast_to(f1,r1_ref.shape)
    low_ref[...]=(n1*vec_ref[1:2,:]+vec_ref[2:3,:]).astype(BF16)

def attention(lens,me,tok,parts,orders,fsdp,small):
    rows,width=tok.shape; share=parts[0].shape[1]; full=parts[0].shape[2]+parts[2].shape[2]
    hbm=pl.BlockSpec(memory_space=pl.ANY)
    sm=pl.BlockSpec(memory_space=pltpu.SMEM)
    wide=3*width
    sizes=((wide,BF16),(width,BF16),(LANES,F32))
    outs=[jax.ShapeDtypeStruct((rows,n),t) for n,t in sizes]
    heads=[jax.ShapeDtypeStruct((width,full),BF16),jax.ShapeDtypeStruct((16,width),F32)]
    fixed=[once((width,full)),once((16,width))]
    cost=pl.CostEstimate(flops=2*rows*width*wide+8*rows*PACK*width,bytes_accessed=rows*wide*4,transcendentals=HEADS*PACK*rows)
    spec=lambda n: pl.BlockSpec((PACK,n),lambda g:(g,0))
    return pl.pallas_call(functools.partial(attention_kernel,orders,fsdp,small),grid=(rows//PACK,),
        in_specs=[sm,sm,spec(width)]+[hbm]*4,out_specs=fixed+[spec(n) for n,_ in sizes]+[pl.BlockSpec((HEADS,PACK,PACK),lambda g:(g,0,0)),spec(width),spec(LANES),spec(width)],
        out_shape=heads+outs+[jax.ShapeDtypeStruct((rows//PACK*HEADS,PACK,PACK),BF16),jax.ShapeDtypeStruct((rows,width),F32),jax.ShapeDtypeStruct((rows,LANES),F32),jax.ShapeDtypeStruct((rows,width),BF16)],
        scratch_shapes=[pltpu.VMEM((PACK,LANES),F32),pltpu.SemaphoreType.DMA((4*parts[0].shape[0],))],
        compiler_params=pltpu.CompilerParams(vmem_limit_bytes=VMEM_MOST),name='attention',cost_estimate=cost)(lens,me,tok,*parts)

def split_three(x,lane):
    hi=x.astype(BF16).astype(F32)
    rest=x-hi
    mid=rest.astype(BF16).astype(F32)
    return jnp.where(lane<16,hi,jnp.where(lane<32,mid,jnp.where(lane<48,rest-mid,0.0)))

def attention_grad_kernel(q_ref,k_ref,v_ref,ctx_ref,dctx_ref,inv_ref,wts_ref,out_ref):
    p=pl.program_id(1)
    width=out_ref.shape[1]//3
    lane=lax.broadcasted_iota(jnp.int32,(PACK,LANES),1)
    at=lambda base: pl.ds(pl.multiple_of(base+p*LANES,LANES),LANES)
    q2=q_ref[...]; k2=k_ref[...]; v2=v_ref[...]; d2=dctx_ref[...].astype(F32)
    invs=[jnp.sum(jnp.where(lane==2*p+half,inv_ref[...],0.0),axis=1,keepdims=True) for half in range(2)]
    d2=d2*jnp.where(lane<HEAD_DIM,invs[0],invs[1])
    prod=d2*ctx_ref[...].astype(F32)
    d2=d2.astype(BF16)
    qt=q2.T; dt=d2.T
    mark=head_lanes(lane,0).astype(BF16)
    vx=jnp.concatenate([v2,mark],axis=1)
    dq=[]; dks=[]; dvs=[]
    for half in range(2):
        here=lane//HEAD_DIM==half
        dm=jnp.where(here,d2,jnp.zeros_like(d2))
        dots=jnp.sum(jnp.where(here,prod,0.0),axis=1,keepdims=True)
        de=(-split_three(jnp.broadcast_to(dots,(PACK,LANES)),lane)).astype(BF16)
        w=wts_ref[half]
        dp=dot_nt(jnp.concatenate([dm,de],axis=1),vx)
        ds=(w.astype(F32)*dp).astype(BF16)
        rows=slice(half*HEAD_DIM,(half+1)*HEAD_DIM)
        dq.append(dot_nn(ds,k2))
        dks.append(dot_nn(qt[rows],ds))
        dvs.append(dot_nn(dt[rows],w))
    out_ref[:,at(0)]=(jnp.where(lane<HEAD_DIM,dq[0],dq[1])*(1/math.sqrt(HEAD_DIM))).astype(BF16)
    out_ref[:,at(width)]=jnp.concatenate(dks,axis=0).T.astype(BF16)
    out_ref[:,at(2*width)]=jnp.concatenate(dvs,axis=0).T.astype(BF16)

def attention_grad(mix,ctx,dctx,inv,wts):
    rows,width=ctx.shape; wide=mix.shape[1]; pairs=HEADS//2
    pair=lambda at: pl.BlockSpec((PACK,LANES),lambda g,p:(g,at*pairs+p))
    return pl.pallas_call(attention_grad_kernel,grid=(rows//PACK,pairs),
        in_specs=[pair(0),pair(1),pair(2),pair(0),pair(0),pl.BlockSpec((PACK,LANES),lambda g,p:(g,0)),pl.BlockSpec((2,PACK,PACK),lambda g,p:(g*pairs+p,0,0))],
        out_specs=pl.BlockSpec((PACK,wide),lambda g,p:(g,0)),out_shape=jax.ShapeDtypeStruct((rows,wide),BF16),
        compiler_params=pltpu.CompilerParams(vmem_limit_bytes=VMEM_MOST),name='attention_grad',
        cost_estimate=pl.CostEstimate(flops=16*rows*PACK*width,bytes_accessed=rows*wide*8,transcendentals=0))(mix,mix,mix,ctx,dctx,inv,wts)
TILE=256
def half_tail(a, e):
    t=1.0/(1.0+0.3275911*a)
    p=t*(0.5*0.254829592+t*(0.5*-0.284496736+t*(0.5*1.421413741+t*(0.5*-1.453152027+t*(0.5*1.061405429)))))
    return p*e

def gelu_pair(x):
    z=jnp.abs(x)*(1/math.sqrt(2))
    e=jnp.exp(-z*z)
    h=half_tail(z,e)
    phi=jnp.where(x>0,1.0-h,h)
    return x*phi, phi+x*(e*(1/math.sqrt(2*math.pi)))

def norm_back(e,n,f):
    return f*(e-jnp.mean(e,axis=1,keepdims=True)-n*jnp.mean(e*n,axis=1,keepdims=True))

def row_segments(lens_ref,first_row,rows):
    row=first_row+lax.broadcasted_iota(jnp.int32,(rows,LANES),0)
    lane=lax.broadcasted_iota(jnp.int32,(rows,LANES),1)
    packs=lens_ref.shape[0]
    seg=jnp.zeros((rows,LANES),jnp.int32)
    for g in range(packs):
        end=jnp.int32(g*PACK)
        for j in range(SEGS_PACK):
            end=end+lens_ref[g,j]
            seg=seg+(row>=end).astype(jnp.int32)
    return seg==lane

def feed_forward_kernel(lens_ref,n1_ref,low_ref,w_ref,vec_ref,act_ref,dg_ref,n2_ref,r2_ref,res_ref,span_ref,score_ref,doc_ref,all_ref):
    i=pl.program_id(0)
    rows,width=n1_ref.shape; reps=act_ref.shape[1]//width
    vec=lambda k: vec_ref[k:k+1,:]
    base=2*reps*width
    low=low_ref[...]
    out=n1_ref[...]*vec(1)+vec(2)+vec(3)
    for q in range(reps):
        c=slice(q*width,(q+1)*width)
        x=dot_nn(low,w_ref[:,c])+vec(8+q)
        a,d=gelu_pair(x)
        a=a.astype(BF16)
        act_ref[:,c]=a; dg_ref[:,c]=d.astype(BF16)
        out=out+dot_nn(a,w_ref[:,(reps+q)*width:(reps+q+1)*width])
    n2,f2=normed(out)
    n2_ref[...]=n2; r2_ref[...]=jnp.broadcast_to(f2,(rows,LANES))
    res=(n2*vec(4)+vec(5)).astype(BF16)
    res_ref[...]=res
    span=dot_nn(res,w_ref[:,base:base+LANES])
    span_ref[...]=span
    score=jnp.broadcast_to(jnp.sum(span*vec_ref[15:16,:LANES],axis=1,keepdims=True),(rows,LANES))
    score_ref[...]=score
    all_ref[pl.ds(pl.multiple_of(i*rows,rows),rows),:]=score
    @pl.when(i==pl.num_programs(0)-1)
    def _():
        member=row_segments(lens_ref,0,all_ref.shape[0])
        s=jnp.where(member,all_ref[...],MASKED)
        top=jnp.max(s,axis=0,keepdims=True)
        total=jnp.sum(jnp.where(member,jnp.exp(s-top),0.0),axis=0,keepdims=True)
        real=lax.broadcasted_iota(jnp.int32,(1,LANES),1)<lens_ref.shape[0]*SEGS_PACK
        doc_ref[...]=jnp.where(real,top+jnp.log(jnp.where(real,total,1.0)),MASKED)

def feed_forward(lens,n1,low,w,vec,reps):
    rows,width=n1.shape; ff=reps*width
    b=lambda n: pl.BlockSpec((TILE,n),lambda i:(i,0))
    s=lambda n,t: jax.ShapeDtypeStruct((rows,n),t)
    return pl.pallas_call(feed_forward_kernel,grid=(rows//TILE,),
        in_specs=[pl.BlockSpec(memory_space=pltpu.SMEM),b(width),b(width),once(w.shape),once(vec.shape)],
        out_specs=[b(ff),b(ff),b(width),b(LANES),b(width),b(LANES),b(LANES),once((1,LANES))],
        out_shape=[s(ff,BF16),s(ff,BF16),s(width,F32),s(LANES,F32),s(width,BF16),s(LANES,F32),s(LANES,F32),jax.ShapeDtypeStruct((1,LANES),F32)],
        scratch_shapes=[pltpu.VMEM((rows,LANES),F32)],
        compiler_params=pltpu.CompilerParams(vmem_limit_bytes=VMEM_MOST),name='feed_forward')(lens,n1,low,w,vec)

def feed_forward_grad_kernel(lens_ref,own_ids_ref,doc_ref,scores_ref,ids_ref,cot_ref,n2_ref,r2_ref,res_ref,span_ref,score_ref,dg_ref,n1_ref,r1_ref,w_ref,aw_ref,vec_ref,
                   low_ref,fsum_ref,dctx_ref,small_ref,spanw_ref,weight_ref,acc_ref):
    i=pl.program_id(0); last=pl.num_programs(0)-1
    rows,width=cot_ref.shape; reps=dg_ref.shape[1]//width
    vec=lambda k: vec_ref[k:k+1,:]
    base=2*reps*width
    @pl.when(i==0)
    def _():
        lane=lax.broadcasted_iota(jnp.int32,(1,LANES),1)
        marg=jnp.zeros((1,LANES),F32)
        for s in range(own_ids_ref.shape[0]):
            hit=ids_ref[...]==own_ids_ref[s].astype(F32)
            x=jnp.where(hit,scores_ref[...],MASKED)
            top=jnp.max(jnp.max(x,axis=1,keepdims=True),axis=0,keepdims=True)
            total=jnp.where(hit,jnp.exp(x-top),0.0)
            total=jnp.sum(jnp.sum(total,axis=1,keepdims=True),axis=0,keepdims=True)
            marg=jnp.where(lane==s,top+jnp.log(total),marg)
        weight_ref[...]=jnp.exp(doc_ref[...]-marg)
        small_ref[...]=jnp.zeros_like(small_ref)
        acc_ref[...]=jnp.zeros_like(acc_ref)
    member=row_segments(lens_ref,i*rows,rows)
    part=jnp.where(member,jnp.exp(jnp.where(member,score_ref[...]-doc_ref[...],0.0))*weight_ref[...],0.0)
    tw=jnp.sum(part,axis=1,keepdims=True)
    ans=vec_ref[15:16,:LANES]
    small_ref[15:16,:LANES]+=jnp.sum(tw*span_ref[...],axis=0,keepdims=True)
    sg=(tw*ans).astype(BF16)
    acc_ref[...]+=dot_tn(res_ref[...],sg)
    @pl.when(i==last)
    def _():
        spanw_ref[...]=acc_ref[...].astype(BF16)
    rg=cot_ref[...].astype(F32)+dot_nt(sg,w_ref[:,base:base+LANES])
    n2=n2_ref[...]
    def colsum(k,v):
        small_ref[k:k+1,:]+=jnp.sum(v,axis=0,keepdims=True)
    colsum(0,rg*n2); colsum(1,rg)
    ssum=norm_back(rg*vec(4),n2,r2_ref[:,:1])
    olow=ssum.astype(BF16); low_ref[:,reps*width:(reps+1)*width]=olow
    colsum(2,olow.astype(F32))
    fg=ssum
    for q in range(reps):
        c=slice(q*width,(q+1)*width)
        il=(dot_nt(olow,w_ref[:,(reps+q)*width:(reps+q+1)*width])*dg_ref[:,c].astype(F32)).astype(BF16)
        low_ref[:,c]=il
        colsum(8+q,il.astype(F32))
        fg=fg+dot_nt(il,w_ref[:,c])
    n1=n1_ref[...]
    colsum(3,fg*n1); colsum(4,fg)
    fsum=norm_back(fg*vec(1),n1,r1_ref[:,:1])
    fsum_ref[...]=fsum
    alow=fsum.astype(BF16); low_ref[:,(reps+1)*width:]=alow
    colsum(5,alow.astype(F32))
    dctx_ref[...]=dot_nt(alow,aw_ref[...]).astype(BF16)

def feed_forward_grad(lens,own_ids,doc,scores,ids,cot,n2,r2,res,span,score,dg,n1,r1,w,mix,vec):
    rows,width=cot.shape; ff=dg.shape[1]
    b=lambda n: pl.BlockSpec((TILE,n),lambda i:(i,0))
    s=lambda n,t: jax.ShapeDtypeStruct((rows,n),t)
    sm=pl.BlockSpec(memory_space=pltpu.SMEM)
    return pl.pallas_call(feed_forward_grad_kernel,grid=(rows//TILE,),
        in_specs=[sm,sm,once(doc.shape),once(scores.shape),once(ids.shape),b(width),b(width),b(LANES),b(width),b(LANES),b(LANES),b(ff),b(width),b(LANES),once(w.shape),pl.BlockSpec((width,width),lambda i:(0,3),pipeline_mode=pl.Buffered(1)),once(vec.shape)],
        out_specs=[b(ff+2*width),b(width),b(width),once(vec.shape),once((width,LANES))],
        out_shape=[s(ff+2*width,BF16),s(width,F32),s(width,BF16),jax.ShapeDtypeStruct(vec.shape,F32),jax.ShapeDtypeStruct((width,LANES),BF16)],
        scratch_shapes=[pltpu.VMEM((1,LANES),F32),pltpu.VMEM((width,LANES),F32)],
        compiler_params=pltpu.CompilerParams(vmem_limit_bytes=VMEM_MOST),name='feed_forward_grad')(lens,own_ids,doc,scores,ids,cot,n2,r2,res,span,score,dg,n1,r1,w,mix,vec)

def put_blocks(me_ref,keep_ref,give_ref,value,at):
    blocks,rows,_=keep_ref.shape
    second=me_ref[0]%2
    for t in range(blocks):
        low=value[2*t*rows:(2*t+1)*rows].astype(BF16)
        high=value[(2*t+1)*rows:(2*t+2)*rows].astype(BF16)
        @pl.when(second==0)
        def _():
            keep_ref[t,:,at]=low; give_ref[t,:,at]=high
        @pl.when(second==1)
        def _():
            keep_ref[t,:,at]=high; give_ref[t,:,at]=low

def early_kernel(reps,me_ref,low_hbm,act_hbm,ctx_hbm,right_ref,keep_ref,give_ref,left_ref,sems):
    j=pl.program_id(0); slots,_,width=left_ref.shape
    sources=[low_hbm]+[act_hbm.at[:,pl.ds(k*width,width)] for k in range(slots-2)]+[ctx_hbm]
    moves=[pltpu.make_async_copy(src,left_ref.at[k],sems.at[k]) for k,src in enumerate(sources)]
    @pl.when(j==0)
    def _():
        for move in moves: move.start()
    for k,move in enumerate(moves):
        @pl.when(j==(0 if k==0 else reps+k-1))
        def _(): move.wait()
    put_blocks(me_ref,keep_ref,give_ref,dot_tn(left_ref[jnp.maximum(j-reps+1,0)],right_ref[...]),slice(None))

def split_outs(dp,width,n):
    block=(dp//2,width//dp,width)
    return [pl.BlockSpec(block,lambda j:(0,0,j))]*2,[jax.ShapeDtypeStruct(block[:2]+(n*width,),BF16)]*2

def early_grads(me,low,act,ctx,right,outer_blocks,dp):
    rows,width=low.shape; reps=act.shape[1]//width
    n=reps+outer_blocks+1
    specs,shapes=split_outs(dp,width,n)
    hbm=pl.BlockSpec(memory_space=pl.ANY)
    column=lambda j: jnp.where(j<reps,j,jnp.where(j<n-1,reps,reps+1))
    return pl.pallas_call(functools.partial(early_kernel,reps),grid=(n,),
        in_specs=[pl.BlockSpec(memory_space=pltpu.SMEM),hbm,hbm,hbm,pl.BlockSpec((rows,width),lambda j:(0,column(j)))],
        out_specs=specs,out_shape=shapes,scratch_shapes=[pltpu.VMEM((outer_blocks+2,rows,width),BF16),pltpu.SemaphoreType.DMA((outer_blocks+2,))],
        compiler_params=pltpu.CompilerParams(vmem_limit_bytes=VMEM_MOST),name='early_weight_grads',
        cost_estimate=pl.CostEstimate(flops=2*rows*width*width*n,bytes_accessed=rows*width*n*4,transcendentals=0))(me,low,act,ctx,right)

def outer_kernel(me_ref,act_ref,olow_ref,keep_ref,give_ref):
    put_blocks(me_ref,keep_ref,give_ref,dot_tn(act_ref[...],olow_ref[...]),slice(None))

def outer_grads(me,act,right,first,dp):
    rows,ff=act.shape; width=right.shape[1]-ff>>1; n=ff//width-first
    specs,shapes=split_outs(dp,width,n)
    return pl.pallas_call(outer_kernel,grid=(n,),
        in_specs=[pl.BlockSpec(memory_space=pltpu.SMEM),pl.BlockSpec((rows,width),lambda j:(0,j+first)),pl.BlockSpec((rows,width),lambda j:(0,ff//width),pipeline_mode=pl.Buffered(1))],
        out_specs=specs,out_shape=shapes,
        compiler_params=pltpu.CompilerParams(vmem_limit_bytes=VMEM_MOST),name='outer_weight_grad',
        cost_estimate=pl.CostEstimate(flops=2*rows*width*width*n,bytes_accessed=rows*width*n*4,transcendentals=0))(me,act,right)

def late_kernel(me_ref,tok_ref,mg_ref,span_ref,keep_ref,give_ref,sum_ref):
    j=pl.program_id(0)
    width=tok_ref.shape[1]
    mg=mg_ref[...]
    sum_ref[...]=jnp.broadcast_to(jnp.sum(mg.astype(F32),axis=0,keepdims=True),sum_ref.shape)
    put_blocks(me_ref,keep_ref,give_ref,dot_tn(tok_ref[...],mg),pl.ds(pl.multiple_of(j*width,LANES),width))
    @pl.when(j==pl.num_programs(0)-1)
    def _():
        full=keep_ref.shape[2]
        put_blocks(me_ref,keep_ref,give_ref,span_ref[...].astype(F32),slice(full-span_ref.shape[1],full))

def late_grads(me,tok,mg,span,dp):
    rows,width=tok.shape; wide=mg.shape[1]
    out=(dp//2,width//dp,wide+span.shape[1])
    return pl.pallas_call(late_kernel,grid=(wide//width,),
        in_specs=[pl.BlockSpec(memory_space=pltpu.SMEM),once((rows,width)),pl.BlockSpec((rows,width),lambda j:(0,j)),once(span.shape)],
        out_specs=[once(out),once(out),pl.BlockSpec((8,width),lambda j:(0,j))],
        out_shape=[jax.ShapeDtypeStruct(out,BF16)]*2+[jax.ShapeDtypeStruct((8,wide),F32)],
        compiler_params=pltpu.CompilerParams(vmem_limit_bytes=VMEM_MOST),name='late_weight_grads',
        cost_estimate=pl.CostEstimate(flops=2*rows*width*wide,bytes_accessed=rows*wide*4,transcendentals=0))(me,tok,mg,span)

def input_kernel(sizes,w_ref,fs_ref,*refs):
    *mgs,out_ref=refs
    width=fs_ref.shape[1]
    total=fs_ref[...]
    start=0
    for mg_ref,n in zip(mgs,sizes):
        for k in range(3):
            total=total+dot_nt(mg_ref[:,k*n:(k+1)*n],w_ref[:,k*width+start:k*width+start+n])
        start+=n
    out_ref[...]=total

def input_grads(w,fs,mgs):
    rows,width=fs.shape
    b=lambda n: pl.BlockSpec((TILE,n),lambda i:(i,0))
    return pl.pallas_call(functools.partial(input_kernel,[m.shape[1]//3 for m in mgs]),grid=(rows//TILE,),
        in_specs=[once((width,3*width)),b(width)]+[b(m.shape[1]) for m in mgs],out_specs=b(width),out_shape=jax.ShapeDtypeStruct((rows,width),F32),
        compiler_params=pltpu.CompilerParams(vmem_limit_bytes=VMEM_MOST),name='input_grad',
        cost_estimate=pl.CostEstimate(flops=6*rows*width*width,bytes_accessed=rows*width*16,transcendentals=0))(w,fs,*mgs)
AXES = ("dp", "fsdp")
LATE_BLOCKS = 3


def pack_lanes(parts):
    flat = jnp.concatenate(parts, axis=-1)
    wide = -(-flat.shape[-1] // LANES) * LANES
    flat = jnp.pad(flat, [(0, 0)] * (flat.ndim - 1) + [(0, wide - flat.shape[-1])])
    return flat.reshape(flat.shape[:-1] + (wide // LANES, LANES))


def unpack_lanes(packed, sizes):
    flat = packed.reshape(packed.shape[:-2] + (-1,))
    starts = [sum(sizes[:i]) for i in range(len(sizes))]
    return [flat[..., a : a + n] for a, n in zip(starts, sizes)]


def to_all(block, devices):
    return lax.all_to_all(jnp.broadcast_to(block[None], (devices,) + block.shape), AXES, 0, 0)


def shards(
    tokens,
    cotangent,
    doc_lengths,
    query_ids,
    qkv_weight,
    query_bias,
    value_bias,
    attn_weight,
    attn_bias,
    first_gain,
    first_shift,
    inner_weight,
    inner_bias,
    outer_weight,
    outer_bias,
    second_gain,
    second_shift,
    span_weight,
    answer_vector,
):
    rows, width = tokens.shape
    packs_here = rows // PACK
    devices = lax.axis_size("dp") * lax.axis_size("fsdp")
    share = qkv_weight.shape[0]
    ff = inner_weight.shape[1]
    reps = ff // width
    segs_here = packs_here * SEGS_PACK
    span = span_weight.shape[1]

    row_params = (attn_bias, first_gain, first_shift, outer_bias, second_gain, second_shift)
    smalls = row_params + (query_bias, value_bias, inner_bias, answer_vector)
    answers = answer_vector.shape[0]
    rows_in = len(row_params) + 2 + reps
    packed = pack_lanes(smalls)
    packed = jnp.pad(packed, ((0, share - packed.shape[0]), (0, 0)))
    id_row = jnp.pad(
        query_ids[:, 0].astype(F32)[None], ((0, 0), (0, LANES - segs_here)), constant_values=-1.0
    )

    orders = bit_orders(lax.axis_size("dp"))
    fsdp = lax.axis_size("fsdp")
    me = jnp.stack([lax.axis_index("dp"), lax.axis_index("fsdp")]).astype(jnp.int32)
    mix = jnp.concatenate([qkv_weight, attn_weight, packed], axis=1)
    mix_near = gather_near(mix)
    near = len(mix_near)
    mix_walk = Gathering(mix_near, orders, 2 * width)
    mix_walk.advance(0)
    mix_walk.send()
    mix_parts = mix_walk.parts()
    inner_turned = (
        inner_weight.reshape(share, devices, reps, share).transpose(0, 2, 1, 3).reshape(share, ff)
    )
    outer_blocks = [outer_weight[q * share : (q + 1) * share] for q in range(reps)]
    rest = jnp.concatenate([inner_turned] + outer_blocks + [span_weight], axis=1)
    rest_full = lax.all_gather(rest, AXES, axis=0, tiled=True)

    (
        mix_full,
        vectors,
        mixed,
        context,
        inverse,
        weights,
        normed_one,
        factor_one,
        first_low,
    ) = attention(doc_lengths, me, tokens, mix_parts, orders, near, (share, rows_in, answers))
    active, gelu_slope, normed_two, factor_two, result, span_rows, token_score, doc_score = (
        feed_forward(doc_lengths, normed_one, first_low, rest_full, vectors, reps)
    )
    exchanged = to_all(jnp.concatenate([doc_score, id_row], axis=0), devices)
    scores_all, ids_all = exchanged[:, 0], exchanged[:, 1]

    lows, first_sum_grad, context_grad, small_sums, span_grad = (
        feed_forward_grad(
            doc_lengths,
            query_ids.reshape(-1),
            doc_score,
            scores_all,
            ids_all,
            cotangent,
            normed_two,
            factor_two,
            result,
            span_rows,
            token_score,
            gelu_slope,
            normed_one,
            factor_one,
            rest_full,
            mix_full,
            vectors,
        )
    )
    early_blocks = reps - LATE_BLOCKS
    dp = lax.axis_size("dp")
    keep, give = early_grads(me, first_low, active, context, lows, early_blocks, dp)
    came = swap(give, "dp", orders[0][0])
    lows, keep = tie(lows, keep)
    outer_walk = Reduction(*outer_grads(me, active, lows, early_blocks, dp), orders[1])
    came, outer_walk.keep = tie(came, outer_walk.keep)
    outer_walk.send()
    early = add_low(keep, came)
    cores = [[d for d in range(dp) if d % 2 == c] for c in range(2)]
    early_dp = lax.psum_scatter(
        early.reshape(-1, early.shape[-1]),
        "dp",
        scatter_dimension=0,
        axis_index_groups=cores,
        tiled=True,
    )
    context_grad, early = tie(context_grad, early)
    mixed_grad = attention_grad(mixed, context, context_grad, inverse, weights)
    mixed_grad, outer_walk.came = tie(mixed_grad, outer_walk.came)
    *late, bias_sums = late_grads(me, tokens, mixed_grad, span_grad, dp)
    late, outer_walk.came = tie(late, outer_walk.came)
    late_walk = Reduction(*late, orders[0])
    late_walk.send()
    outer_walk.add()
    outer_walk.advance(2)
    outer_walk.send()
    n_rows = small_sums.shape[0]
    by_owner = small_sums.reshape(n_rows, devices, share).transpose(1, 0, 2)
    biases = bias_sums[0].reshape(3, devices, share).transpose(1, 0, 2)
    small_grads = pack_lanes(
        [
            by_owner.reshape(devices, n_rows * share),
            biases.reshape(devices, 3 * share),
            small_sums[15, :span].reshape(devices, span // devices),
        ]
    )
    small_grads, late_walk.came, outer_walk.give = tie(
        small_grads, late_walk.came, outer_walk.give
    )
    late_walk.add()
    late_walk.advance(2)
    late_walk.send()
    small_grads, early_dp, late_walk.keep, outer_walk.keep = tie(
        small_grads, early_dp, late_walk.keep, outer_walk.keep
    )
    received = lax.all_to_all(small_grads, AXES, 0, 0)
    early_sum, early_takes = start_near([early_dp])
    scores_all, first_sum_grad, early_sum = tie(scores_all, first_sum_grad, early_sum)
    input_grad = input_grads(mix_full, first_sum_grad, [mixed_grad])
    input_grad, early_takes, late_walk.came, outer_walk.came = tie(
        input_grad, early_takes, late_walk.came, outer_walk.came
    )
    outer_walk.add()
    outer_walk.send()
    late_walk.add()
    late_walk.send()
    received, late_walk.came, outer_walk.came = tie(
        received, late_walk.came, outer_walk.came
    )
    outer_walk.add()
    late_walk.add()
    late_sum, takes = start_near([late_walk.keep, outer_walk.keep])
    received, early_takes, late_sum = tie(received, early_takes, late_sum)
    early_sum = add_near(early_sum, early_takes)
    early_sum, received = tie(early_sum, received)
    mine = jnp.sum(received, axis=0)
    own_rows, own_biases, answer_own = unpack_lanes(
        mine, [n_rows * share, 3 * share, span // devices]
    )
    row_of = lambda k: own_rows[k * share : (k + 1) * share]
    queries = lax.broadcasted_iota(F32, (packs_here * devices, 1), 0)
    member_query = ids_all[:, :segs_here].reshape(1, -1) == queries
    marginal = jax.nn.logsumexp(
        jnp.where(member_query, scores_all[:, :segs_here].reshape(1, -1), MASKED), axis=1
    )
    inner_own = (
        early_sum[:, :ff].reshape(share, reps, devices, share).transpose(0, 2, 1, 3)
    ).reshape(share, ff)
    inner_own, takes = tie(inner_own, takes)
    late_sum = add_near(late_sum, takes)
    outer_own = jnp.concatenate(
        [early_sum[:, ff + q * width : ff + (q + 1) * width] for q in range(early_blocks)]
        + [late_sum[:, 3 * width + span + q * width :][:, :width] for q in range(LATE_BLOCKS)],
        axis=0,
    )
    return (
        jnp.sum(marginal),
        result,
        input_grad,
        late_sum[:, : 3 * width],
        own_biases[:share],
        own_biases[2 * share :],
        early_sum[:, -width:],
        row_of(5),
        row_of(3),
        row_of(4),
        inner_own,
        own_rows[8 * share : (8 + reps) * share],
        outer_own,
        row_of(2),
        row_of(0),
        row_of(1),
        late_sum[:, 3 * width : 3 * width + span],
        answer_own,
    )


def solution(mesh):
    rows = P(AXES, None)
    flat = P(AXES)
    in_specs = (rows,) * 4 + (rows, flat, flat, rows, flat, flat, flat, rows, flat, rows)
    in_specs += (flat, flat, flat, rows, flat)
    out_specs = (P(), rows, rows, rows, flat, flat, rows, flat, flat, flat, rows, flat, rows)
    out_specs += (flat, flat, flat, rows, flat)
    return jax.shard_map(shards, mesh=mesh, in_specs=in_specs, out_specs=out_specs, check_vma=False)
```
